32 devices in a mesh: dp: 8 (over y, x, core), tensor: 4 (over z).
Axes of the slice: x: 2, y: 2, z: 4, core: 2. Of those that a mesh axis runs over, the one named last changes fastest.
Arguments:
- tokens: bfloat16 [8192, 2048], P(('dp', 'tensor')), may hold values from -6 to 6
- positions: int32 [8192], P('dp'), may hold values from 0 to 1023, as said below
- norm_gain: float32 [2, 2, 2048], replicated, may hold values from 0.25 to 1.75
- norm_bias: float32 [2, 2, 2048], replicated, may hold values from -3 to 3
- w_qkv: bfloat16 [2, 2048, 3, 2048], P(None, 'dp', None, 'tensor'), may hold values from -0.125 to 0.125
- b_qkv: float32 [2, 3, 2048], replicated, may hold values from -3 to 3
- w_out: bfloat16 [2, 2048, 2048], P(None, 'tensor', 'dp'), may hold values from -0.5 to 0.5
- w_gate_up: bfloat16 [2, 2048, 2, 5632], P(None, 'dp', None, 'tensor'), may hold values from -0.125 to 0.125
- w_down: bfloat16 [2, 5632, 2048], P(None, 'tensor', 'dp'), may hold values from -0.078125 to 0.078125
- cotangent: bfloat16 [8192, 2048], P(('dp', 'tensor')), may hold values from -6 to 6
Outputs:
- activations: bfloat16 [8192, 2048], P(('dp', 'tensor'))
- input_grad: float32 [8192, 2048], P(('dp', 'tensor'))
- gain_grad: float32 [2, 2, 2048], replicated
- norm_bias_grad: float32 [2, 2, 2048], replicated
- qkv_grad: float32 [2, 2048, 3, 2048], P(None, 'dp', None, 'tensor')
- qkv_bias_grad: float32 [2, 3, 2048], replicated
- out_grad: float32 [2, 2048, 2048], P(None, 'tensor', 'dp')
- gate_up_grad: float32 [2, 2048, 2, 5632], P(None, 'dp', None, 'tensor')
- down_grad: float32 [2, 5632, 2048], P(None, 'tensor', 'dp')
The draws below stay inside these ranges and needn't reach their ends.
Inputs may be any that keep to these rules, and one draw needn't show every extreme that they name: positions[i] counts the tokens before i in its document; documents lie end to end in the sequences of 1024 tokens, so the first token of a sequence has 0 and every other token has 0 or one more than the token before it.
All inputs are finite; a program needn't handle non-finite values.
Results may differ from the reference program's by a relative error of at most 0.023.
Values may be sent and summed in bfloat16 or wider, within the bound.
A program may use at most 320 MiB of HBM per device.

```python
import math
import jax
import jax.numpy as jnp
from jax import lax

D = 2048
HEADS = 32
HD = 64
ROT = 16
FF = 5632
LAYERS = 2
LEN = 1024
TOKENS = 8192
N_DP = 8


def draw_positions(key, part):
    indices = jnp.arange(TOKENS, dtype=jnp.int32)
    within = indices % LEN
    starts = jax.random.randint(key, (TOKENS,), 0, LEN) < 3
    starts = starts & (indices >= LEN) | (within == 0)
    doc_start = lax.cummax(jnp.where(starts, indices, 0), axis=0)
    return (indices - doc_start).astype(jnp.int32)


def raised(drawn, key, source, target, shards_of, factor):
    owner, partner = [(jnp.arange(drawn.shape[dim]) // (drawn.shape[dim] // shards_of)).reshape([-1 if axis == dim else 1 for axis in range(drawn.ndim)]) for dim in (source, target)]
    chosen = jax.random.permutation(key, shards_of)[partner]
    strong = (owner == chosen) | (owner == (partner + shards_of // 2) % shards_of)
    return jnp.where(strong, factor * drawn, drawn)


def block_scale(key, shape, split, low, high):
    loudness, own = 1.0, jax.random.fold_in(key, 6)
    for dim, blocks in split:
        steps = jnp.exp(jax.random.uniform(jax.random.fold_in(own, dim), (blocks,), jnp.float32, low / len(split), high / len(split)))
        loudness = loudness * jnp.repeat(steps, shape[dim] // blocks).reshape([-1 if axis == dim else 1 for axis in range(len(shape))])
    return loudness


def noise(key, extent, spread, limit, pieces=(), kind=jnp.bfloat16):
    values = spread * jax.random.normal(key, extent, jnp.float32)
    if pieces:
        values = values * block_scale(key, extent, pieces, -0.22, 0.18)
    return jnp.clip(values, -limit, limit).astype(kind)


def gaussian_with(key, dims, deviation, most, pieces, heavy, held_as=jnp.bfloat16):
    values = deviation * jax.random.normal(key, dims, jnp.float32)
    if pieces:
        values = values * block_scale(key, dims, pieces, -0.22, 0.18)
    return jnp.clip(raised(values, jax.random.fold_in(key, 3), *heavy), -most, most).astype(held_as)


def setup_inputs(seed: int = 0) -> dict:
    keys = jax.random.split(jax.random.key(seed), 11)
    tokens = noise(keys[0], (TOKENS, D), 1.0, 6.0, ((0, 32),))
    positions = draw_positions(jax.random.fold_in(keys[10], 71), 0)
    norm_gain = jnp.clip(1.0 + 0.15 * jax.random.normal(keys[2], (LAYERS, 2, D), jnp.float32), 0.25, 1.75)
    norm_bias = noise(keys[3], (LAYERS, 2, D), 0.5, 3.0, (), jnp.float32)
    w_qkv = noise(keys[4], (LAYERS, D, 3, D), D ** -0.5, 0.125, ((1, 8), (3, 4)))
    b_qkv = noise(keys[5], (LAYERS, 3, D), 0.5, 3.0, (), jnp.float32)
    w_out = noise(keys[6], (LAYERS, D, D), (D // 16) ** -0.5, 0.5, ((1, 4), (2, 8)))
    w_gate_up = noise(keys[7], (LAYERS, D, 2, FF), D ** -0.5, 0.125, ((1, 8), (3, 4)))
    w_down = noise(keys[8], (LAYERS, FF, D), FF ** -0.5, 0.078125, ((1, 4), (2, 8)))
    cotangent = gaussian_with(keys[9], (TOKENS, D), 1.0, 6.0, ((0, 32),), (0, 1, 32, 2.75))
    return dict(tokens=tokens, positions=positions, norm_gain=norm_gain, norm_bias=norm_bias, w_qkv=w_qkv, b_qkv=b_qkv, w_out=w_out, w_gate_up=w_gate_up, w_down=w_down, cotangent=cotangent)


norm_eps = 1e-05
theta_log = math.log(10000.0)
exact_precision = lax.Precision.HIGHEST

@jax.custom_vjp
def low(v):
    return lax.optimization_barrier(v.astype(jnp.bfloat16)).astype(jnp.float32)

@jax.custom_vjp
def low_back(v):
    return v

def low_keep(v):
    return (low(v), None)

def low_pass(kept, grad):
    return (grad,)

def back_keep(v):
    return (v, None)

def back_low(kept, grad):
    return (low(grad),)
low.defvjp(low_keep, low_pass)
low_back.defvjp(back_keep, back_low)

def layer_norm(hidden, norm_weight, norm_shift):
    average = lax.optimization_barrier(jnp.mean(hidden, axis=-1, keepdims=True))
    centred = hidden - average
    variance = lax.optimization_barrier(jnp.mean(centred * centred, axis=-1, keepdims=True))
    return centred * lax.rsqrt(variance + norm_eps) * norm_weight + norm_shift

def rotary_tables(positions):
    half_rot = ROT // 2
    frequency = jnp.exp(-(jnp.arange(half_rot, dtype=jnp.float32) * 2.0 / ROT) * theta_log)
    angles = positions.astype(jnp.float32)[:, None] * frequency[None, :]
    return (jnp.cos(angles)[:, None, :], jnp.sin(angles)[:, None, :])

def rotate(values, cos_table, sin_table):
    half_rot = ROT // 2
    first_half = values[..., :half_rot]
    second_half = values[..., half_rot:ROT]
    return jnp.concatenate([first_half * cos_table - second_half * sin_table, second_half * cos_table + first_half * sin_table, values[..., ROT:]], axis=-1)

def attend_sequence(inputs):
    queries, key_rows, values, seq_positions = inputs
    scores = jnp.einsum('qhd,khd->hqk', queries, key_rows, precision=exact_precision)
    scores = low_back(scores * (1.0 / math.sqrt(HD)))
    row_index = jnp.arange(LEN, dtype=jnp.int32)
    first_key = row_index - seq_positions
    allowed = (row_index[None, :] <= row_index[:, None]) & (row_index[None, :] >= first_key[:, None])
    weights = low(jax.nn.softmax(jnp.where(allowed[None], scores, -1e+30), axis=-1))
    return jnp.einsum('hqk,khd->qhd', weights, values, precision=exact_precision)

def forward(hidden, norm_gain, norm_bias, w_qkv, b_qkv, w_out, w_gate_up, w_down, positions):
    cos_table, sin_table = rotary_tables(positions)
    for layer_index in range(LAYERS):
        normed_a = low(layer_norm(hidden, norm_gain[layer_index, 0], norm_bias[layer_index, 0]))
        mixed = jnp.dot(normed_a, w_qkv[layer_index].reshape(D, 3 * D), precision=exact_precision)
        mixed = low_back(mixed + b_qkv[layer_index].reshape(3 * D)).reshape(TOKENS, 3, HEADS, HD)
        queries = low(rotate(mixed[:, 0], cos_table, sin_table))
        key_rows = low(rotate(mixed[:, 1], cos_table, sin_table))
        values = low(mixed[:, 2])
        attended = lax.map(jax.checkpoint(attend_sequence), (queries.reshape(N_DP, LEN, HEADS, HD), key_rows.reshape(N_DP, LEN, HEADS, HD), values.reshape(N_DP, LEN, HEADS, HD), positions.reshape(N_DP, LEN)))
        attended = low(low_back(attended.reshape(TOKENS, D)))
        hidden = hidden + low_back(jnp.dot(attended, w_out[layer_index], precision=exact_precision))
        normed_b = low(layer_norm(hidden, norm_gain[layer_index, 1], norm_bias[layer_index, 1]))
        gate_up = jnp.dot(normed_b, w_gate_up[layer_index].reshape(D, 2 * FF), precision=exact_precision)
        gate_up = low_back(gate_up).reshape(TOKENS, 2, FF)
        activated = low(jax.nn.silu(gate_up[:, 0]) * gate_up[:, 1])
        hidden = hidden + low_back(jnp.dot(activated, w_down[layer_index], precision=exact_precision))
    return hidden

def reference(tokens, positions, norm_gain, norm_bias, w_qkv, b_qkv, w_out, w_gate_up, w_down, cotangent):

    def run(hidden, gains, shifts, qkv_weight, qkv_shift, out_weight, gate_weight, down_weight):
        return forward(hidden, gains, shifts, qkv_weight, qkv_shift, out_weight, gate_weight, down_weight, positions)
    result, pullback = jax.vjp(run, tokens.astype(jnp.float32), norm_gain.astype(jnp.float32), norm_bias.astype(jnp.float32), w_qkv.astype(jnp.float32), b_qkv.astype(jnp.float32), w_out.astype(jnp.float32), w_gate_up.astype(jnp.float32), w_down.astype(jnp.float32))
    grads = pullback(cotangent.astype(jnp.float32))
    return (result.astype(jnp.bfloat16), grads[0], grads[1], grads[2], grads[3], grads[4], grads[5], grads[6], grads[7])
```

```python
import functools
import math

import jax
import jax.numpy as jnp
from jax import lax
from jax.experimental import pallas as pl
from jax.experimental.pallas import tpu as pltpu
from jax.sharding import PartitionSpec as P

HD = 64
ROT = 16
LAYERS = 2
PAIR = 2 * HD
MESH = pl.DeviceIdType.MESH
F32 = jnp.float32
BF16 = jnp.bfloat16
VMEM_LIMIT = 62 * 2**20

norm_eps = 1e-05
theta_log = math.log(10000.0)
masked_score = -1e30
rows_rows = (((0,), (0,)), ((), ()))
cols_cols = (((1,), (1,)), ((), ()))
rows_cols = (((1,), (0,)), ((), ()))


def matmul(left, right, dims=rows_cols):
    return lax.dot_general(left, right, dims, preferred_element_type=F32)


def line_order(step, place, count):
    short = jnp.minimum(place, count - 1 - place)
    away = (step + 1) // 2
    nearest = jnp.where(step % 2 == 1, place - away, place + away)
    others = jnp.where(place < count - 1 - place, step, count - 1 - step)
    return jnp.where(step <= 2 * short, nearest, others)


def line_barrier(place, count):
    barrier = pltpu.get_barrier_semaphore()

    @pl.when(place > 0)
    def _():
        pl.semaphore_signal(barrier, inc=1, device_id={"tensor": place - 1}, device_id_type=MESH)

    @pl.when(place < count - 1)
    def _():
        pl.semaphore_signal(barrier, inc=1, device_id={"tensor": place + 1}, device_id_type=MESH)

    middle = (place > 0) & (place < count - 1)

    @pl.when(middle)
    def _():
        pl.semaphore_wait(barrier, 2)

    @pl.when(jnp.logical_not(middle))
    def _():
        pl.semaphore_wait(barrier, 1)


def gather_rows(place, count, held, send_sem, recv_sem, process):
    def hop(block, right):
        return pltpu.make_async_remote_copy(
            src_ref=held.at[block],
            dst_ref=held.at[block],
            send_sem=send_sem.at[0 if right else 1, block],
            recv_sem=recv_sem.at[block],
            device_id={"tensor": place + 1 if right else place - 1},
            device_id_type=MESH,
        )

    def one(step, carry):
        block = line_order(step, place, count)

        @pl.when(step > 0)
        def _():
            hop(block, True).wait_recv()

        @pl.when((block <= place) & (place < count - 1))
        def _():
            hop(block, True).start()

        @pl.when((block >= place) & (place > 0))
        def _():
            hop(block, False).start()

        process(block)
        return carry

    lax.fori_loop(0, count, one, 0)

    def drain(block, carry):
        @pl.when((block <= place) & (place < count - 1))
        def _():
            hop(block, True).wait_send()

        @pl.when((block >= place) & (place > 0))
        def _():
            hop(block, False).wait_send()

        return carry

    lax.fori_loop(0, count, drain, 0)


def scatter_sums(place, count, partial, term, total, sending, arrived, send_sem, recv_sem):
    chunk = min(32, total.shape[0])

    def hop(owner, right):
        if right:
            slot, target = owner, place + 1
        else:
            slot, target = jnp.where(owner == place - 1, count, owner), place - 1
        return pltpu.make_async_remote_copy(
            src_ref=sending.at[owner],
            dst_ref=arrived.at[slot],
            send_sem=send_sem.at[owner],
            recv_sem=recv_sem.at[slot],
            device_id={"tensor": target},
            device_id_type=MESH,
        )

    def landed(slot):
        return pltpu.make_async_remote_copy(
            src_ref=sending.at[place],
            dst_ref=arrived.at[slot],
            send_sem=send_sem.at[place],
            recv_sem=recv_sem.at[slot],
            device_id={"tensor": place},
            device_id_type=MESH,
        )

    def add(slot):
        def rows(number, carry):
            at = pl.ds(pl.multiple_of(number * chunk, chunk), chunk)
            total[at, :] = total[at, :] + arrived[slot, at, :].astype(F32)
            return carry

        lax.fori_loop(0, total.shape[0] // chunk, rows, 0)

    def pack(owner):
        def rows(number, carry):
            at = pl.ds(pl.multiple_of(number * chunk, chunk), chunk)
            sending[owner, at, :] = total[at, :].astype(sending.dtype)
            return carry

        lax.fori_loop(0, total.shape[0] // chunk, rows, 0)

    def pack_sum(owner):
        def rows(number, carry):
            at = pl.ds(pl.multiple_of(number * chunk, chunk), chunk)
            sending[owner, at, :] = (total[at, :] + arrived[owner, at, :].astype(F32)).astype(
                sending.dtype
            )
            return carry

        lax.fori_loop(0, total.shape[0] // chunk, rows, 0)

    def one(step, carry):
        owner = line_order(count - 1 - step, place, count)
        term(owner)
        onward = ((owner > place) & (place > 0)) | ((owner < place) & (place < count - 1))

        @pl.when(onward)
        def _():
            landed(owner).wait_recv()
            pack_sum(owner)

        @pl.when((owner != place) & jnp.logical_not(onward))
        def _():
            pack(owner)

        @pl.when(owner > place)
        def _():
            hop(owner, True).start()

        @pl.when(owner < place)
        def _():
            hop(owner, False).start()

        return carry

    lax.fori_loop(0, count, one, 0)

    @pl.when(place > 0)
    def _():
        landed(place).wait_recv()
        add(place)

    @pl.when(place < count - 1)
    def _():
        landed(count).wait_recv()
        add(count)

    def drain(owner, carry):
        @pl.when(owner > place)
        def _():
            hop(owner, True).wait_send()

        @pl.when(owner < place)
        def _():
            hop(owner, False).wait_send()

        return carry

    lax.fori_loop(0, count, drain, 0)


def each_tile(width, tile, run):
    def one(number, carry):
        run(pl.multiple_of(number * tile, tile), tile)
        return carry

    lax.fori_loop(0, width // tile, one, 0)
    if width % tile:
        run(width // tile * tile, width % tile)


def each_rows(count, chunk, run):
    def one(number, carry):
        run(pl.ds(pl.multiple_of(number * chunk, chunk), chunk))
        return carry

    lax.fori_loop(0, count // chunk, one, 0)


def norm_rows(values):
    average = jnp.mean(values, axis=-1, keepdims=True)
    centred = values - average
    variance = jnp.mean(centred * centred, axis=-1, keepdims=True)
    inverse = lax.rsqrt(variance + norm_eps)
    return centred * inverse, inverse


def add_and_norm(total, before, gain, shift, after, normed):
    def rows(at):
        hidden = before[at, :] + total[at, :]
        after[at, :] = hidden
        scaled, _ = norm_rows(hidden)
        normed[at, :] = (scaled * gain[...] + shift[...]).astype(BF16)

    each_rows(total.shape[0], 16, rows)


def norm_back_rows(total, grad, hidden, gain, out, out_low, gain_sum, shift_sum):
    gain_sum[...] = jnp.zeros_like(gain_sum)
    shift_sum[...] = jnp.zeros_like(shift_sum)

    def rows(at):
        grad_normed = total[at, :]
        scaled, inverse = norm_rows(hidden[at, :])
        weighted = grad_normed * gain[...]
        first = jnp.mean(weighted, axis=-1, keepdims=True)
        product = grad_normed * scaled
        second = jnp.mean(weighted * scaled, axis=-1, keepdims=True)
        result = grad[at, :] + inverse * (weighted - first - scaled * second)
        out[at, :] = result
        out_low[at, :] = result.astype(BF16)
        gain_sum[...] += jnp.sum(product, axis=0, keepdims=True)
        shift_sum[...] += jnp.sum(grad_normed, axis=0, keepdims=True)

    each_rows(total.shape[0], 16, rows)


def line_scratch(count, rows, width):
    return [
        pltpu.VMEM((rows, width), F32),
        pltpu.VMEM((count, rows, width), BF16),
        pltpu.VMEM((count + 1, rows, width), BF16),
        pltpu.SemaphoreType.DMA((count,)),
        pltpu.SemaphoreType.DMA((count + 1,)),
    ]


def gather_scratch(count, rows, width):
    return [
        pltpu.VMEM((count, rows, width), BF16),
        pltpu.SemaphoreType.DMA((2, count)),
        pltpu.SemaphoreType.DMA((count,)),
        pltpu.SemaphoreType.DMA((count,)),
    ]


vmem = pl.BlockSpec(memory_space=pltpu.VMEM)
hbm = pl.BlockSpec(memory_space=pl.ANY)


def line_call(body, out_shape, out_specs, in_specs, scratch, number, flops, moved):
    return pl.pallas_call(
        body,
        out_shape=out_shape,
        in_specs=in_specs,
        out_specs=out_specs,
        scratch_shapes=scratch,
        compiler_params=pltpu.CompilerParams(
            collective_id=number, has_side_effects=True, vmem_limit_bytes=VMEM_LIMIT
        ),
        cost_estimate=pl.CostEstimate(flops=flops, bytes_accessed=moved, transcendentals=0),
    )


def qkv_kernel(
    count, own, weight, bias, cos, sin_up, sin_down, rows_out, mixed_out,
    held, send_sem, recv_sem, out_sem, weight_held, mixed, weight_sem, mixed_sem,
):
    place = lax.axis_index("tensor")
    load = pltpu.make_async_copy(weight, weight_held, weight_sem)
    load.start()
    line_barrier(place, count)
    held[place] = own[...]
    rows = own.shape[0]
    width = mixed.shape[3]
    tile = min(256, width)

    def save(block):
        return (
            pltpu.make_async_copy(held.at[block], rows_out.at[block], out_sem.at[block]),
            pltpu.make_async_copy(mixed.at[:, block], mixed_out.at[:, block], mixed_sem.at[block]),
        )

    def process(block):
        @pl.when(block == place)
        def _():
            load.wait()

        at = pl.ds(pl.multiple_of(block * rows, rows), rows)

        def columns(kind):
            def run(start, size):
                source = pl.ds(pl.multiple_of(kind * width + start, 128), size)
                target = pl.ds(start, size)
                result = matmul(held[block], weight_held[:, source]) + bias[:, source]
                if kind < 2:
                    result = (
                        result * cos[at, :size]
                        + pltpu.roll(result, size - ROT // 2, 1) * sin_up[at, :size]
                        + pltpu.roll(result, ROT // 2, 1) * sin_down[at, :size]
                    )
                if kind == 0:
                    result = result * (1.0 / math.sqrt(HD))
                mixed[kind, block, :, target] = result.astype(BF16)

            return run

        for kind in range(3):
            each_tile(width, tile, columns(kind))
        for copy in save(block):
            copy.start()

    gather_rows(place, count, held, send_sem, recv_sem, process)
    for block in range(count):
        for copy in save(block):
            copy.wait()


def gather_qkv(count, own, weight, bias, tables, width):
    rows, depth = own.shape
    flops = 2 * count * rows * depth * 3 * width
    return line_call(
        functools.partial(qkv_kernel, count),
        (
            jax.ShapeDtypeStruct((count, rows, depth), BF16),
            jax.ShapeDtypeStruct((3, count, rows, width), BF16),
        ),
        (hbm, hbm),
        [vmem, hbm, vmem, vmem, vmem, vmem],
        gather_scratch(count, rows, depth)
        + [
            pltpu.VMEM((depth, 3 * width), BF16),
            pltpu.VMEM((3, count, rows, width), BF16),
            pltpu.SemaphoreType.DMA,
            pltpu.SemaphoreType.DMA((count,)),
        ],
        0,
        flops,
        weight.size * 2 + own.size * 2 * count * 4,
    )(own, weight, bias, *tables)


def project_kernel(
    count, source, weight, before, gain, shift, after, normed,
    total, sending, arrived, send_sem, recv_sem,
):
    place = lax.axis_index("tensor")
    line_barrier(place, count)
    rows = before.shape[0]

    def term(owner):
        at = pl.ds(pl.multiple_of(owner * rows, rows), rows)

        def run(start, size):
            total[:, pl.ds(start, size)] = matmul(source[at, :], weight[:, pl.ds(start, size)])

        each_tile(total.shape[1], 512, run)

    scatter_sums(
        place, count, None, term, total, sending, arrived, send_sem, recv_sem
    )
    add_and_norm(total, before, gain, shift, after, normed)


def project_scatter(count, source, weight, before, gain, shift):
    rows, depth = before.shape
    return line_call(
        functools.partial(project_kernel, count),
        (
            jax.ShapeDtypeStruct((rows, depth), F32),
            jax.ShapeDtypeStruct((rows, depth), BF16),
        ),
        (vmem, vmem),
        [vmem] * 5,
        line_scratch(count, rows, depth),
        1,
        2 * source.size * depth,
        weight.size * 2 + before.size * 12,
    )(source, weight, before, gain, shift)


def feed_kernel(
    count, own, before, gain, shift, w_up, w_down,
    after, normed, rows_out, act_out, slope_out, silu_out,
    held, send_sem, recv_sem, out_sem,
    total, sending, arrived, sum_send, sum_recv,
    up_held, down_held, act, slope, silu, weight_sem, act_sem,
):
    place = lax.axis_index("tensor")
    load_up = pltpu.make_async_copy(w_up, up_held, weight_sem.at[0])
    load_down = pltpu.make_async_copy(w_down, down_held, weight_sem.at[1])
    load_up.start()
    load_down.start()
    line_barrier(place, count)
    held[place] = own[...]
    width = act.shape[2]

    def save(block):
        return (
            pltpu.make_async_copy(held.at[block], rows_out.at[block], out_sem.at[block]),
            pltpu.make_async_copy(act.at[block], act_out.at[block], act_sem.at[0, block]),
            pltpu.make_async_copy(slope.at[block], slope_out.at[block], act_sem.at[1, block]),
            pltpu.make_async_copy(silu.at[block], silu_out.at[block], act_sem.at[2, block]),
        )

    def process(block):
        @pl.when(block == place)
        def _():
            load_up.wait()

        def run(start, size):
            at = pl.ds(start, size)
            gate = matmul(held[block], up_held[:, at])
            up = matmul(held[block], up_held[:, pl.ds(pl.multiple_of(width + start, 128), size)])
            sigmoid = jax.nn.sigmoid(gate)
            soft = gate * sigmoid
            act[block, :, at] = (soft * up).astype(BF16)
            silu[block, :, at] = soft.astype(BF16)
            slope[block, :, at] = (up * sigmoid * (1.0 + gate * (1.0 - sigmoid))).astype(BF16)

        each_tile(width, 256, run)
        for copy in save(block):
            copy.start()

    gather_rows(place, count, held, send_sem, recv_sem, process)
    load_down.wait()

    def term(owner):
        def run(start, size):
            at = pl.ds(start, size)
            total[:, at] = matmul(act[owner], down_held[:, at])

        each_tile(total.shape[1], 512, run)

    scatter_sums(place, count, None, term, total, sending, arrived, sum_send, sum_recv)
    add_and_norm(total, before, gain, shift, after, normed)
    for block in range(count):
        for copy in save(block):
            copy.wait()


def feed_forward(count, own, before, gain, shift, w_up, w_down):
    rows, depth = own.shape
    width = w_down.shape[0]
    wide = jax.ShapeDtypeStruct((count, rows, width), BF16)
    return line_call(
        functools.partial(feed_kernel, count),
        (
            jax.ShapeDtypeStruct((rows, depth), F32),
            jax.ShapeDtypeStruct((rows, depth), BF16),
            jax.ShapeDtypeStruct((count, rows, depth), BF16),
            wide,
            wide,
            wide,
        ),
        (vmem, vmem, hbm, hbm, hbm, hbm),
        [vmem, vmem, vmem, vmem, hbm, hbm],
        gather_scratch(count, rows, depth)
        + line_scratch(count, rows, depth)
        + [
            pltpu.VMEM((depth, 2 * width), BF16),
            pltpu.VMEM((width, depth), BF16),
            pltpu.VMEM((count, rows, width), BF16),
            pltpu.VMEM((count, rows, width), BF16),
            pltpu.VMEM((count, rows, width), BF16),
            pltpu.SemaphoreType.DMA((2,)),
            pltpu.SemaphoreType.DMA((3, count)),
        ],
        2,
        6 * count * rows * depth * width,
        (w_up.size + w_down.size) * 2 + own.size * 60,
    )(own, before, gain, shift, w_up, w_down)


def feed_back_kernel(
    count, own, grad, hidden, gain, w_up, w_down, slope_in, silu_in,
    out, out_low, gain_sum, shift_sum, rows_out, wide_out,
    held, send_sem, recv_sem, out_sem,
    total, sending, arrived, sum_send, sum_recv,
    up_held, down_held, wide, slope, silu, weight_sem, wide_sem,
):
    place = lax.axis_index("tensor")
    loads = (
        pltpu.make_async_copy(w_down, down_held, weight_sem.at[0]),
        pltpu.make_async_copy(slope_in, slope, weight_sem.at[1]),
        pltpu.make_async_copy(silu_in, silu, weight_sem.at[2]),
    )
    load_up = pltpu.make_async_copy(w_up, up_held, weight_sem.at[3])
    for load in loads:
        load.start()
    load_up.start()
    line_barrier(place, count)
    held[place] = own[...]
    width = slope.shape[2]

    def save(block):
        return (
            pltpu.make_async_copy(held.at[block], rows_out.at[block], out_sem.at[block]),
            pltpu.make_async_copy(wide.at[block], wide_out.at[block], wide_sem.at[block]),
        )

    def process(block):
        @pl.when(block == place)
        def _():
            for load in loads:
                load.wait()

        def run(start, size):
            at = pl.ds(start, size)
            grad_act = matmul(held[block], down_held[at, :], cols_cols)
            wide[block, :, at] = (grad_act * slope[block, :, at].astype(F32)).astype(BF16)
            wide[block, :, pl.ds(pl.multiple_of(width + start, 128), size)] = (
                grad_act * silu[block, :, at].astype(F32)
            ).astype(BF16)

        each_tile(width, 256, run)
        for copy in save(block):
            copy.start()

    gather_rows(place, count, held, send_sem, recv_sem, process)
    load_up.wait()

    def term(owner):
        def run(start, size):
            at = pl.ds(start, size)
            total[:, at] = matmul(wide[owner], up_held[at, :], cols_cols)

        each_tile(total.shape[1], 256, run)

    scatter_sums(place, count, None, term, total, sending, arrived, sum_send, sum_recv)
    norm_back_rows(total, grad, hidden, gain, out, out_low, gain_sum, shift_sum)
    for block in range(count):
        for copy in save(block):
            copy.wait()


def feed_backward(count, own, grad, hidden, gain, w_up, w_down, slope, silu):
    rows, depth = own.shape
    width = w_down.shape[0]
    return line_call(
        functools.partial(feed_back_kernel, count),
        (
            jax.ShapeDtypeStruct((rows, depth), F32),
            jax.ShapeDtypeStruct((rows, depth), BF16),
            jax.ShapeDtypeStruct((1, depth), F32),
            jax.ShapeDtypeStruct((1, depth), F32),
            jax.ShapeDtypeStruct((count, rows, depth), BF16),
            jax.ShapeDtypeStruct((count, rows, 2 * width), BF16),
        ),
        (vmem, vmem, vmem, vmem, hbm, hbm),
        [vmem, vmem, vmem, vmem, hbm, hbm, hbm, hbm],
        gather_scratch(count, rows, depth)
        + line_scratch(count, rows, depth)
        + [
            pltpu.VMEM((depth, 2 * width), BF16),
            pltpu.VMEM((width, depth), BF16),
            pltpu.VMEM((count, rows, 2 * width), BF16),
            pltpu.VMEM((count, rows, width), BF16),
            pltpu.VMEM((count, rows, width), BF16),
            pltpu.SemaphoreType.DMA((4,)),
            pltpu.SemaphoreType.DMA((count,)),
        ],
        3,
        6 * count * rows * depth * width,
        (w_up.size + w_down.size) * 2 + own.size * 60,
    )(own, grad, hidden, gain, w_up, w_down, slope, silu)


def grad_attended_kernel(
    count, own, weight, rows_out, result_out,
    held, send_sem, recv_sem, out_sem, weight_held, result, weight_sem, result_sem,
):
    place = lax.axis_index("tensor")
    load = pltpu.make_async_copy(weight, weight_held, weight_sem)
    load.start()
    line_barrier(place, count)
    held[place] = own[...]

    def save(block):
        return (
            pltpu.make_async_copy(held.at[block], rows_out.at[block], out_sem.at[block]),
            pltpu.make_async_copy(result.at[block], result_out.at[block], result_sem.at[block]),
        )

    def process(block):
        @pl.when(block == place)
        def _():
            load.wait()

        def run(start, size):
            at = pl.ds(start, size)
            result[block, :, at] = matmul(held[block], weight_held[at, :], cols_cols).astype(BF16)

        each_tile(result.shape[2], 256, run)
        for copy in save(block):
            copy.start()

    gather_rows(place, count, held, send_sem, recv_sem, process)
    for block in range(count):
        for copy in save(block):
            copy.wait()


def gather_grad_attended(count, own, weight):
    rows, depth = own.shape
    width = weight.shape[0]
    return line_call(
        functools.partial(grad_attended_kernel, count),
        (
            jax.ShapeDtypeStruct((count, rows, depth), BF16),
            jax.ShapeDtypeStruct((count, rows, width), BF16),
        ),
        (hbm, hbm),
        [vmem, hbm],
        gather_scratch(count, rows, depth)
        + [
            pltpu.VMEM((width, depth), BF16),
            pltpu.VMEM((count, rows, width), BF16),
            pltpu.SemaphoreType.DMA,
            pltpu.SemaphoreType.DMA((count,)),
        ],
        4,
        2 * count * rows * depth * width,
        weight.size * 2 + own.size * 40,
    )(own, weight)


def input_back_kernel(
    count, source, weight, grad, hidden, gain, out, out_low, gain_sum, shift_sum,
    total, sending, arrived, send_sem, recv_sem,
):
    place = lax.axis_index("tensor")
    line_barrier(place, count)
    width = source.shape[2]
    rows = total.shape[0]

    def term(owner):
        at_rows = pl.ds(pl.multiple_of(owner * rows, rows), rows)

        def run(start, size):
            at = pl.ds(start, size)
            result = matmul(source[0, at_rows, :], weight[at, :width], cols_cols)
            for kind in range(1, 3):
                result = result + matmul(
                    source[kind, at_rows, :],
                    weight[at, kind * width : (kind + 1) * width],
                    cols_cols,
                )
            total[:, at] = result

        each_tile(total.shape[1], 256, run)

    scatter_sums(place, count, None, term, total, sending, arrived, send_sem, recv_sem)
    norm_back_rows(total, grad, hidden, gain, out, out_low, gain_sum, shift_sum)


def input_backward(count, source, weight, grad, hidden, gain):
    rows, depth = grad.shape
    return line_call(
        functools.partial(input_back_kernel, count),
        (
            jax.ShapeDtypeStruct((rows, depth), F32),
            jax.ShapeDtypeStruct((rows, depth), BF16),
            jax.ShapeDtypeStruct((1, depth), F32),
            jax.ShapeDtypeStruct((1, depth), F32),
        ),
        (vmem, vmem, vmem, vmem),
        [vmem] * 5,
        line_scratch(count, rows, depth),
        5,
        2 * source.size * depth,
        weight.size * 2 + grad.size * 20,
    )(source, weight, grad, hidden, gain)


def usable(first, start, keys, queries):
    key_index = lax.broadcasted_iota(jnp.int32, (keys, queries), 0)
    query_index = start + lax.broadcasted_iota(jnp.int32, (keys, queries), 1)
    return (key_index >= first) & (key_index <= query_index)


def head_lanes(values, head):
    lane = lax.broadcasted_iota(jnp.int32, values.shape, 1)
    return jnp.where((lane // HD) == head, values, jnp.zeros_like(values))


def attend_kernel(block, positions, queries, keys, values, attended, logsums):
    length = keys.shape[0]
    values_across = jnp.transpose(values[...])
    for start in range(0, length, block):
        seen = start + block
        at = slice(start, seen)
        own = queries[at, :]
        index = start + lax.broadcasted_iota(jnp.int32, (1, block), 1)
        allowed = usable(index - positions[:, at], start, seen, block)
        halves = []
        for head in range(2):
            scores = matmul(keys[:seen, :], head_lanes(own, head), cols_cols)
            scores = jnp.where(allowed, scores, masked_score)
            highest = jnp.max(scores, axis=0, keepdims=True)
            weights = jnp.exp(scores - highest)
            sums = jnp.sum(weights, axis=0, keepdims=True)
            result = matmul(values_across[:, :seen], weights.astype(BF16))
            halves.append(result[head * HD : (head + 1) * HD, :] / sums)
            logsums[head : head + 1, at] = highest + jnp.log(sums)
        attended[at, :] = jnp.transpose(jnp.concatenate(halves, axis=0)).astype(BF16)


def pair_spec(length, kind):
    return pl.BlockSpec((None, length, PAIR), lambda pair: (kind, 0, pair))


def attend(mixed, positions):
    _, length, width = mixed.shape
    pairs = width // PAIR
    block = min(256, length)
    return pl.pallas_call(
        functools.partial(attend_kernel, block),
        grid=(pairs,),
        out_shape=(
            jax.ShapeDtypeStruct((length, width), BF16),
            jax.ShapeDtypeStruct((pairs, 2, length), F32),
        ),
        in_specs=[
            pl.BlockSpec((1, length), lambda pair: (0, 0)),
            pair_spec(length, 0),
            pair_spec(length, 1),
            pair_spec(length, 2),
        ],
        out_specs=(
            pl.BlockSpec((length, PAIR), lambda pair: (0, pair)),
            pl.BlockSpec((None, 2, length), lambda pair: (pair, 0, 0)),
        ),
        compiler_params=pltpu.CompilerParams(vmem_limit_bytes=VMEM_LIMIT),
        cost_estimate=pl.CostEstimate(
            flops=8 * length * length * width,
            bytes_accessed=8 * length * width,
            transcendentals=length * length * width // HD,
        ),
    )(positions, mixed, mixed, mixed)


def unrotate(values, cos, sin_up, sin_down):
    return (
        values * cos
        - pltpu.roll(values, PAIR - ROT // 2, 1) * sin_up
        - pltpu.roll(values, ROT // 2, 1) * sin_down
    )


def attend_back_kernel(
    block, positions, queries, keys, values, attended, grad_attended, logsums,
    cos, sin_up, sin_down, grad_mixed, bias_sum, grad_keys, grad_values,
):
    length = keys.shape[0]
    keys_across = jnp.transpose(keys[...])
    grad_keys[...] = jnp.zeros_like(grad_keys)
    grad_values[...] = jnp.zeros_like(grad_values)
    bias_sum[...] = jnp.zeros_like(bias_sum)
    for start in range(0, length, block):
        seen = start + block
        at = slice(start, seen)
        own = queries[at, :]
        grad_own = grad_attended[at, :]
        inner = jnp.transpose(grad_own.astype(F32) * attended[at, :].astype(F32))
        index = start + lax.broadcasted_iota(jnp.int32, (1, block), 1)
        allowed = usable(index - positions[:, at], start, seen, block)
        halves = []
        for head in range(2):
            own_head = head_lanes(own, head)
            grad_head = head_lanes(grad_own, head)
            scores = matmul(keys[:seen, :], own_head, cols_cols)
            weights = jnp.where(allowed, jnp.exp(scores - logsums[head : head + 1, at]), 0.0)
            grad_weights = matmul(values[:seen, :], grad_head, cols_cols)
            row_inner = jnp.sum(inner[head * HD : (head + 1) * HD, :], axis=0, keepdims=True)
            grad_scores = (weights * (grad_weights - row_inner)).astype(BF16)
            grad_values[:seen, :] += matmul(weights.astype(BF16), grad_head)
            grad_keys[:seen, :] += matmul(grad_scores, own_head)
            result = matmul(keys_across[:, :seen], grad_scores)
            halves.append(result[head * HD : (head + 1) * HD, :])
        grad_own_queries = jnp.transpose(jnp.concatenate(halves, axis=0)) * (1.0 / math.sqrt(HD))
        low = unrotate(grad_own_queries, cos[at, :], sin_up[at, :], sin_down[at, :]).astype(BF16)
        grad_mixed[0, at, :] = low
        bias_sum[0:1, :] += jnp.sum(low.astype(F32), axis=0, keepdims=True)
    for start in range(0, length, block):
        at = slice(start, start + block)
        low = unrotate(grad_keys[at, :], cos[at, :], sin_up[at, :], sin_down[at, :]).astype(BF16)
        grad_mixed[1, at, :] = low
        bias_sum[1:2, :] += jnp.sum(low.astype(F32), axis=0, keepdims=True)
        low = grad_values[at, :].astype(BF16)
        grad_mixed[2, at, :] = low
        bias_sum[2:3, :] += jnp.sum(low.astype(F32), axis=0, keepdims=True)


def attend_backward(mixed, positions, attended, grad_attended, logsums, tables):
    _, length, width = mixed.shape
    pairs = width // PAIR
    block = min(256, length)
    across = pl.BlockSpec((length, PAIR), lambda pair: (0, pair))
    table = pl.BlockSpec((length, PAIR), lambda pair: (0, 0))
    return pl.pallas_call(
        functools.partial(attend_back_kernel, block),
        grid=(pairs,),
        out_shape=(
            jax.ShapeDtypeStruct((3, length, width), BF16),
            jax.ShapeDtypeStruct((3, width), F32),
        ),
        in_specs=[
            pl.BlockSpec((1, length), lambda pair: (0, 0)),
            pair_spec(length, 0),
            pair_spec(length, 1),
            pair_spec(length, 2),
            across,
            across,
            pl.BlockSpec((None, 2, length), lambda pair: (pair, 0, 0)),
            table,
            table,
            table,
        ],
        out_specs=(
            pl.BlockSpec((3, length, PAIR), lambda pair: (0, 0, pair)),
            pl.BlockSpec((3, PAIR), lambda pair: (0, pair)),
        ),
        scratch_shapes=[pltpu.VMEM((length, PAIR), F32), pltpu.VMEM((length, PAIR), F32)],
        compiler_params=pltpu.CompilerParams(vmem_limit_bytes=VMEM_LIMIT),
        cost_estimate=pl.CostEstimate(
            flops=20 * length * length * width,
            bytes_accessed=16 * length * width,
            transcendentals=length * length * width // HD,
        ),
    )(positions, mixed, mixed, mixed, attended, grad_attended, logsums, *tables)


def rotary_tables(positions, width):
    half_rot = ROT // 2
    frequency = jnp.exp(-(jnp.arange(half_rot, dtype=F32) * 2.0 / ROT) * theta_log)
    angles = positions.astype(F32)[:, None] * frequency[None, :]
    cos, sin = jnp.cos(angles), jnp.sin(angles)
    length = positions.shape[0]
    rest = jnp.ones((length, HD - ROT), F32)
    none, gap = jnp.zeros((length, half_rot), F32), jnp.zeros((length, HD - ROT), F32)
    copies = width // HD
    return (
        jnp.tile(jnp.concatenate([cos, cos, rest], axis=1), (1, copies)),
        jnp.tile(jnp.concatenate([-sin, none, gap], axis=1), (1, copies)),
        jnp.tile(jnp.concatenate([none, sin, gap], axis=1), (1, copies)),
    )


def all_sum(values, axes):
    for axis in axes:
        size = lax.axis_size(axis)
        if size & (size - 1):
            values = lax.psum(values, axis)
            continue
        step = 1
        while step < size:
            values = values + lax.ppermute(values, axis, [(i, i ^ step) for i in range(size)])
            step *= 2
    return values


def per_device(
    tokens, positions, norm_gain, norm_bias, w_qkv, b_qkv, w_out, w_gate_up, w_down, cotangent
):
    count = lax.axis_size("tensor")
    tensor_rank = lax.axis_index("tensor")
    width = w_qkv.shape[3]
    ff_local = w_gate_up.shape[3]
    rows, depth = tokens.shape
    length = positions.shape[0]
    tables = rotary_tables(positions, min(256, width))
    pair_tables = tuple(table[:, :PAIR] for table in tables)
    positions_row = positions.reshape(1, length)
    gathered = []
    for layer in range(LAYERS):
        gathered.append(
            (
                lax.all_gather(
                    w_qkv[layer].reshape(-1, 3 * width), "dp", axis=0, tiled=True
                ),
                lax.all_gather(w_out[layer], "dp", axis=1, tiled=True),
                lax.all_gather(
                    w_gate_up[layer].reshape(-1, 2 * ff_local), "dp", axis=0, tiled=True
                ),
                lax.all_gather(w_down[layer], "dp", axis=1, tiled=True),
            )
        )
    hidden = tokens.astype(F32)
    scaled, _ = norm_rows(hidden)
    normed = (scaled * norm_gain[0, 0] + norm_bias[0, 0]).astype(BF16)
    kept = []
    for layer in range(LAYERS):
        full_qkv, full_out, full_gu, full_down = gathered[layer]
        bias = lax.dynamic_slice_in_dim(b_qkv[layer], tensor_rank * width, width, 1)
        rows_a, mixed = gather_qkv(
            count, normed, full_qkv, bias.reshape(1, 3 * width), tables, width
        )
        mixed = mixed.reshape(3, length, width)
        attended, logsums = attend(mixed, positions_row)
        hidden_mid, normed_b = project_scatter(
            count, attended, full_out, hidden, norm_gain[layer, 1:2], norm_bias[layer, 1:2]
        )
        following = min(layer + 1, LAYERS - 1)
        hidden_next, normed, rows_b, act, slope, silu = feed_forward(
            count,
            normed_b,
            hidden_mid,
            norm_gain[following, 0:1],
            norm_bias[following, 0:1],
            full_gu,
            full_down,
        )
        kept.append(
            (hidden, rows_a, mixed, attended, logsums, hidden_mid, rows_b, act, slope, silu)
        )
        hidden = hidden_next
    activations = hidden.astype(BF16)
    grad_low = cotangent
    grad = cotangent.astype(F32)
    scattered = [None] * LAYERS
    small = [None] * LAYERS
    for layer in reversed(range(LAYERS)):
        hidden, rows_a, mixed, attended, logsums, hidden_mid, rows_b, act, slope, silu = kept[layer]
        full_qkv, full_out, full_gu, full_down = gathered[layer]
        grad, grad_mid_low, gain_b, shift_b, grad_rows_b, wide = feed_backward(
            count, grad_low, grad, hidden_mid, norm_gain[layer, 1:2], full_gu, full_down, slope, silu
        )
        down_part = matmul(
            act.reshape(length, ff_local), grad_rows_b.reshape(length, depth), rows_rows
        ).astype(BF16)
        down_grad = lax.psum_scatter(down_part, "dp", scatter_dimension=1, tiled=True)
        gu_part = matmul(
            rows_b.reshape(length, depth), wide.reshape(length, 2 * ff_local), rows_rows
        ).astype(BF16)
        gu_grad = lax.psum_scatter(gu_part, "dp", scatter_dimension=0, tiled=True)
        grad_rows_a, grad_attended = gather_grad_attended(count, grad_mid_low, full_out)
        out_part = matmul(attended, grad_rows_a.reshape(length, depth), rows_rows).astype(BF16)
        out_grad = lax.psum_scatter(out_part, "dp", scatter_dimension=1, tiled=True)
        grad_mixed, bias_sum = attend_backward(
            mixed, positions_row, attended, grad_attended.reshape(length, width), logsums, pair_tables
        )
        flat_mixed = grad_mixed.transpose(1, 0, 2).reshape(length, 3 * width)
        qkv_part = matmul(rows_a.reshape(length, depth), flat_mixed, rows_rows).astype(BF16)
        qkv_grad = lax.psum_scatter(qkv_part, "dp", scatter_dimension=0, tiled=True)
        grad, grad_low, gain_a, shift_a = input_backward(
            count, grad_mixed, full_qkv, grad, hidden, norm_gain[layer, 0:1]
        )
        bias_full = lax.dynamic_update_slice(
            jnp.zeros((3, b_qkv.shape[2]), F32), bias_sum, (jnp.int32(0), tensor_rank * width)
        )
        small[layer] = jnp.concatenate([gain_a, gain_b, shift_a, shift_b, bias_full], axis=0)
        scattered[layer] = (
            qkv_grad.astype(F32).reshape(-1, 3, width),
            out_grad.astype(F32),
            gu_grad.astype(F32).reshape(-1, 2, ff_local),
            down_grad.astype(F32),
        )
    sums = all_sum(jnp.stack(small), ("dp", "tensor"))
    stacks = [jnp.stack([scattered[layer][kind] for layer in range(LAYERS)]) for kind in range(4)]
    return (
        activations,
        grad,
        sums[:, 0:2],
        sums[:, 2:4],
        stacks[0],
        sums[:, 4:7],
        stacks[1],
        stacks[2],
        stacks[3],
    )


def norm_parts(hidden):
    average = jnp.mean(hidden, axis=-1, keepdims=True)
    centred = hidden - average
    variance = jnp.mean(centred * centred, axis=-1, keepdims=True)
    inverse = lax.rsqrt(variance + norm_eps)
    return (centred * inverse, inverse)


def norm_back(grad_normed, scaled, inverse, norm_weight):
    weighted = grad_normed * norm_weight
    first_mean = jnp.mean(weighted, axis=-1, keepdims=True)
    second_mean = jnp.mean(weighted * scaled, axis=-1, keepdims=True)
    grad_input = inverse * (weighted - first_mean - scaled * second_mean)
    return (grad_input, jnp.sum(grad_normed * scaled, axis=0), jnp.sum(grad_normed, axis=0))


def plain_tables(positions):
    half_rot = ROT // 2
    frequency = jnp.exp(-(jnp.arange(half_rot, dtype=jnp.float32) * 2.0 / ROT) * theta_log)
    angles = positions.astype(jnp.float32)[:, None] * frequency[None, :]
    return (jnp.cos(angles)[:, None, :], jnp.sin(angles)[:, None, :])


def rotate(values, cos_table, sin_table):
    half_rot = ROT // 2
    first_half = values[..., :half_rot]
    second_half = values[..., half_rot:ROT]
    return jnp.concatenate(
        [
            first_half * cos_table - second_half * sin_table,
            second_half * cos_table + first_half * sin_table,
            values[..., ROT:],
        ],
        axis=-1,
    )


def inner_rows(left, right):
    return lax.dot_general(left, right, rows_rows, preferred_element_type=jnp.float32)


def inner_cols(left, right):
    return lax.dot_general(left, right, cols_cols, preferred_element_type=jnp.float32)


def block_scores(queries, key_rows, positions, number, block_rows, score_scale):
    seq_len = key_rows.shape[0]
    row_start = number * block_rows
    query_block = lax.dynamic_slice_in_dim(queries, row_start, block_rows, 0)
    scores = (
        jnp.einsum("qhd,khd->hqk", query_block, key_rows, preferred_element_type=jnp.float32)
        * score_scale
    )
    row_index = row_start + jnp.arange(block_rows, dtype=jnp.int32)
    first_key = row_index - lax.dynamic_slice_in_dim(positions, row_start, block_rows, 0)
    columns = jnp.arange(seq_len, dtype=jnp.int32)
    allowed = (columns[None, :] <= row_index[:, None]) & (columns[None, :] >= first_key[:, None])
    return (query_block, allowed, jnp.where(allowed[None], scores, masked_score))


def attend_forward(queries, key_rows, values, positions, score_scale):
    seq_len = queries.shape[0]
    block_rows = min(512, seq_len)

    def one_block(number):
        query_block, allowed, scores = block_scores(
            queries, key_rows, positions, number, block_rows, score_scale
        )
        row_max = jnp.max(scores, axis=-1, keepdims=True)
        shifted = jnp.exp(scores - row_max)
        row_sum = jnp.sum(shifted, axis=-1, keepdims=True)
        weights_low = (shifted / row_sum).astype(jnp.bfloat16)
        block_out = jnp.einsum(
            "hqk,khd->qhd", weights_low, values, preferred_element_type=jnp.float32
        )
        return (block_out, row_max + jnp.log(row_sum))

    block_outs, logsums = lax.map(one_block, jnp.arange(seq_len // block_rows, dtype=jnp.int32))
    return (block_outs.reshape(seq_len, -1), logsums)


def attend_back(queries, key_rows, values, positions, logsums, grad_attended, score_scale):
    seq_len = queries.shape[0]
    block_rows = min(512, seq_len)

    def one_block(totals, inputs):
        grad_keys, grad_values = totals
        number, logsum = inputs
        query_block, allowed, scores = block_scores(
            queries, key_rows, positions, number, block_rows, score_scale
        )
        softmax_rows = jnp.exp(scores - logsum)
        grad_block = lax.dynamic_slice_in_dim(grad_attended, number * block_rows, block_rows, 0)
        grad_probs = jnp.einsum(
            "qhd,khd->hqk", grad_block, values, preferred_element_type=jnp.float32
        )
        grad_values = grad_values + jnp.einsum(
            "hqk,qhd->khd",
            softmax_rows.astype(jnp.bfloat16),
            grad_block,
            preferred_element_type=jnp.float32,
        )
        row_inner = jnp.sum(softmax_rows * grad_probs, axis=-1, keepdims=True)
        grad_scores = jnp.where(allowed[None], softmax_rows * (grad_probs - row_inner), 0.0).astype(
            jnp.bfloat16
        )
        grad_query = (
            jnp.einsum("hqk,khd->qhd", grad_scores, key_rows, preferred_element_type=jnp.float32)
            * score_scale
        )
        grad_keys = (
            grad_keys
            + jnp.einsum(
                "hqk,qhd->khd", grad_scores, query_block, preferred_element_type=jnp.float32
            )
            * score_scale
        )
        return ((grad_keys, grad_values), grad_query)

    empty_grad = jnp.zeros(key_rows.shape, jnp.float32)
    numbers = jnp.arange(seq_len // block_rows, dtype=jnp.int32)
    (grad_keys, grad_values), grad_queries = lax.scan(
        one_block, (empty_grad, empty_grad), (numbers, logsums)
    )
    return (grad_queries.reshape(queries.shape), grad_keys, grad_values)


def per_device_plain(
    tokens, positions, norm_gain, norm_bias, w_qkv, b_qkv, w_out, w_gate_up, w_down, cotangent
):
    tensor_rank = lax.axis_index("tensor")
    width_local = w_qkv.shape[3]
    heads_local = width_local // HD
    ff_local = w_gate_up.shape[3]
    local_rows = tokens.shape[0]
    seq_len = positions.shape[0]
    score_scale = 1.0 / math.sqrt(HD)
    cos_table, sin_table = plain_tables(positions)
    hidden = tokens.astype(jnp.float32)
    kept_state = []
    for layer_index in range(LAYERS):
        gathered = (
            lax.all_gather(w_qkv[layer_index], "dp", axis=0, tiled=True),
            lax.all_gather(w_out[layer_index], "dp", axis=1, tiled=True),
            lax.all_gather(w_gate_up[layer_index], "dp", axis=0, tiled=True),
            lax.all_gather(w_down[layer_index], "dp", axis=1, tiled=True),
        )
        full_qkv, full_out, full_gu, full_down = gathered
        scaled_a, inverse_a = norm_parts(hidden)
        normed_a = (scaled_a * norm_gain[layer_index, 0] + norm_bias[layer_index, 0]).astype(
            jnp.bfloat16
        )
        rows_a = lax.all_gather(normed_a, "tensor", axis=0, tiled=True)
        bias_local = lax.dynamic_slice_in_dim(
            b_qkv[layer_index], tensor_rank * width_local, width_local, 1
        )
        mixed = jnp.dot(
            rows_a,
            full_qkv.reshape(full_qkv.shape[0], 3 * width_local),
            preferred_element_type=jnp.float32,
        ) + bias_local.reshape(3 * width_local)
        mixed = mixed.reshape(seq_len, 3, heads_local, HD)
        queries = rotate(mixed[:, 0], cos_table, sin_table).astype(jnp.bfloat16)
        key_rows = rotate(mixed[:, 1], cos_table, sin_table).astype(jnp.bfloat16)
        values = mixed[:, 2].astype(jnp.bfloat16)
        attended, logsums = attend_forward(queries, key_rows, values, positions, score_scale)
        attended = attended.astype(jnp.bfloat16)

        def project_attn(row_start, row_count, source=attended, weight=full_out):
            return jnp.dot(source, weight, preferred_element_type=jnp.float32)

        branch_a = lax.psum_scatter(
            project_attn(jnp.int32(0), local_rows * lax.axis_size("tensor")).astype(jnp.bfloat16),
            "tensor",
            scatter_dimension=0,
            tiled=True,
        ).astype(jnp.float32)
        hidden_mid = hidden + branch_a
        scaled_b, inverse_b = norm_parts(hidden_mid)
        normed_b = (scaled_b * norm_gain[layer_index, 1] + norm_bias[layer_index, 1]).astype(
            jnp.bfloat16
        )
        rows_b = lax.all_gather(normed_b, "tensor", axis=0, tiled=True)
        gate_up = jnp.dot(
            rows_b,
            full_gu.reshape(full_gu.shape[0], 2 * ff_local),
            preferred_element_type=jnp.float32,
        ).reshape(seq_len, 2, ff_local)
        activated = (jax.nn.silu(gate_up[:, 0]) * gate_up[:, 1]).astype(jnp.bfloat16)

        def project_mlp(row_start, row_count, source=activated, weight=full_down):
            return jnp.dot(source, weight, preferred_element_type=jnp.float32)

        hidden = hidden_mid + lax.psum_scatter(
            project_mlp(jnp.int32(0), local_rows * lax.axis_size("tensor")).astype(jnp.bfloat16),
            "tensor",
            scatter_dimension=0,
            tiled=True,
        ).astype(jnp.float32)
        kept_state.append(
            (
                gathered,
                scaled_a,
                inverse_a,
                rows_a,
                queries,
                key_rows,
                values,
                logsums,
                attended,
                scaled_b,
                inverse_b,
                rows_b,
                gate_up,
                activated,
            )
        )
    activations = hidden.astype(jnp.bfloat16)
    grad = cotangent.astype(jnp.float32)
    weight_parts = [None] * LAYERS
    gain_rows = [None] * LAYERS
    shift_rows = [None] * LAYERS
    qkv_shift_rows = [None] * LAYERS
    for layer_index in reversed(range(LAYERS)):
        (
            gathered,
            scaled_a,
            inverse_a,
            rows_a,
            queries,
            key_rows,
            values,
            logsums,
            attended,
            scaled_b,
            inverse_b,
            rows_b,
            gate_up,
            activated,
        ) = kept_state[layer_index]
        full_qkv, full_out, full_gu, full_down = (
            lax.all_gather(w_qkv[layer_index], "dp", axis=0, tiled=True),
            lax.all_gather(w_out[layer_index], "dp", axis=1, tiled=True),
            lax.all_gather(w_gate_up[layer_index], "dp", axis=0, tiled=True),
            lax.all_gather(w_down[layer_index], "dp", axis=1, tiled=True),
        )
        grad_rows_b = lax.all_gather(grad.astype(jnp.bfloat16), "tensor", axis=0, tiled=True)
        grad_down_weight = inner_rows(activated, grad_rows_b)
        grad_act = inner_cols(grad_rows_b, full_down)
        gate_part = gate_up[:, 0]
        up_part = gate_up[:, 1]
        sigmoid_gate = jax.nn.sigmoid(gate_part)
        grad_gate = grad_act * up_part * sigmoid_gate * (1.0 + gate_part * (1.0 - sigmoid_gate))
        grad_up = grad_act * jax.nn.silu(gate_part)
        grad_gate_up = (
            jnp.stack([grad_gate, grad_up], axis=1)
            .astype(jnp.bfloat16)
            .reshape(seq_len, 2 * ff_local)
        )
        grad_gu_weight = inner_rows(rows_b, grad_gate_up).reshape(full_gu.shape)
        flat_gu = full_gu.reshape(full_gu.shape[0], 2 * ff_local)

        def back_mlp(row_start, row_count, source=grad_gate_up, weight=flat_gu):
            return inner_cols(source, weight)

        grad_normed_b = lax.psum_scatter(
            back_mlp(jnp.int32(0), local_rows * lax.axis_size("tensor")).astype(jnp.bfloat16),
            "tensor",
            scatter_dimension=0,
            tiled=True,
        ).astype(jnp.float32)
        grad_in_b, gain_b, shift_b = norm_back(
            grad_normed_b, scaled_b, inverse_b, norm_gain[layer_index, 1]
        )
        grad = grad + grad_in_b
        grad_rows_a = lax.all_gather(grad.astype(jnp.bfloat16), "tensor", axis=0, tiled=True)
        grad_out_weight = inner_rows(attended, grad_rows_a)
        grad_attended = inner_cols(grad_rows_a, full_out).astype(jnp.bfloat16)
        grad_attended = grad_attended.reshape(seq_len, heads_local, HD)
        grad_queries, grad_keys, grad_values = attend_back(
            queries, key_rows, values, positions, logsums, grad_attended, score_scale
        )
        grad_queries = rotate(grad_queries, cos_table, -sin_table)
        grad_keys = rotate(grad_keys, cos_table, -sin_table)
        grad_mixed = jnp.stack([grad_queries, grad_keys, grad_values], axis=1)
        grad_mixed = grad_mixed.reshape(seq_len, 3 * width_local).astype(jnp.bfloat16)
        qkv_shift_local = jnp.sum(grad_mixed, axis=0, dtype=jnp.float32).reshape(3, width_local)
        qkv_shift_rows[layer_index] = lax.dynamic_update_slice(
            jnp.zeros((3, b_qkv.shape[2]), jnp.float32),
            qkv_shift_local,
            (jnp.int32(0), tensor_rank * width_local),
        )
        grad_qkv_weight = inner_rows(rows_a, grad_mixed).reshape(full_qkv.shape)
        flat_qkv = full_qkv.reshape(full_qkv.shape[0], 3 * width_local)

        def back_attn(row_start, row_count, source=grad_mixed, weight=flat_qkv):
            return inner_cols(source, weight)

        grad_normed_a = lax.psum_scatter(
            back_attn(jnp.int32(0), local_rows * lax.axis_size("tensor")).astype(jnp.bfloat16),
            "tensor",
            scatter_dimension=0,
            tiled=True,
        ).astype(jnp.float32)
        grad_in_a, gain_a, shift_a = norm_back(
            grad_normed_a, scaled_a, inverse_a, norm_gain[layer_index, 0]
        )
        grad = grad + grad_in_a
        gain_rows[layer_index] = jnp.stack([gain_a, gain_b])
        shift_rows[layer_index] = jnp.stack([shift_a, shift_b])
        weight_parts[layer_index] = (
            lax.psum_scatter(
                grad_qkv_weight.astype(jnp.bfloat16), "dp", scatter_dimension=0, tiled=True
            ).astype(jnp.float32),
            lax.psum_scatter(
                grad_out_weight.astype(jnp.bfloat16), "dp", scatter_dimension=1, tiled=True
            ).astype(jnp.float32),
            lax.psum_scatter(
                grad_gu_weight.astype(jnp.bfloat16), "dp", scatter_dimension=0, tiled=True
            ).astype(jnp.float32),
            lax.psum_scatter(
                grad_down_weight.astype(jnp.bfloat16), "dp", scatter_dimension=1, tiled=True
            ).astype(jnp.float32),
        )
    stack_qkv = jnp.stack([weight_parts[number][0] for number in range(LAYERS)])
    stack_out = jnp.stack([weight_parts[number][1] for number in range(LAYERS)])
    stack_gu = jnp.stack([weight_parts[number][2] for number in range(LAYERS)])
    stack_down = jnp.stack([weight_parts[number][3] for number in range(LAYERS)])
    gain_grad, norm_bias_grad, qkv_bias_grad = lax.psum(
        (jnp.stack(gain_rows), jnp.stack(shift_rows), jnp.stack(qkv_shift_rows)), ("dp", "tensor")
    )
    return (
        activations,
        grad,
        gain_grad,
        norm_bias_grad,
        stack_qkv,
        qkv_bias_grad,
        stack_out,
        stack_gu,
        stack_down,
    )


def solution(mesh):
    in_specs = (
        P(("dp", "tensor"), None),
        P("dp"),
        P(),
        P(),
        P(None, "dp", None, "tensor"),
        P(),
        P(None, "tensor", "dp"),
        P(None, "dp", None, "tensor"),
        P(None, "tensor", "dp"),
        P(("dp", "tensor"), None),
    )
    out_specs = (
        P(("dp", "tensor"), None),
        P(("dp", "tensor"), None),
        P(),
        P(),
        P(None, "dp", None, "tensor"),
        P(),
        P(None, "tensor", "dp"),
        P(None, "dp", None, "tensor"),
        P(None, "tensor", "dp"),
    )
    def run(*operands):
        fits = operands[7].shape[3] % 128 == 0 and operands[4].shape[3] % PAIR == 0
        return (per_device if fits else per_device_plain)(*operands)

    return jax.shard_map(
        run, mesh=mesh, in_specs=in_specs, out_specs=out_specs, check_vma=False
    )
```

```python
import functools
import math

import jax
import jax.numpy as jnp
from jax import lax
from jax.experimental import pallas as pl
from jax.experimental.pallas import tpu as pltpu
from jax.sharding import PartitionSpec as P

HD = 64
ROT = 16
LAYERS = 2
PAIR = 2 * HD
MESH = pl.DeviceIdType.MESH
F32 = jnp.float32
BF16 = jnp.bfloat16
VMEM_LIMIT = 62 * 2**20

norm_eps = 1e-05
theta_log = math.log(10000.0)
masked_score = -1e30
rows_rows = (((0,), (0,)), ((), ()))
cols_cols = (((1,), (1,)), ((), ()))
rows_cols = (((1,), (0,)), ((), ()))


def matmul(left, right, dims=rows_cols):
    return lax.dot_general(left, right, dims, preferred_element_type=F32)


def line_barrier(place, count):
    barrier = pltpu.get_barrier_semaphore()

    @pl.when(place > 0)
    def _():
        pl.semaphore_signal(barrier, inc=1, device_id={"tensor": place - 1}, device_id_type=MESH)

    @pl.when(place < count - 1)
    def _():
        pl.semaphore_signal(barrier, inc=1, device_id={"tensor": place + 1}, device_id_type=MESH)

    middle = (place > 0) & (place < count - 1)

    @pl.when(middle)
    def _():
        pl.semaphore_wait(barrier, 2)

    @pl.when(jnp.logical_not(middle))
    def _():
        pl.semaphore_wait(barrier, 1)


def each_tile(width, tile, run):
    def one(number, carry):
        run(pl.multiple_of(number * tile, tile), tile)
        return carry

    lax.fori_loop(0, width // tile, one, 0)
    if width % tile:
        run(width // tile * tile, width % tile)


class Line:
    def __init__(self, count, pieces, shares, sending, arrived, sum_send, sum_recv, held, send_sem, recv_sem):
        self.count, self.pieces = count, pieces
        self.shares, self.sending, self.arrived = shares, sending, arrived
        self.sum_send, self.sum_recv = sum_send, sum_recv
        self.held, self.send_sem, self.recv_sem = held, send_sem, recv_sem
        self.place = lax.axis_index("tensor")
        self.rows = (held if held is not None else sending).shape[1] // pieces

    def at(self, piece):
        return pl.ds(pl.multiple_of(piece * self.rows, self.rows), self.rows)

    def sum_hop(self, piece, owner):
        right = owner > self.place
        target = jnp.where(right, self.place + 1, self.place - 1)
        slot = jnp.where(right | (owner != target), owner, self.count)
        return pltpu.make_async_remote_copy(
            src_ref=self.sending.at[owner, self.at(piece)],
            dst_ref=self.arrived.at[slot, self.at(piece)],
            send_sem=self.sum_send.at[owner, piece],
            recv_sem=self.sum_recv.at[slot, piece],
            device_id={"tensor": target},
            device_id_type=MESH,
        )

    def sum_landed(self, piece, slot):
        return pltpu.make_async_remote_copy(
            src_ref=self.sending.at[0, self.at(piece)],
            dst_ref=self.arrived.at[slot, self.at(piece)],
            send_sem=self.sum_send.at[0, piece],
            recv_sem=self.sum_recv.at[slot, piece],
            device_id={"tensor": self.place},
            device_id_type=MESH,
        )

    def row_hop(self, piece, block, right):
        return pltpu.make_async_remote_copy(
            src_ref=self.held.at[block, self.at(piece)],
            dst_ref=self.held.at[block, self.at(piece)],
            send_sem=self.send_sem.at[jnp.where(right, 0, 1), block, piece],
            recv_sem=self.recv_sem.at[block, piece],
            device_id={"tensor": jnp.where(right, self.place + 1, self.place - 1)},
            device_id_type=MESH,
        )

    def sides(self, away, run):
        def one(side, carry):
            block = jnp.where(side == 0, self.place + away, self.place - away)

            @pl.when((block >= 0) & (block < self.count))
            def _():
                run(block, side == 0)

            return carry

        lax.fori_loop(0, 2, one, 0)

    def chunks(self, run):
        chunk = min(16, self.rows)

        def one(number, carry):
            run(pl.multiple_of(number * chunk, chunk), chunk)
            return carry

        lax.fori_loop(0, self.rows // chunk, one, 0)

    def pass_on(self, piece, owner, right):
        side = piece % 2
        first = pl.multiple_of(piece * self.rows, self.rows)
        onward = jnp.where(right, self.place > 0, self.place < self.count - 1)

        @pl.when(onward)
        def _():
            self.sum_landed(piece, owner).wait_recv()

            def rows(start, size):
                at = pl.ds(pl.multiple_of(first + start, size), size)
                self.sending[owner, at, :] = (
                    self.shares[side, owner, pl.ds(start, size), :]
                    + self.arrived[owner, at, :].astype(F32)
                ).astype(BF16)

            self.chunks(rows)

        @pl.when(jnp.logical_not(onward))
        def _():
            def rows(start, size):
                at = pl.ds(pl.multiple_of(first + start, size), size)
                self.sending[owner, at, :] = self.shares[side, owner, pl.ds(start, size), :].astype(BF16)

            self.chunks(rows)

        self.sum_hop(piece, owner).start()

    def collect(self, piece):
        side = piece % 2
        first = pl.multiple_of(piece * self.rows, self.rows)

        def add(slot):
            self.sum_landed(piece, slot).wait_recv()

            def rows(start, size):
                at = pl.ds(pl.multiple_of(first + start, size), size)
                mine = pl.ds(start, size)
                self.shares[side, self.place, mine, :] = self.shares[
                    side, self.place, mine, :
                ] + self.arrived[slot, at, :].astype(F32)

            self.chunks(rows)

        @pl.when(self.place > 0)
        def _():
            add(self.place)

        @pl.when(self.place < self.count - 1)
        def _():
            add(self.count)

    def own_rows(self, piece, run):
        side = piece % 2
        first = pl.multiple_of(piece * self.rows, self.rows)

        def rows(start, size):
            at = pl.ds(pl.multiple_of(first + start, size), size)
            run(at, self.shares[side, self.place, pl.ds(start, size), :])

        self.chunks(rows)

    def run(self, term, finish, process):
        count, pieces, place = self.count, self.pieces, self.place
        scatter, gather = term is not None, process is not None
        if scatter:
            term(0)

        def period(number, carry):
            if scatter:

                @pl.when(number < pieces)
                def _():
                    self.sides(count - 1, lambda owner, right: self.pass_on(number, owner, right))

            @pl.when(number >= 1)
            def _():
                piece = number - 1
                if scatter:
                    self.collect(piece)
                finish(piece)
                if gather:

                    @pl.when(place < count - 1)
                    def _():
                        self.row_hop(piece, place, True).start()

                    @pl.when(place > 0)
                    def _():
                        self.row_hop(piece, place, False).start()

            if scatter:

                @pl.when(number + 1 < pieces)
                def _():
                    term(number + 1)

            def slot(step, inner):
                if scatter:

                    @pl.when((number < pieces) & (step < count - 1))
                    def _():
                        self.sides(
                            count - 1 - step,
                            lambda owner, right: self.pass_on(number, owner, right),
                        )

                if gather:

                    @pl.when(number >= 1)
                    def _():
                        def forward(block, right):
                            self.row_hop(number - 1, block, True).wait_recv()
                            onward = jnp.where(right, place > 0, place < count - 1)

                            @pl.when(onward)
                            def _():
                                self.row_hop(number - 1, block, jnp.logical_not(right)).start()

                        self.sides(step, forward)

                    @pl.when((step == 1) & (number >= 2))
                    def _():
                        process(number - 2)

                return inner

            lax.fori_loop(1, count, slot, 0)
            return carry

        lax.fori_loop(0, pieces + 1, period, 0)
        if gather:
            process(pieces - 1)

    def drain(self):
        def piece_sends(piece, carry):
            def owner_sends(owner, inner):
                if self.sending is not None:

                    @pl.when(owner != self.place)
                    def _():
                        self.sum_hop(piece, owner).wait_send()

                if self.held is not None:

                    @pl.when((owner <= self.place) & (self.place < self.count - 1))
                    def _():
                        self.row_hop(piece, owner, True).wait_send()

                    @pl.when((owner >= self.place) & (self.place > 0))
                    def _():
                        self.row_hop(piece, owner, False).wait_send()

                return inner

            lax.fori_loop(0, self.count, owner_sends, 0)
            return carry

        lax.fori_loop(0, self.pieces, piece_sends, 0)


def norm_rows(values):
    average = jnp.mean(values, axis=-1, keepdims=True)
    centred = values - average
    variance = jnp.mean(centred * centred, axis=-1, keepdims=True)
    inverse = lax.rsqrt(variance + norm_eps)
    return centred * inverse, inverse


def scatter_scratch(count, pieces, rows, width):
    return [
        pltpu.VMEM((2, count, rows // pieces, width), F32),
        pltpu.VMEM((count, rows, width), BF16),
        pltpu.VMEM((count + 1, rows, width), BF16),
        pltpu.SemaphoreType.DMA((count, pieces)),
        pltpu.SemaphoreType.DMA((count + 1, pieces)),
    ]


def gather_scratch(count, pieces, rows, width):
    return [
        pltpu.VMEM((count, rows, width), BF16),
        pltpu.SemaphoreType.DMA((2, count, pieces)),
        pltpu.SemaphoreType.DMA((count, pieces)),
    ]


vmem = pl.BlockSpec(memory_space=pltpu.VMEM)
hbm = pl.BlockSpec(memory_space=pl.ANY)


class Loads:
    def __init__(self, pairs, sems):
        self.copies = [
            pltpu.make_async_copy(source, target, sems.at[number])
            for number, (source, target) in enumerate(pairs)
        ]
        for copy in self.copies:
            copy.start()

    def wait(self, *numbers):
        for number in numbers:
            self.copies[number].wait()


class Saves:
    def __init__(self, pairs, sems, line):
        self.pairs, self.sems, self.line = pairs, sems, line

    def copy(self, number, piece):
        source, target = self.pairs[number]
        rows = self.line.at(piece)
        where = (slice(None),) * (len(source.shape) - 2) + (rows,)
        return pltpu.make_async_copy(
            source.at[where], target.at[where], self.sems.at[number, piece]
        )

    def start(self, piece):
        for number in range(len(self.pairs)):
            self.copy(number, piece).start()

    def wait(self):
        for number in range(len(self.pairs)):
            for piece in range(self.line.pieces):
                self.copy(number, piece).wait()


def flat_rows(ref, rows, columns=slice(None)):
    values = ref[:, rows, columns]
    return values.reshape(values.shape[0] * values.shape[1], values.shape[2])


def put_rows(ref, rows, columns, values):
    count = ref.shape[0]
    ref[:, rows, columns] = values.reshape(count, values.shape[0] // count, values.shape[1])


def line_call(body, out_shape, out_specs, in_specs, scratch, number, flops, moved):
    return pl.pallas_call(
        body,
        out_shape=out_shape,
        in_specs=in_specs,
        out_specs=out_specs,
        scratch_shapes=scratch,
        compiler_params=pltpu.CompilerParams(
            collective_id=number, has_side_effects=True, vmem_limit_bytes=VMEM_LIMIT
        ),
        cost_estimate=pl.CostEstimate(flops=flops, bytes_accessed=moved, transcendentals=0),
    )


def pieces_of(rows):
    return 4 if rows % 64 == 0 else 1


def query_key_value(line, weight, bias, tables, mixed):
    cos, sin_up, sin_down = tables
    width = mixed.shape[3]

    def process(piece):
        rows = line.at(piece)

        def columns(kind):
            def run(start, size):
                source = pl.ds(pl.multiple_of(kind * width + start, 128), size)
                result = matmul(flat_rows(line.held, rows), weight[:, source]) + bias[:, source]
                if kind < 2:
                    result = (
                        result * flat_rows(cos, rows, slice(0, size))
                        + pltpu.roll(result, size - ROT // 2, 1) * flat_rows(sin_up, rows, slice(0, size))
                        + pltpu.roll(result, ROT // 2, 1) * flat_rows(sin_down, rows, slice(0, size))
                    )
                if kind == 0:
                    result = result * (1.0 / math.sqrt(HD))
                put_rows(mixed.at[kind], rows, pl.ds(start, size), result.astype(BF16))

            return run

        for kind in range(3):
            each_tile(width, min(256, width), columns(kind))

    return process


def gate_and_up(line, weight, act, slope, silu):
    width = act.shape[2]

    def process(piece):
        rows = line.at(piece)

        def run(start, size):
            at = pl.ds(start, size)
            own = flat_rows(line.held, rows)
            gate = matmul(own, weight[:, at])
            up = matmul(own, weight[:, pl.ds(pl.multiple_of(width + start, 128), size)])
            sigmoid = jax.nn.sigmoid(gate)
            soft = gate * sigmoid
            put_rows(act, rows, at, (soft * up).astype(BF16))
            put_rows(silu, rows, at, soft.astype(BF16))
            put_rows(slope, rows, at, (up * sigmoid * (1.0 + gate * (1.0 - sigmoid))).astype(BF16))

        each_tile(width, 256, run)

    return process


def grad_gate_and_up(line, weight, slope, silu, wide):
    width = slope.shape[2]

    def process(piece):
        rows = line.at(piece)

        def run(start, size):
            at = pl.ds(start, size)
            grad_act = matmul(flat_rows(line.held, rows), weight[at, :], cols_cols)
            put_rows(wide, rows, at, (grad_act * flat_rows(slope, rows, at).astype(F32)).astype(BF16))
            put_rows(
                wide,
                rows,
                pl.ds(pl.multiple_of(width + start, 128), size),
                (grad_act * flat_rows(silu, rows, at).astype(F32)).astype(BF16),
            )

        each_tile(width, 256, run)

    return process


def through_transposed(line, weight, result):
    def process(piece):
        rows = line.at(piece)

        def run(start, size):
            at = pl.ds(start, size)
            put_rows(
                result, rows, at, matmul(flat_rows(line.held, rows), weight[at, :], cols_cols).astype(BF16)
            )

        each_tile(result.shape[2], 256, run)

    return process


def share_of(line, source, weight):
    def term(piece):
        rows = line.at(piece)

        def run(start, size):
            at = pl.ds(start, size)
            put_rows(
                line.shares.at[piece % 2],
                slice(None),
                at,
                matmul(flat_rows(source, rows), weight[:, at]),
            )

        each_tile(line.shares.shape[3], 256, run)

    return term


def share_transposed(line, sources, weight):
    width = sources[0].shape[2]

    def term(piece):
        rows = line.at(piece)

        def run(start, size):
            at = pl.ds(start, size)
            result = matmul(flat_rows(sources[0], rows), weight[at, :width], cols_cols)
            for number in range(1, len(sources)):
                result = result + matmul(
                    flat_rows(sources[number], rows),
                    weight[at, number * width : (number + 1) * width],
                    cols_cols,
                )
            put_rows(line.shares.at[piece % 2], slice(None), at, result)

        each_tile(line.shares.shape[3], 256, run)

    return term


def add_and_norm(line, before, gain, shift, after):
    def finish(piece):
        def rows(at, total):
            hidden = before[at, :] + total
            after[at, :] = hidden
            scaled, _ = norm_rows(hidden)
            line.held[line.place, at, :] = (scaled * gain[...] + shift[...]).astype(BF16)

        line.own_rows(piece, rows)

    return finish


def norm_backward(line, grad, hidden, gain, out, gain_sum, shift_sum):
    gain_sum[...] = jnp.zeros_like(gain_sum)
    shift_sum[...] = jnp.zeros_like(shift_sum)

    def finish(piece):
        def rows(at, grad_normed):
            scaled, inverse = norm_rows(hidden[at, :])
            weighted = grad_normed * gain[...]
            first = jnp.mean(weighted, axis=-1, keepdims=True)
            second = jnp.mean(weighted * scaled, axis=-1, keepdims=True)
            result = grad[at, :] + inverse * (weighted - first - scaled * second)
            out[at, :] = result
            if line.held is not None:
                line.held[line.place, at, :] = result.astype(BF16)
            gain_sum[...] += jnp.sum(grad_normed * scaled, axis=0, keepdims=True)
            shift_sum[...] += jnp.sum(grad_normed, axis=0, keepdims=True)

        line.own_rows(piece, rows)

    return finish


def split(refs, *sizes):
    parts, start = [], 0
    for size in sizes:
        parts.append(refs[start : start + size])
        start += size
    return parts


def first_kernel(count, pieces, *refs):
    (own, weight, bias, *tables), (rows_out, mixed_out), gather, rest = split(refs, 6, 2, 3, 4)
    weight_held, mixed, load_sem, save_sem = rest
    line = Line(count, pieces, None, None, None, None, None, *gather)
    loads = Loads([(weight, weight_held)], load_sem)
    line_barrier(line.place, count)
    saves = Saves([(line.held, rows_out), (mixed, mixed_out)], save_sem, line)
    compute = query_key_value(line, weight_held, bias, tables, mixed)

    def finish(piece):
        rows = line.at(piece)
        line.held[line.place, rows, :] = own[rows, :]

    def process(piece):
        @pl.when(piece == 0)
        def _():
            loads.wait(0)

        compute(piece)
        saves.start(piece)

    line.run(None, finish, process)
    line.drain()
    saves.wait()


def first(count, own, weight, bias, tables, width):
    rows, depth = own.shape
    pieces = pieces_of(rows)
    return line_call(
        functools.partial(first_kernel, count, pieces),
        (
            jax.ShapeDtypeStruct((count, rows, depth), BF16),
            jax.ShapeDtypeStruct((3, count, rows, width), BF16),
        ),
        (hbm, hbm),
        [vmem, hbm, vmem, vmem, vmem, vmem],
        gather_scratch(count, pieces, rows, depth)
        + [
            pltpu.VMEM(weight.shape, BF16),
            pltpu.VMEM((3, count, rows, width), BF16),
            pltpu.SemaphoreType.DMA((1,)),
            pltpu.SemaphoreType.DMA((2, pieces)),
        ],
        0,
        2 * count * rows * weight.size,
        weight.size * 2 + own.size * 2 * count * 4,
    )(own, weight, bias, *tables)


def middle_kernel(count, pieces, *refs):
    ins, outs, scatter, gather, rest = split(refs, 6, 5, 5, 3, 8)
    source, w_out, before, gain, shift, w_up = ins
    after, rows_out, act_out, slope_out, silu_out = outs
    source_held, out_held, up_held, act, slope, silu, load_sem, save_sem = rest
    line = Line(count, pieces, *scatter, *gather)
    loads = Loads([(source, source_held), (w_out, out_held), (w_up, up_held)], load_sem)
    line_barrier(line.place, count)
    saves = Saves(
        [(line.held, rows_out), (act, act_out), (slope, slope_out), (silu, silu_out)], save_sem, line
    )
    compute = gate_and_up(line, up_held, act, slope, silu)

    def process(piece):
        @pl.when(piece == 0)
        def _():
            loads.wait(2)

        compute(piece)
        saves.start(piece)

    loads.wait(0, 1)
    line.run(
        share_of(line, source_held, out_held), add_and_norm(line, before, gain, shift, after), process
    )
    line.drain()
    saves.wait()


def middle(count, source, w_out, before, gain, shift, w_up):
    rows, depth = before.shape
    pieces = pieces_of(rows)
    width = w_up.shape[1] // 2
    wide = jax.ShapeDtypeStruct((count, rows, width), BF16)
    return line_call(
        functools.partial(middle_kernel, count, pieces),
        (
            jax.ShapeDtypeStruct((rows, depth), F32),
            jax.ShapeDtypeStruct((count, rows, depth), BF16),
            wide,
            wide,
            wide,
        ),
        (vmem, hbm, hbm, hbm, hbm),
        [hbm, hbm, vmem, vmem, vmem, hbm],
        scatter_scratch(count, pieces, rows, depth)
        + gather_scratch(count, pieces, rows, depth)
        + [
            pltpu.VMEM(source.shape, BF16),
            pltpu.VMEM(w_out.shape, BF16),
            pltpu.VMEM(w_up.shape, BF16),
            pltpu.VMEM(wide.shape, BF16),
            pltpu.VMEM(wide.shape, BF16),
            pltpu.VMEM(wide.shape, BF16),
            pltpu.SemaphoreType.DMA((3,)),
            pltpu.SemaphoreType.DMA((4, pieces)),
        ],
        1,
        2 * count * rows * (w_out.size + w_up.size),
        (w_out.size + w_up.size) * 2 + before.size * 60,
    )(source, w_out, before, gain, shift, w_up)


def between_kernel(count, pieces, *refs):
    ins, outs, scatter, gather, rest = split(refs, 10, 3, 5, 3, 6)
    source, w_down, before, gain, shift, weight, bias, *tables = ins
    after, rows_out, mixed_out = outs
    source_held, down_held, weight_held, mixed, load_sem, save_sem = rest
    line = Line(count, pieces, *scatter, *gather)
    loads = Loads([(source, source_held), (w_down, down_held), (weight, weight_held)], load_sem)
    line_barrier(line.place, count)
    saves = Saves([(line.held, rows_out), (mixed, mixed_out)], save_sem, line)
    compute = query_key_value(line, weight_held, bias, tables, mixed)

    def process(piece):
        @pl.when(piece == 0)
        def _():
            loads.wait(2)

        compute(piece)
        saves.start(piece)

    loads.wait(0, 1)
    line.run(
        share_of(line, source_held, down_held), add_and_norm(line, before, gain, shift, after), process
    )
    line.drain()
    saves.wait()


def between(count, source, w_down, before, gain, shift, weight, bias, tables):
    rows, depth = before.shape
    pieces = pieces_of(rows)
    mixed = (3, count, rows, weight.shape[1] // 3)
    return line_call(
        functools.partial(between_kernel, count, pieces),
        (
            jax.ShapeDtypeStruct((rows, depth), F32),
            jax.ShapeDtypeStruct((count, rows, depth), BF16),
            jax.ShapeDtypeStruct(mixed, BF16),
        ),
        (vmem, hbm, hbm),
        [hbm, hbm, vmem, vmem, vmem, hbm, vmem, vmem, vmem, vmem],
        scatter_scratch(count, pieces, rows, depth)
        + gather_scratch(count, pieces, rows, depth)
        + [
            pltpu.VMEM(source.shape, BF16),
            pltpu.VMEM(w_down.shape, BF16),
            pltpu.VMEM(weight.shape, BF16),
            pltpu.VMEM(mixed, BF16),
            pltpu.SemaphoreType.DMA((3,)),
            pltpu.SemaphoreType.DMA((2, pieces)),
        ],
        2,
        2 * count * rows * (w_down.size + weight.size),
        (w_down.size + weight.size) * 2 + before.size * 60,
    )(source, w_down, before, gain, shift, weight, bias, *tables)


def turn_kernel(count, pieces, *refs):
    ins, outs, scatter, gather, rest = split(refs, 6, 3, 5, 3, 7)
    source, w_down, before, own, slope_in, silu_in = ins
    after, rows_out, wide_out = outs
    source_held, down_held, slope, silu, wide, load_sem, save_sem = rest
    line = Line(count, pieces, *scatter, *gather)
    loads = Loads(
        [(source, source_held), (w_down, down_held), (slope_in, slope), (silu_in, silu)], load_sem
    )
    line_barrier(line.place, count)
    saves = Saves([(line.held, rows_out), (wide, wide_out)], save_sem, line)
    compute = grad_gate_and_up(line, down_held, slope, silu, wide)

    def finish(piece):
        def rows(at, total):
            after[at, :] = (before[at, :] + total).astype(BF16)
            line.held[line.place, at, :] = own[at, :]

        line.own_rows(piece, rows)

    def process(piece):
        @pl.when(piece == 0)
        def _():
            loads.wait(2, 3)

        compute(piece)
        saves.start(piece)

    loads.wait(0, 1)
    line.run(share_of(line, source_held, down_held), finish, process)
    line.drain()
    saves.wait()


def turn(count, source, w_down, before, own, slope, silu):
    rows, depth = before.shape
    pieces = pieces_of(rows)
    width = w_down.shape[0]
    return line_call(
        functools.partial(turn_kernel, count, pieces),
        (
            jax.ShapeDtypeStruct((rows, depth), BF16),
            jax.ShapeDtypeStruct((count, rows, depth), BF16),
            jax.ShapeDtypeStruct((count, rows, 2 * width), BF16),
        ),
        (vmem, hbm, hbm),
        [hbm, hbm, vmem, vmem, hbm, hbm],
        scatter_scratch(count, pieces, rows, depth)
        + gather_scratch(count, pieces, rows, depth)
        + [
            pltpu.VMEM(source.shape, BF16),
            pltpu.VMEM(w_down.shape, BF16),
            pltpu.VMEM(slope.shape, BF16),
            pltpu.VMEM(silu.shape, BF16),
            pltpu.VMEM((count, rows, 2 * width), BF16),
            pltpu.SemaphoreType.DMA((4,)),
            pltpu.SemaphoreType.DMA((2, pieces)),
        ],
        3,
        4 * count * rows * w_down.size,
        w_down.size * 2 + before.size * 60,
    )(source, w_down, before, own, slope, silu)


def middle_back_kernel(count, pieces, *refs):
    ins, outs, scatter, gather, rest = split(refs, 6, 5, 5, 3, 6)
    source, w_up, grad, hidden, gain, w_out = ins
    out, gain_sum, shift_sum, rows_out, result_out = outs
    source_held, up_held, out_held, result, load_sem, save_sem = rest
    line = Line(count, pieces, *scatter, *gather)
    loads = Loads([(source, source_held), (w_up, up_held), (w_out, out_held)], load_sem)
    line_barrier(line.place, count)
    saves = Saves([(line.held, rows_out), (result, result_out)], save_sem, line)
    compute = through_transposed(line, out_held, result)

    def process(piece):
        @pl.when(piece == 0)
        def _():
            loads.wait(2)

        compute(piece)
        saves.start(piece)

    loads.wait(0, 1)
    line.run(
        share_transposed(line, [source_held], up_held),
        norm_backward(line, grad, hidden, gain, out, gain_sum, shift_sum),
        process,
    )
    line.drain()
    saves.wait()


def middle_back(count, source, w_up, grad, hidden, gain, w_out):
    rows, depth = grad.shape
    pieces = pieces_of(rows)
    width = w_out.shape[0]
    return line_call(
        functools.partial(middle_back_kernel, count, pieces),
        (
            jax.ShapeDtypeStruct((rows, depth), F32),
            jax.ShapeDtypeStruct((1, depth), F32),
            jax.ShapeDtypeStruct((1, depth), F32),
            jax.ShapeDtypeStruct((count, rows, depth), BF16),
            jax.ShapeDtypeStruct((count, rows, width), BF16),
        ),
        (vmem, vmem, vmem, hbm, hbm),
        [hbm, hbm, vmem, vmem, vmem, hbm],
        scatter_scratch(count, pieces, rows, depth)
        + gather_scratch(count, pieces, rows, depth)
        + [
            pltpu.VMEM(source.shape, BF16),
            pltpu.VMEM(w_up.shape, BF16),
            pltpu.VMEM(w_out.shape, BF16),
            pltpu.VMEM((count, rows, width), BF16),
            pltpu.SemaphoreType.DMA((3,)),
            pltpu.SemaphoreType.DMA((2, pieces)),
        ],
        4,
        2 * count * rows * (w_up.size + w_out.size),
        (w_up.size + w_out.size) * 2 + grad.size * 60,
    )(source, w_up, grad, hidden, gain, w_out)


def between_back_kernel(count, pieces, *refs):
    ins, outs, scatter, gather, rest = split(refs, 8, 5, 5, 3, 8)
    source, weight, grad, hidden, gain, w_down, slope_in, silu_in = ins
    out, gain_sum, shift_sum, rows_out, wide_out = outs
    source_held, weight_held, down_held, slope, silu, wide, load_sem, save_sem = rest
    line = Line(count, pieces, *scatter, *gather)
    loads = Loads(
        [
            (source, source_held),
            (weight, weight_held),
            (w_down, down_held),
            (slope_in, slope),
            (silu_in, silu),
        ],
        load_sem,
    )
    line_barrier(line.place, count)
    saves = Saves([(line.held, rows_out), (wide, wide_out)], save_sem, line)
    compute = grad_gate_and_up(line, down_held, slope, silu, wide)

    def process(piece):
        @pl.when(piece == 0)
        def _():
            loads.wait(2, 3, 4)

        compute(piece)
        saves.start(piece)

    loads.wait(0, 1)
    line.run(
        share_transposed(line, [source_held.at[kind] for kind in range(3)], weight_held),
        norm_backward(line, grad, hidden, gain, out, gain_sum, shift_sum),
        process,
    )
    line.drain()
    saves.wait()


def between_back(count, source, weight, grad, hidden, gain, w_down, slope, silu):
    rows, depth = grad.shape
    pieces = pieces_of(rows)
    width = w_down.shape[0]
    return line_call(
        functools.partial(between_back_kernel, count, pieces),
        (
            jax.ShapeDtypeStruct((rows, depth), F32),
            jax.ShapeDtypeStruct((1, depth), F32),
            jax.ShapeDtypeStruct((1, depth), F32),
            jax.ShapeDtypeStruct((count, rows, depth), BF16),
            jax.ShapeDtypeStruct((count, rows, 2 * width), BF16),
        ),
        (vmem, vmem, vmem, hbm, hbm),
        [hbm, hbm, vmem, vmem, vmem, hbm, hbm, hbm],
        scatter_scratch(count, pieces, rows, depth)
        + gather_scratch(count, pieces, rows, depth)
        + [
            pltpu.VMEM(source.shape, BF16),
            pltpu.VMEM(weight.shape, BF16),
            pltpu.VMEM(w_down.shape, BF16),
            pltpu.VMEM(slope.shape, BF16),
            pltpu.VMEM(silu.shape, BF16),
            pltpu.VMEM((count, rows, 2 * width), BF16),
            pltpu.SemaphoreType.DMA((5,)),
            pltpu.SemaphoreType.DMA((2, pieces)),
        ],
        5,
        2 * count * rows * (w_down.size + weight.size),
        (w_down.size + weight.size) * 2 + grad.size * 60,
    )(source, weight, grad, hidden, gain, w_down, slope, silu)


def last_kernel(count, pieces, *refs):
    ins, outs, scatter, rest = split(refs, 5, 3, 5, 3)
    source, weight, grad, hidden, gain = ins
    source_held, weight_held, load_sem = rest
    line = Line(count, pieces, *scatter, None, None, None)
    loads = Loads([(source, source_held), (weight, weight_held)], load_sem)
    line_barrier(line.place, count)
    loads.wait(0, 1)
    line.run(
        share_transposed(line, [source_held.at[kind] for kind in range(3)], weight_held),
        norm_backward(line, grad, hidden, gain, *outs),
        None,
    )
    line.drain()


def last(count, source, weight, grad, hidden, gain):
    rows, depth = grad.shape
    pieces = pieces_of(rows)
    return line_call(
        functools.partial(last_kernel, count, pieces),
        (
            jax.ShapeDtypeStruct((rows, depth), F32),
            jax.ShapeDtypeStruct((1, depth), F32),
            jax.ShapeDtypeStruct((1, depth), F32),
        ),
        (vmem, vmem, vmem),
        [hbm, hbm, vmem, vmem, vmem],
        scatter_scratch(count, pieces, rows, depth)
        + [
            pltpu.VMEM(source.shape, BF16),
            pltpu.VMEM(weight.shape, BF16),
            pltpu.SemaphoreType.DMA((2,)),
        ],
        6,
        2 * count * rows * weight.size,
        weight.size * 2 + grad.size * 20,
    )(source, weight, grad, hidden, gain)


def usable(first, start, keys, queries):
    key_index = lax.broadcasted_iota(jnp.int32, (keys, queries), 0)
    query_index = start + lax.broadcasted_iota(jnp.int32, (keys, queries), 1)
    return (key_index >= first) & (key_index <= query_index)


def head_lanes(values, head):
    lane = lax.broadcasted_iota(jnp.int32, values.shape, 1)
    return jnp.where((lane // HD) == head, values, jnp.zeros_like(values))


def attend_kernel(block, positions, queries, keys, values, attended, logsums):
    length = keys.shape[0]
    values_across = jnp.transpose(values[...])
    for start in range(0, length, block):
        seen = start + block
        at = slice(start, seen)
        own = queries[at, :]
        index = start + lax.broadcasted_iota(jnp.int32, (1, block), 1)
        allowed = usable(index - positions[:, at], start, seen, block)
        halves = []
        for head in range(2):
            scores = matmul(keys[:seen, :], head_lanes(own, head), cols_cols)
            scores = jnp.where(allowed, scores, masked_score)
            highest = jnp.max(scores, axis=0, keepdims=True)
            weights = jnp.exp(scores - highest)
            sums = jnp.sum(weights, axis=0, keepdims=True)
            result = matmul(values_across[:, :seen], weights.astype(BF16))
            halves.append(result[head * HD : (head + 1) * HD, :] / sums)
            logsums[head : head + 1, at] = highest + jnp.log(sums)
        attended[at, :] = jnp.transpose(jnp.concatenate(halves, axis=0)).astype(BF16)


def pair_spec(length, kind):
    return pl.BlockSpec((None, length, PAIR), lambda pair: (kind, 0, pair))


def attend(mixed, positions):
    _, length, width = mixed.shape
    pairs = width // PAIR
    block = min(256, length)
    return pl.pallas_call(
        functools.partial(attend_kernel, block),
        grid=(pairs,),
        out_shape=(
            jax.ShapeDtypeStruct((length, width), BF16),
            jax.ShapeDtypeStruct((pairs, 2, length), F32),
        ),
        in_specs=[
            pl.BlockSpec((1, length), lambda pair: (0, 0)),
            pair_spec(length, 0),
            pair_spec(length, 1),
            pair_spec(length, 2),
        ],
        out_specs=(
            pl.BlockSpec((length, PAIR), lambda pair: (0, pair)),
            pl.BlockSpec((None, 2, length), lambda pair: (pair, 0, 0)),
        ),
        compiler_params=pltpu.CompilerParams(vmem_limit_bytes=VMEM_LIMIT),
        cost_estimate=pl.CostEstimate(
            flops=8 * length * length * width,
            bytes_accessed=8 * length * width,
            transcendentals=length * length * width // HD,
        ),
    )(positions, mixed, mixed, mixed)


def unrotate(values, cos, sin_up, sin_down):
    return (
        values * cos
        - pltpu.roll(values, PAIR - ROT // 2, 1) * sin_up
        - pltpu.roll(values, ROT // 2, 1) * sin_down
    )


def attend_back_kernel(
    block, positions, queries, keys, values, attended, grad_attended, logsums,
    cos, sin_up, sin_down, grad_mixed, bias_sum, grad_keys, grad_values,
):
    length = keys.shape[0]
    keys_across = jnp.transpose(keys[...])
    grad_keys[...] = jnp.zeros_like(grad_keys)
    grad_values[...] = jnp.zeros_like(grad_values)
    bias_sum[...] = jnp.zeros_like(bias_sum)
    for start in range(0, length, block):
        seen = start + block
        at = slice(start, seen)
        own = queries[at, :]
        grad_own = grad_attended[at, :]
        inner = jnp.transpose(grad_own.astype(F32) * attended[at, :].astype(F32))
        index = start + lax.broadcasted_iota(jnp.int32, (1, block), 1)
        allowed = usable(index - positions[:, at], start, seen, block)
        halves = []
        for head in range(2):
            own_head = head_lanes(own, head)
            grad_head = head_lanes(grad_own, head)
            scores = matmul(keys[:seen, :], own_head, cols_cols)
            weights = jnp.where(allowed, jnp.exp(scores - logsums[head : head + 1, at]), 0.0)
            grad_weights = matmul(values[:seen, :], grad_head, cols_cols)
            row_inner = jnp.sum(inner[head * HD : (head + 1) * HD, :], axis=0, keepdims=True)
            grad_scores = (weights * (grad_weights - row_inner)).astype(BF16)
            grad_values[:seen, :] += matmul(weights.astype(BF16), grad_head)
            grad_keys[:seen, :] += matmul(grad_scores, own_head)
            result = matmul(keys_across[:, :seen], grad_scores)
            halves.append(result[head * HD : (head + 1) * HD, :])
        grad_own_queries = jnp.transpose(jnp.concatenate(halves, axis=0)) * (1.0 / math.sqrt(HD))
        low = unrotate(grad_own_queries, cos[at, :], sin_up[at, :], sin_down[at, :]).astype(BF16)
        grad_mixed[0, at, :] = low
        bias_sum[0:1, :] += jnp.sum(low.astype(F32), axis=0, keepdims=True)
    for start in range(0, length, block):
        at = slice(start, start + block)
        low = unrotate(grad_keys[at, :], cos[at, :], sin_up[at, :], sin_down[at, :]).astype(BF16)
        grad_mixed[1, at, :] = low
        bias_sum[1:2, :] += jnp.sum(low.astype(F32), axis=0, keepdims=True)
        low = grad_values[at, :].astype(BF16)
        grad_mixed[2, at, :] = low
        bias_sum[2:3, :] += jnp.sum(low.astype(F32), axis=0, keepdims=True)


def attend_backward(mixed, positions, attended, grad_attended, logsums, tables):
    _, length, width = mixed.shape
    pairs = width // PAIR
    block = min(256, length)
    across = pl.BlockSpec((length, PAIR), lambda pair: (0, pair))
    table = pl.BlockSpec((length, PAIR), lambda pair: (0, 0))
    return pl.pallas_call(
        functools.partial(attend_back_kernel, block),
        grid=(pairs,),
        out_shape=(
            jax.ShapeDtypeStruct((3, length, width), BF16),
            jax.ShapeDtypeStruct((3, width), F32),
        ),
        in_specs=[
            pl.BlockSpec((1, length), lambda pair: (0, 0)),
            pair_spec(length, 0),
            pair_spec(length, 1),
            pair_spec(length, 2),
            across,
            across,
            pl.BlockSpec((None, 2, length), lambda pair: (pair, 0, 0)),
            table,
            table,
            table,
        ],
        out_specs=(
            pl.BlockSpec((3, length, PAIR), lambda pair: (0, 0, pair)),
            pl.BlockSpec((3, PAIR), lambda pair: (0, pair)),
        ),
        scratch_shapes=[pltpu.VMEM((length, PAIR), F32), pltpu.VMEM((length, PAIR), F32)],
        compiler_params=pltpu.CompilerParams(vmem_limit_bytes=VMEM_LIMIT),
        cost_estimate=pl.CostEstimate(
            flops=20 * length * length * width,
            bytes_accessed=16 * length * width,
            transcendentals=length * length * width // HD,
        ),
    )(positions, mixed, mixed, mixed, attended, grad_attended, logsums, *tables)


def rotary_tables(positions, width):
    half_rot = ROT // 2
    frequency = jnp.exp(-(jnp.arange(half_rot, dtype=F32) * 2.0 / ROT) * theta_log)
    angles = positions.astype(F32)[:, None] * frequency[None, :]
    cos, sin = jnp.cos(angles), jnp.sin(angles)
    length = positions.shape[0]
    rest = jnp.ones((length, HD - ROT), F32)
    none, gap = jnp.zeros((length, half_rot), F32), jnp.zeros((length, HD - ROT), F32)
    copies = width // HD
    return (
        jnp.tile(jnp.concatenate([cos, cos, rest], axis=1), (1, copies)),
        jnp.tile(jnp.concatenate([-sin, none, gap], axis=1), (1, copies)),
        jnp.tile(jnp.concatenate([none, sin, gap], axis=1), (1, copies)),
    )


def all_sum(values, axes):
    for axis in axes:
        size = lax.axis_size(axis)
        if size & (size - 1):
            values = lax.psum(values, axis)
            continue
        step = 1
        while step < size:
            values = values + lax.ppermute(values, axis, [(i, i ^ step) for i in range(size)])
            step *= 2
    return values


def owner_sum(part, axis):
    return lax.psum_scatter(part, "dp", scatter_dimension=axis, tiled=True)


def after(values, *others):
    return lax.optimization_barrier((values, *others))


def per_device(
    tokens, positions, norm_gain, norm_bias, w_qkv, b_qkv, w_out, w_gate_up, w_down, cotangent
):
    count = lax.axis_size("tensor")
    tensor_rank = lax.axis_index("tensor")
    width = w_qkv.shape[3]
    ff_local = w_gate_up.shape[3]
    rows, depth = tokens.shape
    length = positions.shape[0]
    tables = rotary_tables(positions, min(256, width))
    pair_tables = tuple(table[:, :PAIR] for table in tables)
    positions_row = positions.reshape(1, length)

    def whole(weight, axis):
        return lax.all_gather(weight, "dp", axis=axis, tiled=True)

    flat = [
        [
            w_qkv[layer].reshape(-1, 3 * width),
            w_out[layer],
            w_gate_up[layer].reshape(-1, 2 * ff_local),
            w_down[layer],
        ]
        for layer in range(LAYERS)
    ]
    axes = (0, 1, 0, 1)
    gathered = [[whole(flat[0][kind], axes[kind]) for kind in range(3)] + [None]]
    hidden = tokens.astype(F32)
    scaled, _ = norm_rows(hidden)
    normed = (scaled * norm_gain[0, 0] + norm_bias[0, 0]).astype(BF16)
    block_tables = tuple(table.reshape(count, rows, -1) for table in tables)
    biases = [
        lax.dynamic_slice_in_dim(b_qkv[layer], tensor_rank * width, width, 1).reshape(1, 3 * width)
        for layer in range(LAYERS)
    ]
    rows_a, mixed = first(count, normed, gathered[0][0], biases[0], block_tables, width)
    mixed, flat[0][3] = after(mixed, flat[0][3])
    gathered[0][3] = whole(flat[0][3], axes[3])
    kept = []
    for layer in range(LAYERS):
        mixed = mixed.reshape(3, length, width)
        attended, logsums = attend(mixed, positions_row)
        if layer + 1 < LAYERS:
            attended, *flat[layer + 1] = after(attended, *flat[layer + 1])
            gathered.append([whole(flat[layer + 1][kind], axes[kind]) for kind in range(4)])
        full_qkv, full_out, full_gu, full_down = gathered[layer]
        hidden_mid, rows_b, act, slope, silu = middle(
            count,
            attended.reshape(count, rows, width),
            full_out,
            hidden,
            norm_gain[layer, 1:2],
            norm_bias[layer, 1:2],
            full_gu,
        )
        kept.append((hidden, rows_a, mixed, attended, logsums, hidden_mid, rows_b, act, slope, silu))
        if layer + 1 < LAYERS:
            hidden, rows_a, mixed = between(
                count,
                act,
                full_down,
                hidden_mid,
                norm_gain[layer + 1, 0:1],
                norm_bias[layer + 1, 0:1],
                gathered[layer + 1][0],
                biases[layer + 1],
                block_tables,
            )
        else:
            activations, grad_rows_b, wide = turn(
                count, act, full_down, hidden_mid, cotangent, slope, silu
            )
    grad = cotangent.astype(F32)
    scattered = [None] * LAYERS
    small = [None] * LAYERS
    for layer in reversed(range(LAYERS)):
        hidden, rows_a, mixed, attended, logsums, hidden_mid, rows_b, act, slope, silu = kept[layer]
        full_qkv, full_out, full_gu, full_down = gathered[layer]
        later = scattered[layer + 1] if layer + 1 < LAYERS else None
        gu_part = matmul(
            rows_b.reshape(length, depth), wide.reshape(length, 2 * ff_local), rows_rows
        ).astype(BF16)
        down_part = matmul(
            act.reshape(length, ff_local), grad_rows_b.reshape(length, depth), rows_rows
        ).astype(BF16)
        wide, down_part, gu_part = after(wide, down_part, gu_part)
        gu_grad, down_grad = owner_sum(gu_part, 0), owner_sum(down_part, 1)
        if later:
            wide, later[2] = after(wide, later[2])
        grad, gain_b, shift_b, grad_rows_a, grad_attended = middle_back(
            count, wide, full_gu, grad, hidden_mid, norm_gain[layer, 1:2], full_out
        )
        out_part = matmul(attended, grad_rows_a.reshape(length, depth), rows_rows).astype(BF16)
        grad_attended, out_part = after(grad_attended, out_part)
        out_grad = owner_sum(out_part, 1)
        if later:
            grad_attended, later[3] = after(grad_attended, later[3])
        grad_mixed, bias_sum = attend_backward(
            mixed, positions_row, attended, grad_attended.reshape(length, width), logsums, pair_tables
        )
        flat_mixed = grad_mixed.transpose(1, 0, 2).reshape(length, 3 * width)
        qkv_part = matmul(rows_a.reshape(length, depth), flat_mixed, rows_rows).astype(BF16)
        grad_mixed, qkv_part = after(grad_mixed, qkv_part)
        qkv_grad = owner_sum(qkv_part, 0)
        if later:
            grad_mixed, later[0], later[1] = after(grad_mixed, later[0], later[1])
        source = grad_mixed.reshape(3, count, rows, width)
        if layer:
            below = kept[layer - 1]
            grad, gain_a, shift_a, grad_rows_b, wide = between_back(
                count,
                source,
                full_qkv,
                grad,
                hidden,
                norm_gain[layer, 0:1],
                gathered[layer - 1][3],
                below[8],
                below[9],
            )
        else:
            grad, gain_a, shift_a = last(count, source, full_qkv, grad, hidden, norm_gain[layer, 0:1])
        bias_full = lax.dynamic_update_slice(
            jnp.zeros((3, b_qkv.shape[2]), F32), bias_sum, (jnp.int32(0), tensor_rank * width)
        )
        small[layer] = jnp.concatenate([gain_a, gain_b, shift_a, shift_b, bias_full], axis=0)
        scattered[layer] = [qkv_grad, out_grad, gu_grad, down_grad]
    sums = all_sum(jnp.stack(small), ("dp", "tensor"))
    shapes = ((-1, 3, width), (width, -1), (-1, 2, ff_local), (ff_local, -1))
    stacks = [
        jnp.stack([scattered[layer][kind].astype(F32).reshape(shape) for layer in range(LAYERS)])
        for kind, shape in enumerate(shapes)
    ]
    return (
        activations,
        grad,
        sums[:, 0:2],
        sums[:, 2:4],
        stacks[0],
        sums[:, 4:7],
        stacks[1],
        stacks[2],
        stacks[3],
    )


def norm_parts(hidden):
    average = jnp.mean(hidden, axis=-1, keepdims=True)
    centred = hidden - average
    variance = jnp.mean(centred * centred, axis=-1, keepdims=True)
    inverse = lax.rsqrt(variance + norm_eps)
    return (centred * inverse, inverse)


def norm_back(grad_normed, scaled, inverse, norm_weight):
    weighted = grad_normed * norm_weight
    first_mean = jnp.mean(weighted, axis=-1, keepdims=True)
    second_mean = jnp.mean(weighted * scaled, axis=-1, keepdims=True)
    grad_input = inverse * (weighted - first_mean - scaled * second_mean)
    return (grad_input, jnp.sum(grad_normed * scaled, axis=0), jnp.sum(grad_normed, axis=0))


def plain_tables(positions):
    half_rot = ROT // 2
    frequency = jnp.exp(-(jnp.arange(half_rot, dtype=jnp.float32) * 2.0 / ROT) * theta_log)
    angles = positions.astype(jnp.float32)[:, None] * frequency[None, :]
    return (jnp.cos(angles)[:, None, :], jnp.sin(angles)[:, None, :])


def rotate(values, cos_table, sin_table):
    half_rot = ROT // 2
    first_half = values[..., :half_rot]
    second_half = values[..., half_rot:ROT]
    return jnp.concatenate(
        [
            first_half * cos_table - second_half * sin_table,
            second_half * cos_table + first_half * sin_table,
            values[..., ROT:],
        ],
        axis=-1,
    )


def inner_rows(left, right):
    return lax.dot_general(left, right, rows_rows, preferred_element_type=jnp.float32)


def inner_cols(left, right):
    return lax.dot_general(left, right, cols_cols, preferred_element_type=jnp.float32)


def block_scores(queries, key_rows, positions, number, block_rows, score_scale):
    seq_len = key_rows.shape[0]
    row_start = number * block_rows
    query_block = lax.dynamic_slice_in_dim(queries, row_start, block_rows, 0)
    scores = (
        jnp.einsum("qhd,khd->hqk", query_block, key_rows, preferred_element_type=jnp.float32)
        * score_scale
    )
    row_index = row_start + jnp.arange(block_rows, dtype=jnp.int32)
    first_key = row_index - lax.dynamic_slice_in_dim(positions, row_start, block_rows, 0)
    columns = jnp.arange(seq_len, dtype=jnp.int32)
    allowed = (columns[None, :] <= row_index[:, None]) & (columns[None, :] >= first_key[:, None])
    return (query_block, allowed, jnp.where(allowed[None], scores, masked_score))


def attend_forward(queries, key_rows, values, positions, score_scale):
    seq_len = queries.shape[0]
    block_rows = min(512, seq_len)

    def one_block(number):
        query_block, allowed, scores = block_scores(
            queries, key_rows, positions, number, block_rows, score_scale
        )
        row_max = jnp.max(scores, axis=-1, keepdims=True)
        shifted = jnp.exp(scores - row_max)
        row_sum = jnp.sum(shifted, axis=-1, keepdims=True)
        weights_low = (shifted / row_sum).astype(jnp.bfloat16)
        block_out = jnp.einsum(
            "hqk,khd->qhd", weights_low, values, preferred_element_type=jnp.float32
        )
        return (block_out, row_max + jnp.log(row_sum))

    block_outs, logsums = lax.map(one_block, jnp.arange(seq_len // block_rows, dtype=jnp.int32))
    return (block_outs.reshape(seq_len, -1), logsums)


def attend_back(queries, key_rows, values, positions, logsums, grad_attended, score_scale):
    seq_len = queries.shape[0]
    block_rows = min(512, seq_len)

    def one_block(totals, inputs):
        grad_keys, grad_values = totals
        number, logsum = inputs
        query_block, allowed, scores = block_scores(
            queries, key_rows, positions, number, block_rows, score_scale
        )
        softmax_rows = jnp.exp(scores - logsum)
        grad_block = lax.dynamic_slice_in_dim(grad_attended, number * block_rows, block_rows, 0)
        grad_probs = jnp.einsum(
            "qhd,khd->hqk", grad_block, values, preferred_element_type=jnp.float32
        )
        grad_values = grad_values + jnp.einsum(
            "hqk,qhd->khd",
            softmax_rows.astype(jnp.bfloat16),
            grad_block,
            preferred_element_type=jnp.float32,
        )
        row_inner = jnp.sum(softmax_rows * grad_probs, axis=-1, keepdims=True)
        grad_scores = jnp.where(allowed[None], softmax_rows * (grad_probs - row_inner), 0.0).astype(
            jnp.bfloat16
        )
        grad_query = (
            jnp.einsum("hqk,khd->qhd", grad_scores, key_rows, preferred_element_type=jnp.float32)
            * score_scale
        )
        grad_keys = (
            grad_keys
            + jnp.einsum(
                "hqk,qhd->khd", grad_scores, query_block, preferred_element_type=jnp.float32
            )
            * score_scale
        )
        return ((grad_keys, grad_values), grad_query)

    empty_grad = jnp.zeros(key_rows.shape, jnp.float32)
    numbers = jnp.arange(seq_len // block_rows, dtype=jnp.int32)
    (grad_keys, grad_values), grad_queries = lax.scan(
        one_block, (empty_grad, empty_grad), (numbers, logsums)
    )
    return (grad_queries.reshape(queries.shape), grad_keys, grad_values)


def per_device_plain(
    tokens, positions, norm_gain, norm_bias, w_qkv, b_qkv, w_out, w_gate_up, w_down, cotangent
):
    tensor_rank = lax.axis_index("tensor")
    width_local = w_qkv.shape[3]
    heads_local = width_local // HD
    ff_local = w_gate_up.shape[3]
    local_rows = tokens.shape[0]
    seq_len = positions.shape[0]
    score_scale = 1.0 / math.sqrt(HD)
    cos_table, sin_table = plain_tables(positions)
    hidden = tokens.astype(jnp.float32)
    kept_state = []
    for layer_index in range(LAYERS):
        gathered = (
            lax.all_gather(w_qkv[layer_index], "dp", axis=0, tiled=True),
            lax.all_gather(w_out[layer_index], "dp", axis=1, tiled=True),
            lax.all_gather(w_gate_up[layer_index], "dp", axis=0, tiled=True),
            lax.all_gather(w_down[layer_index], "dp", axis=1, tiled=True),
        )
        full_qkv, full_out, full_gu, full_down = gathered
        scaled_a, inverse_a = norm_parts(hidden)
        normed_a = (scaled_a * norm_gain[layer_index, 0] + norm_bias[layer_index, 0]).astype(
            jnp.bfloat16
        )
        rows_a = lax.all_gather(normed_a, "tensor", axis=0, tiled=True)
        bias_local = lax.dynamic_slice_in_dim(
            b_qkv[layer_index], tensor_rank * width_local, width_local, 1
        )
        mixed = jnp.dot(
            rows_a,
            full_qkv.reshape(full_qkv.shape[0], 3 * width_local),
            preferred_element_type=jnp.float32,
        ) + bias_local.reshape(3 * width_local)
        mixed = mixed.reshape(seq_len, 3, heads_local, HD)
        queries = rotate(mixed[:, 0], cos_table, sin_table).astype(jnp.bfloat16)
        key_rows = rotate(mixed[:, 1], cos_table, sin_table).astype(jnp.bfloat16)
        values = mixed[:, 2].astype(jnp.bfloat16)
        attended, logsums = attend_forward(queries, key_rows, values, positions, score_scale)
        attended = attended.astype(jnp.bfloat16)

        def project_attn(row_start, row_count, source=attended, weight=full_out):
            return jnp.dot(source, weight, preferred_element_type=jnp.float32)

        branch_a = lax.psum_scatter(
            project_attn(jnp.int32(0), local_rows * lax.axis_size("tensor")).astype(jnp.bfloat16),
            "tensor",
            scatter_dimension=0,
            tiled=True,
        ).astype(jnp.float32)
        hidden_mid = hidden + branch_a
        scaled_b, inverse_b = norm_parts(hidden_mid)
        normed_b = (scaled_b * norm_gain[layer_index, 1] + norm_bias[layer_index, 1]).astype(
            jnp.bfloat16
        )
        rows_b = lax.all_gather(normed_b, "tensor", axis=0, tiled=True)
        gate_up = jnp.dot(
            rows_b,
            full_gu.reshape(full_gu.shape[0], 2 * ff_local),
            preferred_element_type=jnp.float32,
        ).reshape(seq_len, 2, ff_local)
        activated = (jax.nn.silu(gate_up[:, 0]) * gate_up[:, 1]).astype(jnp.bfloat16)

        def project_mlp(row_start, row_count, source=activated, weight=full_down):
            return jnp.dot(source, weight, preferred_element_type=jnp.float32)

        hidden = hidden_mid + lax.psum_scatter(
            project_mlp(jnp.int32(0), local_rows * lax.axis_size("tensor")).astype(jnp.bfloat16),
            "tensor",
            scatter_dimension=0,
            tiled=True,
        ).astype(jnp.float32)
        kept_state.append(
            (
                gathered,
                scaled_a,
                inverse_a,
                rows_a,
                queries,
                key_rows,
                values,
                logsums,
                attended,
                scaled_b,
                inverse_b,
                rows_b,
                gate_up,
                activated,
            )
        )
    activations = hidden.astype(jnp.bfloat16)
    grad = cotangent.astype(jnp.float32)
    weight_parts = [None] * LAYERS
    gain_rows = [None] * LAYERS
    shift_rows = [None] * LAYERS
    qkv_shift_rows = [None] * LAYERS
    for layer_index in reversed(range(LAYERS)):
        (
            gathered,
            scaled_a,
            inverse_a,
            rows_a,
            queries,
            key_rows,
            values,
            logsums,
            attended,
            scaled_b,
            inverse_b,
            rows_b,
            gate_up,
            activated,
        ) = kept_state[layer_index]
        full_qkv, full_out, full_gu, full_down = (
            lax.all_gather(w_qkv[layer_index], "dp", axis=0, tiled=True),
            lax.all_gather(w_out[layer_index], "dp", axis=1, tiled=True),
            lax.all_gather(w_gate_up[layer_index], "dp", axis=0, tiled=True),
            lax.all_gather(w_down[layer_index], "dp", axis=1, tiled=True),
        )
        grad_rows_b = lax.all_gather(grad.astype(jnp.bfloat16), "tensor", axis=0, tiled=True)
        grad_down_weight = inner_rows(activated, grad_rows_b)
        grad_act = inner_cols(grad_rows_b, full_down)
        gate_part = gate_up[:, 0]
        up_part = gate_up[:, 1]
        sigmoid_gate = jax.nn.sigmoid(gate_part)
        grad_gate = grad_act * up_part * sigmoid_gate * (1.0 + gate_part * (1.0 - sigmoid_gate))
        grad_up = grad_act * jax.nn.silu(gate_part)
        grad_gate_up = (
            jnp.stack([grad_gate, grad_up], axis=1)
            .astype(jnp.bfloat16)
            .reshape(seq_len, 2 * ff_local)
        )
        grad_gu_weight = inner_rows(rows_b, grad_gate_up).reshape(full_gu.shape)
        flat_gu = full_gu.reshape(full_gu.shape[0], 2 * ff_local)

        def back_mlp(row_start, row_count, source=grad_gate_up, weight=flat_gu):
            return inner_cols(source, weight)

        grad_normed_b = lax.psum_scatter(
            back_mlp(jnp.int32(0), local_rows * lax.axis_size("tensor")).astype(jnp.bfloat16),
            "tensor",
            scatter_dimension=0,
            tiled=True,
        ).astype(jnp.float32)
        grad_in_b, gain_b, shift_b = norm_back(
            grad_normed_b, scaled_b, inverse_b, norm_gain[layer_index, 1]
        )
        grad = grad + grad_in_b
        grad_rows_a = lax.all_gather(grad.astype(jnp.bfloat16), "tensor", axis=0, tiled=True)
        grad_out_weight = inner_rows(attended, grad_rows_a)
        grad_attended = inner_cols(grad_rows_a, full_out).astype(jnp.bfloat16)
        grad_attended = grad_attended.reshape(seq_len, heads_local, HD)
        grad_queries, grad_keys, grad_values = attend_back(
            queries, key_rows, values, positions, logsums, grad_attended, score_scale
        )
        grad_queries = rotate(grad_queries, cos_table, -sin_table)
        grad_keys = rotate(grad_keys, cos_table, -sin_table)
        grad_mixed = jnp.stack([grad_queries, grad_keys, grad_values], axis=1)
        grad_mixed = grad_mixed.reshape(seq_len, 3 * width_local).astype(jnp.bfloat16)
        qkv_shift_local = jnp.sum(grad_mixed, axis=0, dtype=jnp.float32).reshape(3, width_local)
        qkv_shift_rows[layer_index] = lax.dynamic_update_slice(
            jnp.zeros((3, b_qkv.shape[2]), jnp.float32),
            qkv_shift_local,
            (jnp.int32(0), tensor_rank * width_local),
        )
        grad_qkv_weight = inner_rows(rows_a, grad_mixed).reshape(full_qkv.shape)
        flat_qkv = full_qkv.reshape(full_qkv.shape[0], 3 * width_local)

        def back_attn(row_start, row_count, source=grad_mixed, weight=flat_qkv):
            return inner_cols(source, weight)

        grad_normed_a = lax.psum_scatter(
            back_attn(jnp.int32(0), local_rows * lax.axis_size("tensor")).astype(jnp.bfloat16),
            "tensor",
            scatter_dimension=0,
            tiled=True,
        ).astype(jnp.float32)
        grad_in_a, gain_a, shift_a = norm_back(
            grad_normed_a, scaled_a, inverse_a, norm_gain[layer_index, 0]
        )
        grad = grad + grad_in_a
        gain_rows[layer_index] = jnp.stack([gain_a, gain_b])
        shift_rows[layer_index] = jnp.stack([shift_a, shift_b])
        weight_parts[layer_index] = (
            lax.psum_scatter(
                grad_qkv_weight.astype(jnp.bfloat16), "dp", scatter_dimension=0, tiled=True
            ).astype(jnp.float32),
            lax.psum_scatter(
                grad_out_weight.astype(jnp.bfloat16), "dp", scatter_dimension=1, tiled=True
            ).astype(jnp.float32),
            lax.psum_scatter(
                grad_gu_weight.astype(jnp.bfloat16), "dp", scatter_dimension=0, tiled=True
            ).astype(jnp.float32),
            lax.psum_scatter(
                grad_down_weight.astype(jnp.bfloat16), "dp", scatter_dimension=1, tiled=True
            ).astype(jnp.float32),
        )
    stack_qkv = jnp.stack([weight_parts[number][0] for number in range(LAYERS)])
    stack_out = jnp.stack([weight_parts[number][1] for number in range(LAYERS)])
    stack_gu = jnp.stack([weight_parts[number][2] for number in range(LAYERS)])
    stack_down = jnp.stack([weight_parts[number][3] for number in range(LAYERS)])
    gain_grad, norm_bias_grad, qkv_bias_grad = lax.psum(
        (jnp.stack(gain_rows), jnp.stack(shift_rows), jnp.stack(qkv_shift_rows)), ("dp", "tensor")
    )
    return (
        activations,
        grad,
        gain_grad,
        norm_bias_grad,
        stack_qkv,
        qkv_bias_grad,
        stack_out,
        stack_gu,
        stack_down,
    )


def solution(mesh):
    in_specs = (
        P(("dp", "tensor"), None),
        P("dp"),
        P(),
        P(),
        P(None, "dp", None, "tensor"),
        P(),
        P(None, "tensor", "dp"),
        P(None, "dp", None, "tensor"),
        P(None, "tensor", "dp"),
        P(("dp", "tensor"), None),
    )
    out_specs = (
        P(("dp", "tensor"), None),
        P(("dp", "tensor"), None),
        P(),
        P(),
        P(None, "dp", None, "tensor"),
        P(),
        P(None, "tensor", "dp"),
        P(None, "dp", None, "tensor"),
        P(None, "tensor", "dp"),
    )
    def run(*operands):
        fits = operands[7].shape[3] % 128 == 0 and operands[4].shape[3] % PAIR == 0
        return (per_device if fits else per_device_plain)(*operands)

    return jax.shard_map(
        run, mesh=mesh, in_specs=in_specs, out_specs=out_specs, check_vma=False
    )
```

```python
import functools
import math

import jax
import jax.numpy as jnp
from jax import lax
from jax.experimental import pallas as pl
from jax.experimental.pallas import tpu as pltpu
from jax.sharding import PartitionSpec as P

HD = 64
ROT = 16
LAYERS = 2
PAIR = 2 * HD
MESH = pl.DeviceIdType.MESH
F32 = jnp.float32
BF16 = jnp.bfloat16
VMEM_LIMIT = 62 * 2**20
LAG = 6

norm_eps = 1e-05
theta_log = math.log(10000.0)
masked_score = -1e30
rows_rows = (((0,), (0,)), ((), ()))
cols_cols = (((1,), (1,)), ((), ()))
rows_cols = (((1,), (0,)), ((), ()))


def matmul(left, right, dims=rows_cols):
    return lax.dot_general(left, right, dims, preferred_element_type=F32)


def line_barrier(place, count, others=()):
    barrier = pltpu.get_barrier_semaphore()
    for other in others:
        pl.semaphore_signal(barrier, inc=1, device_id={"dp": other}, device_id_type=MESH)

    @pl.when(place > 0)
    def _():
        pl.semaphore_signal(barrier, inc=1, device_id={"tensor": place - 1}, device_id_type=MESH)

    @pl.when(place < count - 1)
    def _():
        pl.semaphore_signal(barrier, inc=1, device_id={"tensor": place + 1}, device_id_type=MESH)

    middle = (place > 0) & (place < count - 1)

    @pl.when(middle)
    def _():
        pl.semaphore_wait(barrier, 2 + len(others))

    @pl.when(jnp.logical_not(middle))
    def _():
        pl.semaphore_wait(barrier, 1 + len(others))


def each_tile(width, tile, run):
    def one(number, carry):
        run(pl.multiple_of(number * tile, tile), tile)
        return carry

    lax.fori_loop(0, width // tile, one, 0)
    if width % tile:
        run(width // tile * tile, width % tile)


class Line:
    def __init__(self, count, pieces, shares, sending, arrived, sum_send, sum_recv, held, send_sem, recv_sem):
        self.count, self.pieces = count, pieces
        self.shares, self.sending, self.arrived = shares, sending, arrived
        self.sum_send, self.sum_recv = sum_send, sum_recv
        self.held, self.send_sem, self.recv_sem = held, send_sem, recv_sem
        self.place = lax.axis_index("tensor")
        self.rows = (held if held is not None else sending).shape[1] // pieces

    def at(self, piece):
        return pl.ds(pl.multiple_of(piece * self.rows, self.rows), self.rows)

    def sum_hop(self, piece, owner):
        right = owner > self.place
        target = jnp.where(right, self.place + 1, self.place - 1)
        slot = jnp.where(right | (owner != target), owner, self.count)
        return pltpu.make_async_remote_copy(
            src_ref=self.sending.at[owner, self.at(piece)],
            dst_ref=self.arrived.at[slot, self.at(piece)],
            send_sem=self.sum_send.at[owner, piece],
            recv_sem=self.sum_recv.at[slot, piece],
            device_id={"tensor": target},
            device_id_type=MESH,
        )

    def sum_landed(self, piece, slot):
        return pltpu.make_async_remote_copy(
            src_ref=self.sending.at[0, self.at(piece)],
            dst_ref=self.arrived.at[slot, self.at(piece)],
            send_sem=self.sum_send.at[0, piece],
            recv_sem=self.sum_recv.at[slot, piece],
            device_id={"tensor": self.place},
            device_id_type=MESH,
        )

    def row_hop(self, piece, block, right):
        return pltpu.make_async_remote_copy(
            src_ref=self.held.at[block, self.at(piece)],
            dst_ref=self.held.at[block, self.at(piece)],
            send_sem=self.send_sem.at[jnp.where(right, 0, 1), block, piece],
            recv_sem=self.recv_sem.at[block, piece],
            device_id={"tensor": jnp.where(right, self.place + 1, self.place - 1)},
            device_id_type=MESH,
        )

    def sides(self, away, run):
        def one(side, carry):
            block = jnp.where(side == 0, self.place + away, self.place - away)

            @pl.when((block >= 0) & (block < self.count))
            def _():
                run(block, side == 0)

            return carry

        lax.fori_loop(0, 2, one, 0)

    def chunks(self, run):
        chunk = min(16, self.rows)

        def one(number, carry):
            run(pl.multiple_of(number * chunk, chunk), chunk)
            return carry

        lax.fori_loop(0, self.rows // chunk, one, 0)

    def pass_on(self, piece, owner, right):
        first = pl.multiple_of(piece * self.rows, self.rows)
        onward = jnp.where(right, self.place > 0, self.place < self.count - 1)

        @pl.when(onward)
        def _():
            self.sum_landed(piece, owner).wait_recv()

            def rows(start, size):
                at = pl.ds(pl.multiple_of(first + start, size), size)
                self.sending[owner, at, :] = (
                    self.shares[owner, at, :]
                    + self.arrived[owner, at, :].astype(F32)
                ).astype(BF16)

            self.chunks(rows)

        @pl.when(jnp.logical_not(onward))
        def _():
            def rows(start, size):
                at = pl.ds(pl.multiple_of(first + start, size), size)
                self.sending[owner, at, :] = self.shares[owner, at, :].astype(BF16)

            self.chunks(rows)

        self.sum_hop(piece, owner).start()

    def collect(self, piece):
        first = pl.multiple_of(piece * self.rows, self.rows)

        def add(slot):
            self.sum_landed(piece, slot).wait_recv()

            def rows(start, size):
                at = pl.ds(pl.multiple_of(first + start, size), size)
                self.shares[self.place, at, :] = self.shares[self.place, at, :] + self.arrived[
                    slot, at, :
                ].astype(F32)

            self.chunks(rows)

        @pl.when(self.place > 0)
        def _():
            add(self.place)

        @pl.when(self.place < self.count - 1)
        def _():
            add(self.count)

    def own_rows(self, piece, run):
        first = pl.multiple_of(piece * self.rows, self.rows)

        def rows(start, size):
            at = pl.ds(pl.multiple_of(first + start, size), size)
            run(at, self.shares[self.place, at, :])

        self.chunks(rows)

    def run(self, term, finish, process, each_tick=None):
        count, pieces, place = self.count, self.pieces, self.place
        scatter, gather = term is not None, process is not None
        lead = count - 1 if scatter else 0
        if scatter:
            term(0)

        def tick(number, carry):
            if each_tick is not None:
                each_tick(number)

            def valid(piece):
                return (piece >= 0) & (piece < pieces)

            if scatter:

                def sum_step(step, inner):
                    piece = number - step

                    @pl.when(valid(piece))
                    def _():
                        self.sides(
                            count - 1 - step,
                            lambda owner, right: self.pass_on(piece, owner, right),
                        )

                    return inner

                lax.fori_loop(0, count - 1, sum_step, 0)
            mine = number - lead

            @pl.when(valid(mine))
            def _():
                if scatter:
                    self.collect(mine)
                finish(mine)
                if gather:

                    @pl.when(place < count - 1)
                    def _():
                        self.row_hop(mine, place, True).start()

                    @pl.when(place > 0)
                    def _():
                        self.row_hop(mine, place, False).start()

            if gather:

                def row_step(step, inner):
                    piece = mine - step

                    def forward(block, right):
                        self.row_hop(piece, block, True).wait_recv()
                        onward = jnp.where(right, place > 0, place < count - 1)

                        @pl.when(onward)
                        def _():
                            self.row_hop(piece, block, jnp.logical_not(right)).start()

                    @pl.when(valid(piece))
                    def _():
                        self.sides(step, forward)

                    return inner

                lax.fori_loop(1, count, row_step, 0)
            if scatter:

                @pl.when(number + 1 < pieces)
                def _():
                    term(number + 1)

            if gather:

                @pl.when(valid(mine - (count - 1)))
                def _():
                    process(mine - (count - 1))

            return carry

        lax.fori_loop(0, pieces + lead + (count - 1 if gather else 0), tick, 0)

    def drain(self):
        def piece_sends(piece, carry):
            def owner_sends(owner, inner):
                if self.sending is not None:

                    @pl.when(owner != self.place)
                    def _():
                        self.sum_hop(piece, owner).wait_send()

                if self.held is not None:

                    @pl.when((owner <= self.place) & (self.place < self.count - 1))
                    def _():
                        self.row_hop(piece, owner, True).wait_send()

                    @pl.when((owner >= self.place) & (self.place > 0))
                    def _():
                        self.row_hop(piece, owner, False).wait_send()

                return inner

            lax.fori_loop(0, self.count, owner_sends, 0)
            return carry

        lax.fori_loop(0, self.pieces, piece_sends, 0)


def norm_rows(values):
    average = jnp.mean(values, axis=-1, keepdims=True)
    centred = values - average
    variance = jnp.mean(centred * centred, axis=-1, keepdims=True)
    inverse = lax.rsqrt(variance + norm_eps)
    return centred * inverse, inverse


def scatter_scratch(count, pieces, rows, width):
    return [
        pltpu.VMEM((count, rows, width), F32),
        pltpu.VMEM((count, rows, width), BF16),
        pltpu.VMEM((count + 1, rows, width), BF16),
        pltpu.SemaphoreType.DMA((count, pieces)),
        pltpu.SemaphoreType.DMA((count + 1, pieces)),
    ]


def gather_scratch(count, pieces, rows, width):
    return [
        pltpu.VMEM((count, rows, width), BF16),
        pltpu.SemaphoreType.DMA((2, count, pieces)),
        pltpu.SemaphoreType.DMA((count, pieces)),
    ]


vmem = pl.BlockSpec(memory_space=pltpu.VMEM)
hbm = pl.BlockSpec(memory_space=pl.ANY)


class Loads:
    def __init__(self, pairs, sems):
        self.copies = [
            pltpu.make_async_copy(source, target, sems.at[number])
            for number, (source, target) in enumerate(pairs)
        ]
        for copy in self.copies:
            copy.start()

    def wait(self, *numbers):
        for number in numbers:
            self.copies[number].wait()


class Saves:
    def __init__(self, pairs, sems, line):
        self.pairs, self.sems, self.line = pairs, sems, line

    def copy(self, number, piece):
        source, target = self.pairs[number]
        rows = self.line.at(piece)
        where = (slice(None),) * (len(source.shape) - 2) + (rows,)
        return pltpu.make_async_copy(
            source.at[where], target.at[where], self.sems.at[number, piece]
        )

    def start(self, piece):
        for number in range(len(self.pairs)):
            self.copy(number, piece).start()

    def wait(self):
        for number in range(len(self.pairs)):
            for piece in range(self.line.pieces):
                self.copy(number, piece).wait()


def flat_rows(ref, rows, columns=slice(None)):
    values = ref[:, rows, columns]
    return values.reshape(values.shape[0] * values.shape[1], values.shape[2])


def put_rows(ref, rows, columns, values):
    count = ref.shape[0]
    ref[:, rows, columns] = values.reshape(count, values.shape[0] // count, values.shape[1])


def line_call(body, out_shape, out_specs, in_specs, scratch, number, flops, moved):
    return pl.pallas_call(
        body,
        out_shape=out_shape,
        in_specs=in_specs,
        out_specs=out_specs,
        scratch_shapes=scratch,
        compiler_params=pltpu.CompilerParams(
            collective_id=number, has_side_effects=True, vmem_limit_bytes=VMEM_LIMIT
        ),
        cost_estimate=pl.CostEstimate(flops=flops, bytes_accessed=moved, transcendentals=0),
    )


def pieces_of(rows):
    return 4 if rows % 64 == 0 else 1


def query_key_value(line, weight, bias, tables, mixed):
    cos, sin_up, sin_down = tables
    width = mixed.shape[3]

    def process(piece):
        rows = line.at(piece)

        def columns(kind):
            def run(start, size):
                source = pl.ds(pl.multiple_of(kind * width + start, 128), size)
                result = matmul(flat_rows(line.held, rows), weight[:, source]) + bias[:, source]
                if kind < 2:
                    result = (
                        result * flat_rows(cos, rows, slice(0, size))
                        + pltpu.roll(result, size - ROT // 2, 1) * flat_rows(sin_up, rows, slice(0, size))
                        + pltpu.roll(result, ROT // 2, 1) * flat_rows(sin_down, rows, slice(0, size))
                    )
                if kind == 0:
                    result = result * (1.0 / math.sqrt(HD))
                put_rows(mixed.at[kind], rows, pl.ds(start, size), result.astype(BF16))

            return run

        for kind in range(3):
            each_tile(width, min(256, width), columns(kind))

    return process


def gate_and_up(line, weight, act, slope, silu):
    width = act.shape[2]

    def process(piece):
        rows = line.at(piece)

        def run(start, size):
            at = pl.ds(start, size)
            own = flat_rows(line.held, rows)
            gate = matmul(own, weight[:, at])
            up = matmul(own, weight[:, pl.ds(pl.multiple_of(width + start, 128), size)])
            sigmoid = jax.nn.sigmoid(gate)
            soft = gate * sigmoid
            put_rows(act, rows, at, (soft * up).astype(BF16))
            put_rows(silu, rows, at, soft.astype(BF16))
            put_rows(slope, rows, at, (up * sigmoid * (1.0 + gate * (1.0 - sigmoid))).astype(BF16))

        each_tile(width, 256, run)

    return process


def grad_gate_and_up(line, weight, slope, silu, wide):
    width = slope.shape[2]

    def process(piece):
        rows = line.at(piece)

        def run(start, size):
            at = pl.ds(start, size)
            grad_act = matmul(flat_rows(line.held, rows), weight[at, :], cols_cols)
            put_rows(wide, rows, at, (grad_act * flat_rows(slope, rows, at).astype(F32)).astype(BF16))
            put_rows(
                wide,
                rows,
                pl.ds(pl.multiple_of(width + start, 128), size),
                (grad_act * flat_rows(silu, rows, at).astype(F32)).astype(BF16),
            )

        each_tile(width, 256, run)

    return process


def through_transposed(line, weight, result):
    def process(piece):
        rows = line.at(piece)

        def run(start, size):
            at = pl.ds(start, size)
            put_rows(
                result, rows, at, matmul(flat_rows(line.held, rows), weight[at, :], cols_cols).astype(BF16)
            )

        each_tile(result.shape[2], 256, run)

    return process


def share_of(line, source, weight):
    def term(piece):
        rows = line.at(piece)

        def run(start, size):
            at = pl.ds(start, size)
            put_rows(line.shares, rows, at, matmul(flat_rows(source, rows), weight[:, at]))

        each_tile(line.shares.shape[2], 256, run)

    return term


def share_transposed(line, sources, weight):
    width = sources[0].shape[2]

    def term(piece):
        rows = line.at(piece)

        def run(start, size):
            at = pl.ds(start, size)
            result = matmul(flat_rows(sources[0], rows), weight[at, :width], cols_cols)
            for number in range(1, len(sources)):
                result = result + matmul(
                    flat_rows(sources[number], rows),
                    weight[at, number * width : (number + 1) * width],
                    cols_cols,
                )
            put_rows(line.shares, rows, at, result)

        each_tile(line.shares.shape[2], 256, run)

    return term


def add_and_norm(line, before, gain, shift, after):
    def finish(piece):
        def rows(at, total):
            hidden = before[at, :] + total
            after[at, :] = hidden
            scaled, _ = norm_rows(hidden)
            line.held[line.place, at, :] = (scaled * gain[...] + shift[...]).astype(BF16)

        line.own_rows(piece, rows)

    return finish


def norm_backward(line, grad, hidden, gain, out, gain_sum, shift_sum):
    gain_sum[...] = jnp.zeros_like(gain_sum)
    shift_sum[...] = jnp.zeros_like(shift_sum)

    def finish(piece):
        def rows(at, grad_normed):
            scaled, inverse = norm_rows(hidden[at, :])
            weighted = grad_normed * gain[...]
            first = jnp.mean(weighted, axis=-1, keepdims=True)
            second = jnp.mean(weighted * scaled, axis=-1, keepdims=True)
            result = grad[at, :] + inverse * (weighted - first - scaled * second)
            out[at, :] = result
            if line.held is not None:
                line.held[line.place, at, :] = result.astype(BF16)
            gain_sum[...] += jnp.sum(grad_normed * scaled, axis=0, keepdims=True)
            shift_sum[...] += jnp.sum(grad_normed, axis=0, keepdims=True)

        line.own_rows(piece, rows)

    return finish


def split(refs, *sizes):
    parts, start = [], 0
    for size in sizes:
        parts.append(refs[start : start + size])
        start += size
    return parts


def first_kernel(count, pieces, *refs):
    (own, weight, bias, *tables), (rows_out, mixed_out), gather, rest = split(refs, 6, 2, 3, 4)
    weight_held, mixed, load_sem, save_sem = rest
    line = Line(count, pieces, None, None, None, None, None, *gather)
    loads = Loads([(weight, weight_held)], load_sem)
    line_barrier(line.place, count)
    saves = Saves([(line.held, rows_out), (mixed, mixed_out)], save_sem, line)
    compute = query_key_value(line, weight_held, bias, tables, mixed)

    def finish(piece):
        rows = line.at(piece)
        line.held[line.place, rows, :] = own[rows, :]

    def process(piece):
        @pl.when(piece == 0)
        def _():
            loads.wait(0)

        compute(piece)
        saves.start(piece)

    line.run(None, finish, process)

    line.drain()
    saves.wait()


def first(count, own, weight, bias, tables, width):
    rows, depth = own.shape
    pieces = pieces_of(rows)
    return line_call(
        functools.partial(first_kernel, count, pieces),
        (
            jax.ShapeDtypeStruct((count, rows, depth), BF16),
            jax.ShapeDtypeStruct((3, count, rows, width), BF16),
        ),
        (hbm, hbm),
        [vmem, hbm, vmem, vmem, vmem, vmem],
        gather_scratch(count, pieces, rows, depth)
        + [
            pltpu.VMEM(weight.shape, BF16),
            pltpu.VMEM((3, count, rows, width), BF16),
            pltpu.SemaphoreType.DMA((1,)),
            pltpu.SemaphoreType.DMA((2, pieces)),
        ],
        0,
        2 * count * rows * weight.size,
        weight.size * 2 + own.size * 2 * count * 4,
    )(own, weight, bias, *tables)


def middle_kernel(count, pieces, lag, *refs):
    ins, outs, scatter, gather, rest = split(refs, 6, 5, 5, 3, 9)
    source, w_out, before, gain, shift, w_up = ins
    after, rows_out, act_out, slope_out, silu_out = outs
    source_held, out_held, up_held, act, slope, silu, load_sem, save_sem, turn = rest
    line = Line(count, pieces, *scatter, *gather)
    loads = Loads([(source, source_held), (w_out, out_held), (w_up, up_held)], load_sem)
    member = lax.axis_index("dp")
    core = member % 2
    partner = member + 1 - 2 * core
    line_barrier(line.place, count, (partner,) if lag else ())
    saves = Saves(
        [(line.held, rows_out), (act, act_out), (slope, slope_out), (silu, silu_out)], save_sem, line
    )
    compute = gate_and_up(line, up_held, act, slope, silu)

    def process(piece):
        @pl.when(piece == 0)
        def _():
            loads.wait(2)

        compute(piece)
        saves.start(piece)

    def signal(number):
        @pl.when((core == 0) & (number == lag))
        def _():
            pl.semaphore_signal(turn, inc=1, device_id={"dp": partner}, device_id_type=MESH)

    loads.wait(0, 1)
    if lag:

        @pl.when(core == 1)
        def _():
            pl.semaphore_wait(turn, 1)

    line.run(
        share_of(line, source_held, out_held),
        add_and_norm(line, before, gain, shift, after),
        process,
        signal if lag else None,
    )
    line.drain()
    saves.wait()


def middle(count, source, w_out, before, gain, shift, w_up, lag=0):
    rows, depth = before.shape
    pieces = pieces_of(rows)
    width = w_up.shape[1] // 2
    wide = jax.ShapeDtypeStruct((count, rows, width), BF16)
    return line_call(
        functools.partial(middle_kernel, count, pieces, lag),
        (
            jax.ShapeDtypeStruct((rows, depth), F32),
            jax.ShapeDtypeStruct((count, rows, depth), BF16),
            wide,
            wide,
            wide,
        ),
        (vmem, hbm, hbm, hbm, hbm),
        [hbm, hbm, vmem, vmem, vmem, hbm],
        scatter_scratch(count, pieces, rows, depth)
        + gather_scratch(count, pieces, rows, depth)
        + [
            pltpu.VMEM(source.shape, BF16),
            pltpu.VMEM(w_out.shape, BF16),
            pltpu.VMEM(w_up.shape, BF16),
            pltpu.VMEM(wide.shape, BF16),
            pltpu.VMEM(wide.shape, BF16),
            pltpu.VMEM(wide.shape, BF16),
            pltpu.SemaphoreType.DMA((3,)),
            pltpu.SemaphoreType.DMA((4, pieces)),
            pltpu.SemaphoreType.REGULAR,
        ],
        7 if lag else 1,
        2 * count * rows * (w_out.size + w_up.size),
        (w_out.size + w_up.size) * 2 + before.size * 60,
    )(source, w_out, before, gain, shift, w_up)


def between_kernel(count, pieces, *refs):
    ins, outs, scatter, gather, rest = split(refs, 10, 3, 5, 3, 6)
    source, w_down, before, gain, shift, weight, bias, *tables = ins
    after, rows_out, mixed_out = outs
    source_held, down_held, weight_held, mixed, load_sem, save_sem = rest
    line = Line(count, pieces, *scatter, *gather)
    loads = Loads([(source, source_held), (w_down, down_held), (weight, weight_held)], load_sem)
    line_barrier(line.place, count)
    saves = Saves([(line.held, rows_out), (mixed, mixed_out)], save_sem, line)
    compute = query_key_value(line, weight_held, bias, tables, mixed)

    def process(piece):
        @pl.when(piece == 0)
        def _():
            loads.wait(2)

        compute(piece)
        saves.start(piece)

    loads.wait(0, 1)
    line.run(
        share_of(line, source_held, down_held), add_and_norm(line, before, gain, shift, after), process
    )
    line.drain()
    saves.wait()


def between(count, source, w_down, before, gain, shift, weight, bias, tables):
    rows, depth = before.shape
    pieces = pieces_of(rows)
    mixed = (3, count, rows, weight.shape[1] // 3)
    return line_call(
        functools.partial(between_kernel, count, pieces),
        (
            jax.ShapeDtypeStruct((rows, depth), F32),
            jax.ShapeDtypeStruct((count, rows, depth), BF16),
            jax.ShapeDtypeStruct(mixed, BF16),
        ),
        (vmem, hbm, hbm),
        [hbm, hbm, vmem, vmem, vmem, hbm, vmem, vmem, vmem, vmem],
        scatter_scratch(count, pieces, rows, depth)
        + gather_scratch(count, pieces, rows, depth)
        + [
            pltpu.VMEM(source.shape, BF16),
            pltpu.VMEM(w_down.shape, BF16),
            pltpu.VMEM(weight.shape, BF16),
            pltpu.VMEM(mixed, BF16),
            pltpu.SemaphoreType.DMA((3,)),
            pltpu.SemaphoreType.DMA((2, pieces)),
        ],
        2,
        2 * count * rows * (w_down.size + weight.size),
        (w_down.size + weight.size) * 2 + before.size * 60,
    )(source, w_down, before, gain, shift, weight, bias, *tables)


def turn_kernel(count, pieces, *refs):
    ins, outs, scatter, gather, rest = split(refs, 6, 3, 5, 3, 7)
    source, w_down, before, own, slope_in, silu_in = ins
    after, rows_out, wide_out = outs
    source_held, down_held, slope, silu, wide, load_sem, save_sem = rest
    line = Line(count, pieces, *scatter, *gather)
    loads = Loads(
        [(source, source_held), (w_down, down_held), (slope_in, slope), (silu_in, silu)], load_sem
    )
    line_barrier(line.place, count)
    saves = Saves([(line.held, rows_out), (wide, wide_out)], save_sem, line)
    compute = grad_gate_and_up(line, down_held, slope, silu, wide)

    def finish(piece):
        def rows(at, total):
            after[at, :] = (before[at, :] + total).astype(BF16)
            line.held[line.place, at, :] = own[at, :]

        line.own_rows(piece, rows)

    def process(piece):
        @pl.when(piece == 0)
        def _():
            loads.wait(2, 3)

        compute(piece)
        saves.start(piece)

    loads.wait(0, 1)
    line.run(share_of(line, source_held, down_held), finish, process)
    line.drain()
    saves.wait()


def turn(count, source, w_down, before, own, slope, silu):
    rows, depth = before.shape
    pieces = pieces_of(rows)
    width = w_down.shape[0]
    return line_call(
        functools.partial(turn_kernel, count, pieces),
        (
            jax.ShapeDtypeStruct((rows, depth), BF16),
            jax.ShapeDtypeStruct((count, rows, depth), BF16),
            jax.ShapeDtypeStruct((count, rows, 2 * width), BF16),
        ),
        (vmem, hbm, hbm),
        [hbm, hbm, vmem, vmem, hbm, hbm],
        scatter_scratch(count, pieces, rows, depth)
        + gather_scratch(count, pieces, rows, depth)
        + [
            pltpu.VMEM(source.shape, BF16),
            pltpu.VMEM(w_down.shape, BF16),
            pltpu.VMEM(slope.shape, BF16),
            pltpu.VMEM(silu.shape, BF16),
            pltpu.VMEM((count, rows, 2 * width), BF16),
            pltpu.SemaphoreType.DMA((4,)),
            pltpu.SemaphoreType.DMA((2, pieces)),
        ],
        3,
        4 * count * rows * w_down.size,
        w_down.size * 2 + before.size * 60,
    )(source, w_down, before, own, slope, silu)


def middle_back_kernel(count, pieces, *refs):
    ins, outs, scatter, gather, rest = split(refs, 6, 5, 5, 3, 6)
    source, w_up, grad, hidden, gain, w_out = ins
    out, gain_sum, shift_sum, rows_out, result_out = outs
    source_held, up_held, out_held, result, load_sem, save_sem = rest
    line = Line(count, pieces, *scatter, *gather)
    loads = Loads([(source, source_held), (w_up, up_held), (w_out, out_held)], load_sem)
    line_barrier(line.place, count)
    saves = Saves([(line.held, rows_out), (result, result_out)], save_sem, line)
    compute = through_transposed(line, out_held, result)

    def process(piece):
        @pl.when(piece == 0)
        def _():
            loads.wait(2)

        compute(piece)
        saves.start(piece)

    loads.wait(0, 1)
    line.run(
        share_transposed(line, [source_held], up_held),
        norm_backward(line, grad, hidden, gain, out, gain_sum, shift_sum),
        process,
    )
    line.drain()
    saves.wait()


def middle_back(count, source, w_up, grad, hidden, gain, w_out):
    rows, depth = grad.shape
    pieces = pieces_of(rows)
    width = w_out.shape[0]
    return line_call(
        functools.partial(middle_back_kernel, count, pieces),
        (
            jax.ShapeDtypeStruct((rows, depth), F32),
            jax.ShapeDtypeStruct((1, depth), F32),
            jax.ShapeDtypeStruct((1, depth), F32),
            jax.ShapeDtypeStruct((count, rows, depth), BF16),
            jax.ShapeDtypeStruct((count, rows, width), BF16),
        ),
        (vmem, vmem, vmem, hbm, hbm),
        [hbm, hbm, vmem, vmem, vmem, hbm],
        scatter_scratch(count, pieces, rows, depth)
        + gather_scratch(count, pieces, rows, depth)
        + [
            pltpu.VMEM(source.shape, BF16),
            pltpu.VMEM(w_up.shape, BF16),
            pltpu.VMEM(w_out.shape, BF16),
            pltpu.VMEM((count, rows, width), BF16),
            pltpu.SemaphoreType.DMA((3,)),
            pltpu.SemaphoreType.DMA((2, pieces)),
        ],
        4,
        2 * count * rows * (w_up.size + w_out.size),
        (w_up.size + w_out.size) * 2 + grad.size * 60,
    )(source, w_up, grad, hidden, gain, w_out)


def between_back_kernel(count, pieces, *refs):
    ins, outs, scatter, gather, rest = split(refs, 8, 5, 5, 3, 8)
    source, weight, grad, hidden, gain, w_down, slope_in, silu_in = ins
    out, gain_sum, shift_sum, rows_out, wide_out = outs
    source_held, weight_held, down_held, slope, silu, wide, load_sem, save_sem = rest
    line = Line(count, pieces, *scatter, *gather)
    loads = Loads(
        [
            (source, source_held),
            (weight, weight_held),
            (w_down, down_held),
            (slope_in, slope),
            (silu_in, silu),
        ],
        load_sem,
    )
    line_barrier(line.place, count)
    saves = Saves([(line.held, rows_out), (wide, wide_out)], save_sem, line)
    compute = grad_gate_and_up(line, down_held, slope, silu, wide)

    def process(piece):
        @pl.when(piece == 0)
        def _():
            loads.wait(2, 3, 4)

        compute(piece)
        saves.start(piece)

    loads.wait(0, 1)
    line.run(
        share_transposed(line, [source_held.at[kind] for kind in range(3)], weight_held),
        norm_backward(line, grad, hidden, gain, out, gain_sum, shift_sum),
        process,
    )
    line.drain()
    saves.wait()


def between_back(count, source, weight, grad, hidden, gain, w_down, slope, silu):
    rows, depth = grad.shape
    pieces = pieces_of(rows)
    width = w_down.shape[0]
    return line_call(
        functools.partial(between_back_kernel, count, pieces),
        (
            jax.ShapeDtypeStruct((rows, depth), F32),
            jax.ShapeDtypeStruct((1, depth), F32),
            jax.ShapeDtypeStruct((1, depth), F32),
            jax.ShapeDtypeStruct((count, rows, depth), BF16),
            jax.ShapeDtypeStruct((count, rows, 2 * width), BF16),
        ),
        (vmem, vmem, vmem, hbm, hbm),
        [hbm, hbm, vmem, vmem, vmem, hbm, hbm, hbm],
        scatter_scratch(count, pieces, rows, depth)
        + gather_scratch(count, pieces, rows, depth)
        + [
            pltpu.VMEM(source.shape, BF16),
            pltpu.VMEM(weight.shape, BF16),
            pltpu.VMEM(w_down.shape, BF16),
            pltpu.VMEM(slope.shape, BF16),
            pltpu.VMEM(silu.shape, BF16),
            pltpu.VMEM((count, rows, 2 * width), BF16),
            pltpu.SemaphoreType.DMA((5,)),
            pltpu.SemaphoreType.DMA((2, pieces)),
        ],
        5,
        2 * count * rows * (w_down.size + weight.size),
        (w_down.size + weight.size) * 2 + grad.size * 60,
    )(source, weight, grad, hidden, gain, w_down, slope, silu)


def last_kernel(count, pieces, *refs):
    ins, outs, scatter, rest = split(refs, 5, 3, 5, 3)
    source, weight, grad, hidden, gain = ins
    source_held, weight_held, load_sem = rest
    line = Line(count, pieces, *scatter, None, None, None)
    loads = Loads([(source, source_held), (weight, weight_held)], load_sem)
    line_barrier(line.place, count)
    loads.wait(0, 1)
    line.run(
        share_transposed(line, [source_held.at[kind] for kind in range(3)], weight_held),
        norm_backward(line, grad, hidden, gain, *outs),
        None,
    )
    line.drain()


def last(count, source, weight, grad, hidden, gain):
    rows, depth = grad.shape
    pieces = pieces_of(rows)
    return line_call(
        functools.partial(last_kernel, count, pieces),
        (
            jax.ShapeDtypeStruct((rows, depth), F32),
            jax.ShapeDtypeStruct((1, depth), F32),
            jax.ShapeDtypeStruct((1, depth), F32),
        ),
        (vmem, vmem, vmem),
        [hbm, hbm, vmem, vmem, vmem],
        scatter_scratch(count, pieces, rows, depth)
        + [
            pltpu.VMEM(source.shape, BF16),
            pltpu.VMEM(weight.shape, BF16),
            pltpu.SemaphoreType.DMA((2,)),
        ],
        6,
        2 * count * rows * weight.size,
        weight.size * 2 + grad.size * 20,
    )(source, weight, grad, hidden, gain)


def usable(first, start, keys, queries):
    key_index = lax.broadcasted_iota(jnp.int32, (keys, queries), 0)
    query_index = start + lax.broadcasted_iota(jnp.int32, (keys, queries), 1)
    return (key_index >= first) & (key_index <= query_index)


def head_lanes(values, head):
    lane = lax.broadcasted_iota(jnp.int32, values.shape, 1)
    return jnp.where((lane // HD) == head, values, jnp.zeros_like(values))


def attend_kernel(block, positions, queries, keys, values, attended, logsums):
    length = keys.shape[0]
    values_across = jnp.transpose(values[...])
    for start in range(0, length, block):
        seen = start + block
        at = slice(start, seen)
        own = queries[at, :]
        index = start + lax.broadcasted_iota(jnp.int32, (1, block), 1)
        allowed = usable(index - positions[:, at], start, seen, block)
        halves = []
        for head in range(2):
            scores = matmul(keys[:seen, :], head_lanes(own, head), cols_cols)
            scores = jnp.where(allowed, scores, masked_score)
            highest = jnp.max(scores, axis=0, keepdims=True)
            weights = jnp.exp(scores - highest)
            sums = jnp.sum(weights, axis=0, keepdims=True)
            result = matmul(values_across[:, :seen], weights.astype(BF16))
            halves.append(result[head * HD : (head + 1) * HD, :] / sums)
            logsums[head : head + 1, at] = highest + jnp.log(sums)
        attended[at, :] = jnp.transpose(jnp.concatenate(halves, axis=0)).astype(BF16)


def pair_spec(length, kind):
    return pl.BlockSpec((None, length, PAIR), lambda pair: (kind, 0, pair))


def attend(mixed, positions):
    _, length, width = mixed.shape
    pairs = width // PAIR
    block = min(256, length)
    return pl.pallas_call(
        functools.partial(attend_kernel, block),
        grid=(pairs,),
        out_shape=(
            jax.ShapeDtypeStruct((length, width), BF16),
            jax.ShapeDtypeStruct((pairs, 2, length), F32),
        ),
        in_specs=[
            pl.BlockSpec((1, length), lambda pair: (0, 0)),
            pair_spec(length, 0),
            pair_spec(length, 1),
            pair_spec(length, 2),
        ],
        out_specs=(
            pl.BlockSpec((length, PAIR), lambda pair: (0, pair)),
            pl.BlockSpec((None, 2, length), lambda pair: (pair, 0, 0)),
        ),
        compiler_params=pltpu.CompilerParams(vmem_limit_bytes=VMEM_LIMIT),
        cost_estimate=pl.CostEstimate(
            flops=8 * length * length * width,
            bytes_accessed=8 * length * width,
            transcendentals=length * length * width // HD,
        ),
    )(positions, mixed, mixed, mixed)


def unrotate(values, cos, sin_up, sin_down):
    return (
        values * cos
        - pltpu.roll(values, PAIR - ROT // 2, 1) * sin_up
        - pltpu.roll(values, ROT // 2, 1) * sin_down
    )


def attend_back_kernel(
    block, positions, queries, keys, values, attended, grad_attended, logsums,
    cos, sin_up, sin_down, grad_mixed, bias_sum, grad_keys, grad_values,
):
    length = keys.shape[0]
    keys_across = jnp.transpose(keys[...])
    grad_keys[...] = jnp.zeros_like(grad_keys)
    grad_values[...] = jnp.zeros_like(grad_values)
    bias_sum[...] = jnp.zeros_like(bias_sum)
    for start in range(0, length, block):
        seen = start + block
        at = slice(start, seen)
        own = queries[at, :]
        grad_own = grad_attended[at, :]
        inner = jnp.transpose(grad_own.astype(F32) * attended[at, :].astype(F32))
        index = start + lax.broadcasted_iota(jnp.int32, (1, block), 1)
        allowed = usable(index - positions[:, at], start, seen, block)
        halves = []
        for head in range(2):
            own_head = head_lanes(own, head)
            grad_head = head_lanes(grad_own, head)
            scores = matmul(keys[:seen, :], own_head, cols_cols)
            weights = jnp.where(allowed, jnp.exp(scores - logsums[head : head + 1, at]), 0.0)
            grad_weights = matmul(values[:seen, :], grad_head, cols_cols)
            row_inner = jnp.sum(inner[head * HD : (head + 1) * HD, :], axis=0, keepdims=True)
            grad_scores = (weights * (grad_weights - row_inner)).astype(BF16)
            grad_values[:seen, :] += matmul(weights.astype(BF16), grad_head)
            grad_keys[:seen, :] += matmul(grad_scores, own_head)
            result = matmul(keys_across[:, :seen], grad_scores)
            halves.append(result[head * HD : (head + 1) * HD, :])
        grad_own_queries = jnp.transpose(jnp.concatenate(halves, axis=0)) * (1.0 / math.sqrt(HD))
        low = unrotate(grad_own_queries, cos[at, :], sin_up[at, :], sin_down[at, :]).astype(BF16)
        grad_mixed[0, at, :] = low
        bias_sum[0:1, :] += jnp.sum(low.astype(F32), axis=0, keepdims=True)
    for start in range(0, length, block):
        at = slice(start, start + block)
        low = unrotate(grad_keys[at, :], cos[at, :], sin_up[at, :], sin_down[at, :]).astype(BF16)
        grad_mixed[1, at, :] = low
        bias_sum[1:2, :] += jnp.sum(low.astype(F32), axis=0, keepdims=True)
        low = grad_values[at, :].astype(BF16)
        grad_mixed[2, at, :] = low
        bias_sum[2:3, :] += jnp.sum(low.astype(F32), axis=0, keepdims=True)


def attend_backward(mixed, positions, attended, grad_attended, logsums, tables):
    _, length, width = mixed.shape
    pairs = width // PAIR
    block = min(256, length)
    across = pl.BlockSpec((length, PAIR), lambda pair: (0, pair))
    table = pl.BlockSpec((length, PAIR), lambda pair: (0, 0))
    return pl.pallas_call(
        functools.partial(attend_back_kernel, block),
        grid=(pairs,),
        out_shape=(
            jax.ShapeDtypeStruct((3, length, width), BF16),
            jax.ShapeDtypeStruct((3, width), F32),
        ),
        in_specs=[
            pl.BlockSpec((1, length), lambda pair: (0, 0)),
            pair_spec(length, 0),
            pair_spec(length, 1),
            pair_spec(length, 2),
            across,
            across,
            pl.BlockSpec((None, 2, length), lambda pair: (pair, 0, 0)),
            table,
            table,
            table,
        ],
        out_specs=(
            pl.BlockSpec((3, length, PAIR), lambda pair: (0, 0, pair)),
            pl.BlockSpec((3, PAIR), lambda pair: (0, pair)),
        ),
        scratch_shapes=[pltpu.VMEM((length, PAIR), F32), pltpu.VMEM((length, PAIR), F32)],
        compiler_params=pltpu.CompilerParams(vmem_limit_bytes=VMEM_LIMIT),
        cost_estimate=pl.CostEstimate(
            flops=20 * length * length * width,
            bytes_accessed=16 * length * width,
            transcendentals=length * length * width // HD,
        ),
    )(positions, mixed, mixed, mixed, attended, grad_attended, logsums, *tables)


def rotary_tables(positions, width):
    half_rot = ROT // 2
    frequency = jnp.exp(-(jnp.arange(half_rot, dtype=F32) * 2.0 / ROT) * theta_log)
    angles = positions.astype(F32)[:, None] * frequency[None, :]
    cos, sin = jnp.cos(angles), jnp.sin(angles)
    length = positions.shape[0]
    rest = jnp.ones((length, HD - ROT), F32)
    none, gap = jnp.zeros((length, half_rot), F32), jnp.zeros((length, HD - ROT), F32)
    copies = width // HD
    return (
        jnp.tile(jnp.concatenate([cos, cos, rest], axis=1), (1, copies)),
        jnp.tile(jnp.concatenate([-sin, none, gap], axis=1), (1, copies)),
        jnp.tile(jnp.concatenate([none, sin, gap], axis=1), (1, copies)),
    )


def all_sum(values, axes):
    for axis in axes:
        size = lax.axis_size(axis)
        if size & (size - 1):
            values = lax.psum(values, axis)
            continue
        step = 1
        while step < size:
            values = values + lax.ppermute(values, axis, [(i, i ^ step) for i in range(size)])
            step *= 2
    return values


def owner_sum(part, axis):
    return lax.psum_scatter(part, "dp", scatter_dimension=axis, tiled=True)


def after(values, *others):
    return lax.optimization_barrier((values, *others))


def per_device(
    tokens, positions, norm_gain, norm_bias, w_qkv, b_qkv, w_out, w_gate_up, w_down, cotangent
):
    count = lax.axis_size("tensor")
    tensor_rank = lax.axis_index("tensor")
    width = w_qkv.shape[3]
    ff_local = w_gate_up.shape[3]
    rows, depth = tokens.shape
    length = positions.shape[0]
    tables = rotary_tables(positions, min(256, width))
    pair_tables = tuple(table[:, :PAIR] for table in tables)
    positions_row = positions.reshape(1, length)

    def whole(weight, axis):
        return lax.all_gather(weight, "dp", axis=axis, tiled=True)

    flat = [
        [
            w_qkv[layer].reshape(-1, 3 * width),
            w_out[layer],
            w_gate_up[layer].reshape(-1, 2 * ff_local),
            w_down[layer],
        ]
        for layer in range(LAYERS)
    ]
    axes = (0, 1, 0, 1)
    gathered = [[whole(flat[0][kind], axes[kind]) for kind in range(3)] + [None]]
    hidden = tokens.astype(F32)
    scaled, _ = norm_rows(hidden)
    normed = (scaled * norm_gain[0, 0] + norm_bias[0, 0]).astype(BF16)
    block_tables = tuple(table.reshape(count, rows, -1) for table in tables)
    biases = [
        lax.dynamic_slice_in_dim(b_qkv[layer], tensor_rank * width, width, 1).reshape(1, 3 * width)
        for layer in range(LAYERS)
    ]
    rows_a, mixed = first(count, normed, gathered[0][0], biases[0], block_tables, width)
    mixed, flat[0][3] = after(mixed, flat[0][3])
    gathered[0][3] = whole(flat[0][3], axes[3])
    kept = []
    for layer in range(LAYERS):
        mixed = mixed.reshape(3, length, width)
        attended, logsums = attend(mixed, positions_row)
        if layer + 1 < LAYERS:
            attended, *flat[layer + 1] = after(attended, *flat[layer + 1])
            gathered.append([whole(flat[layer + 1][kind], axes[kind]) for kind in range(4)])
        full_qkv, full_out, full_gu, full_down = gathered[layer]
        hidden_mid, rows_b, act, slope, silu = middle(
            count,
            attended.reshape(count, rows, width),
            full_out,
            hidden,
            norm_gain[layer, 1:2],
            norm_bias[layer, 1:2],
            full_gu,
            LAG if layer == 0 else 0,
        )
        kept.append((hidden, rows_a, mixed, attended, logsums, hidden_mid, rows_b, act, slope, silu))
        if layer + 1 < LAYERS:
            hidden, rows_a, mixed = between(
                count,
                act,
                full_down,
                hidden_mid,
                norm_gain[layer + 1, 0:1],
                norm_bias[layer + 1, 0:1],
                gathered[layer + 1][0],
                biases[layer + 1],
                block_tables,
            )
        else:
            activations, grad_rows_b, wide = turn(
                count, act, full_down, hidden_mid, cotangent, slope, silu
            )
    grad = cotangent.astype(F32)
    scattered = [None] * LAYERS
    small = [None] * LAYERS
    for layer in reversed(range(LAYERS)):
        hidden, rows_a, mixed, attended, logsums, hidden_mid, rows_b, act, slope, silu = kept[layer]
        full_qkv, full_out, full_gu, full_down = gathered[layer]
        later = scattered[layer + 1] if layer + 1 < LAYERS else None
        gu_part = matmul(
            rows_b.reshape(length, depth), wide.reshape(length, 2 * ff_local), rows_rows
        ).astype(BF16)
        down_part = matmul(
            act.reshape(length, ff_local), grad_rows_b.reshape(length, depth), rows_rows
        ).astype(BF16)
        wide, down_part, gu_part = after(wide, down_part, gu_part)
        gu_grad, down_grad = owner_sum(gu_part, 0), owner_sum(down_part, 1)
        if later:
            wide, later[2] = after(wide, later[2])
        grad, gain_b, shift_b, grad_rows_a, grad_attended = middle_back(
            count, wide, full_gu, grad, hidden_mid, norm_gain[layer, 1:2], full_out
        )
        out_part = matmul(attended, grad_rows_a.reshape(length, depth), rows_rows).astype(BF16)
        grad_attended, out_part = after(grad_attended, out_part)
        out_grad = owner_sum(out_part, 1)
        if later:
            grad_attended, later[3] = after(grad_attended, later[3])
        grad_mixed, bias_sum = attend_backward(
            mixed, positions_row, attended, grad_attended.reshape(length, width), logsums, pair_tables
        )
        flat_mixed = grad_mixed.transpose(1, 0, 2).reshape(length, 3 * width)
        qkv_part = matmul(rows_a.reshape(length, depth), flat_mixed, rows_rows).astype(BF16)
        grad_mixed, qkv_part = after(grad_mixed, qkv_part)
        qkv_grad = owner_sum(qkv_part, 0)
        if later:
            grad_mixed, later[0], later[1] = after(grad_mixed, later[0], later[1])
        source = grad_mixed.reshape(3, count, rows, width)
        if layer:
            below = kept[layer - 1]
            grad, gain_a, shift_a, grad_rows_b, wide = between_back(
                count,
                source,
                full_qkv,
                grad,
                hidden,
                norm_gain[layer, 0:1],
                gathered[layer - 1][3],
                below[8],
                below[9],
            )
        else:
            grad, gain_a, shift_a = last(count, source, full_qkv, grad, hidden, norm_gain[layer, 0:1])
        bias_full = lax.dynamic_update_slice(
            jnp.zeros((3, b_qkv.shape[2]), F32), bias_sum, (jnp.int32(0), tensor_rank * width)
        )
        small[layer] = jnp.concatenate([gain_a, gain_b, shift_a, shift_b, bias_full], axis=0)
        scattered[layer] = [qkv_grad, out_grad, gu_grad, down_grad]
    sums = all_sum(jnp.stack(small), ("dp", "tensor"))
    shapes = ((-1, 3, width), (width, -1), (-1, 2, ff_local), (ff_local, -1))
    stacks = [
        jnp.stack([scattered[layer][kind].astype(F32).reshape(shape) for layer in range(LAYERS)])
        for kind, shape in enumerate(shapes)
    ]
    return (
        activations,
        grad,
        sums[:, 0:2],
        sums[:, 2:4],
        stacks[0],
        sums[:, 4:7],
        stacks[1],
        stacks[2],
        stacks[3],
    )


def norm_parts(hidden):
    average = jnp.mean(hidden, axis=-1, keepdims=True)
    centred = hidden - average
    variance = jnp.mean(centred * centred, axis=-1, keepdims=True)
    inverse = lax.rsqrt(variance + norm_eps)
    return (centred * inverse, inverse)


def norm_back(grad_normed, scaled, inverse, norm_weight):
    weighted = grad_normed * norm_weight
    first_mean = jnp.mean(weighted, axis=-1, keepdims=True)
    second_mean = jnp.mean(weighted * scaled, axis=-1, keepdims=True)
    grad_input = inverse * (weighted - first_mean - scaled * second_mean)
    return (grad_input, jnp.sum(grad_normed * scaled, axis=0), jnp.sum(grad_normed, axis=0))


def plain_tables(positions):
    half_rot = ROT // 2
    frequency = jnp.exp(-(jnp.arange(half_rot, dtype=jnp.float32) * 2.0 / ROT) * theta_log)
    angles = positions.astype(jnp.float32)[:, None] * frequency[None, :]
    return (jnp.cos(angles)[:, None, :], jnp.sin(angles)[:, None, :])


def rotate(values, cos_table, sin_table):
    half_rot = ROT // 2
    first_half = values[..., :half_rot]
    second_half = values[..., half_rot:ROT]
    return jnp.concatenate(
        [
            first_half * cos_table - second_half * sin_table,
            second_half * cos_table + first_half * sin_table,
            values[..., ROT:],
        ],
        axis=-1,
    )


def inner_rows(left, right):
    return lax.dot_general(left, right, rows_rows, preferred_element_type=jnp.float32)


def inner_cols(left, right):
    return lax.dot_general(left, right, cols_cols, preferred_element_type=jnp.float32)


def block_scores(queries, key_rows, positions, number, block_rows, score_scale):
    seq_len = key_rows.shape[0]
    row_start = number * block_rows
    query_block = lax.dynamic_slice_in_dim(queries, row_start, block_rows, 0)
    scores = (
        jnp.einsum("qhd,khd->hqk", query_block, key_rows, preferred_element_type=jnp.float32)
        * score_scale
    )
    row_index = row_start + jnp.arange(block_rows, dtype=jnp.int32)
    first_key = row_index - lax.dynamic_slice_in_dim(positions, row_start, block_rows, 0)
    columns = jnp.arange(seq_len, dtype=jnp.int32)
    allowed = (columns[None, :] <= row_index[:, None]) & (columns[None, :] >= first_key[:, None])
    return (query_block, allowed, jnp.where(allowed[None], scores, masked_score))


def attend_forward(queries, key_rows, values, positions, score_scale):
    seq_len = queries.shape[0]
    block_rows = min(512, seq_len)

    def one_block(number):
        query_block, allowed, scores = block_scores(
            queries, key_rows, positions, number, block_rows, score_scale
        )
        row_max = jnp.max(scores, axis=-1, keepdims=True)
        shifted = jnp.exp(scores - row_max)
        row_sum = jnp.sum(shifted, axis=-1, keepdims=True)
        weights_low = (shifted / row_sum).astype(jnp.bfloat16)
        block_out = jnp.einsum(
            "hqk,khd->qhd", weights_low, values, preferred_element_type=jnp.float32
        )
        return (block_out, row_max + jnp.log(row_sum))

    block_outs, logsums = lax.map(one_block, jnp.arange(seq_len // block_rows, dtype=jnp.int32))
    return (block_outs.reshape(seq_len, -1), logsums)


def attend_back(queries, key_rows, values, positions, logsums, grad_attended, score_scale):
    seq_len = queries.shape[0]
    block_rows = min(512, seq_len)

    def one_block(totals, inputs):
        grad_keys, grad_values = totals
        number, logsum = inputs
        query_block, allowed, scores = block_scores(
            queries, key_rows, positions, number, block_rows, score_scale
        )
        softmax_rows = jnp.exp(scores - logsum)
        grad_block = lax.dynamic_slice_in_dim(grad_attended, number * block_rows, block_rows, 0)
        grad_probs = jnp.einsum(
            "qhd,khd->hqk", grad_block, values, preferred_element_type=jnp.float32
        )
        grad_values = grad_values + jnp.einsum(
            "hqk,qhd->khd",
            softmax_rows.astype(jnp.bfloat16),
            grad_block,
            preferred_element_type=jnp.float32,
        )
        row_inner = jnp.sum(softmax_rows * grad_probs, axis=-1, keepdims=True)
        grad_scores = jnp.where(allowed[None], softmax_rows * (grad_probs - row_inner), 0.0).astype(
            jnp.bfloat16
        )
        grad_query = (
            jnp.einsum("hqk,khd->qhd", grad_scores, key_rows, preferred_element_type=jnp.float32)
            * score_scale
        )
        grad_keys = (
            grad_keys
            + jnp.einsum(
                "hqk,qhd->khd", grad_scores, query_block, preferred_element_type=jnp.float32
            )
            * score_scale
        )
        return ((grad_keys, grad_values), grad_query)

    empty_grad = jnp.zeros(key_rows.shape, jnp.float32)
    numbers = jnp.arange(seq_len // block_rows, dtype=jnp.int32)
    (grad_keys, grad_values), grad_queries = lax.scan(
        one_block, (empty_grad, empty_grad), (numbers, logsums)
    )
    return (grad_queries.reshape(queries.shape), grad_keys, grad_values)


def per_device_plain(
    tokens, positions, norm_gain, norm_bias, w_qkv, b_qkv, w_out, w_gate_up, w_down, cotangent
):
    tensor_rank = lax.axis_index("tensor")
    width_local = w_qkv.shape[3]
    heads_local = width_local // HD
    ff_local = w_gate_up.shape[3]
    local_rows = tokens.shape[0]
    seq_len = positions.shape[0]
    score_scale = 1.0 / math.sqrt(HD)
    cos_table, sin_table = plain_tables(positions)
    hidden = tokens.astype(jnp.float32)
    kept_state = []
    for layer_index in range(LAYERS):
        gathered = (
            lax.all_gather(w_qkv[layer_index], "dp", axis=0, tiled=True),
            lax.all_gather(w_out[layer_index], "dp", axis=1, tiled=True),
            lax.all_gather(w_gate_up[layer_index], "dp", axis=0, tiled=True),
            lax.all_gather(w_down[layer_index], "dp", axis=1, tiled=True),
        )
        full_qkv, full_out, full_gu, full_down = gathered
        scaled_a, inverse_a = norm_parts(hidden)
        normed_a = (scaled_a * norm_gain[layer_index, 0] + norm_bias[layer_index, 0]).astype(
            jnp.bfloat16
        )
        rows_a = lax.all_gather(normed_a, "tensor", axis=0, tiled=True)
        bias_local = lax.dynamic_slice_in_dim(
            b_qkv[layer_index], tensor_rank * width_local, width_local, 1
        )
        mixed = jnp.dot(
            rows_a,
            full_qkv.reshape(full_qkv.shape[0], 3 * width_local),
            preferred_element_type=jnp.float32,
        ) + bias_local.reshape(3 * width_local)
        mixed = mixed.reshape(seq_len, 3, heads_local, HD)
        queries = rotate(mixed[:, 0], cos_table, sin_table).astype(jnp.bfloat16)
        key_rows = rotate(mixed[:, 1], cos_table, sin_table).astype(jnp.bfloat16)
        values = mixed[:, 2].astype(jnp.bfloat16)
        attended, logsums = attend_forward(queries, key_rows, values, positions, score_scale)
        attended = attended.astype(jnp.bfloat16)

        def project_attn(row_start, row_count, source=attended, weight=full_out):
            return jnp.dot(source, weight, preferred_element_type=jnp.float32)

        branch_a = lax.psum_scatter(
            project_attn(jnp.int32(0), local_rows * lax.axis_size("tensor")).astype(jnp.bfloat16),
            "tensor",
            scatter_dimension=0,
            tiled=True,
        ).astype(jnp.float32)
        hidden_mid = hidden + branch_a
        scaled_b, inverse_b = norm_parts(hidden_mid)
        normed_b = (scaled_b * norm_gain[layer_index, 1] + norm_bias[layer_index, 1]).astype(
            jnp.bfloat16
        )
        rows_b = lax.all_gather(normed_b, "tensor", axis=0, tiled=True)
        gate_up = jnp.dot(
            rows_b,
            full_gu.reshape(full_gu.shape[0], 2 * ff_local),
            preferred_element_type=jnp.float32,
        ).reshape(seq_len, 2, ff_local)
        activated = (jax.nn.silu(gate_up[:, 0]) * gate_up[:, 1]).astype(jnp.bfloat16)

        def project_mlp(row_start, row_count, source=activated, weight=full_down):
            return jnp.dot(source, weight, preferred_element_type=jnp.float32)

        hidden = hidden_mid + lax.psum_scatter(
            project_mlp(jnp.int32(0), local_rows * lax.axis_size("tensor")).astype(jnp.bfloat16),
            "tensor",
            scatter_dimension=0,
            tiled=True,
        ).astype(jnp.float32)
        kept_state.append(
            (
                gathered,
                scaled_a,
                inverse_a,
                rows_a,
                queries,
                key_rows,
                values,
                logsums,
                attended,
                scaled_b,
                inverse_b,
                rows_b,
                gate_up,
                activated,
            )
        )
    activations = hidden.astype(jnp.bfloat16)
    grad = cotangent.astype(jnp.float32)
    weight_parts = [None] * LAYERS
    gain_rows = [None] * LAYERS
    shift_rows = [None] * LAYERS
    qkv_shift_rows = [None] * LAYERS
    for layer_index in reversed(range(LAYERS)):
        (
            gathered,
            scaled_a,
            inverse_a,
            rows_a,
            queries,
            key_rows,
            values,
            logsums,
            attended,
            scaled_b,
            inverse_b,
            rows_b,
            gate_up,
            activated,
        ) = kept_state[layer_index]
        full_qkv, full_out, full_gu, full_down = (
            lax.all_gather(w_qkv[layer_index], "dp", axis=0, tiled=True),
            lax.all_gather(w_out[layer_index], "dp", axis=1, tiled=True),
            lax.all_gather(w_gate_up[layer_index], "dp", axis=0, tiled=True),
            lax.all_gather(w_down[layer_index], "dp", axis=1, tiled=True),
        )
        grad_rows_b = lax.all_gather(grad.astype(jnp.bfloat16), "tensor", axis=0, tiled=True)
        grad_down_weight = inner_rows(activated, grad_rows_b)
        grad_act = inner_cols(grad_rows_b, full_down)
        gate_part = gate_up[:, 0]
        up_part = gate_up[:, 1]
        sigmoid_gate = jax.nn.sigmoid(gate_part)
        grad_gate = grad_act * up_part * sigmoid_gate * (1.0 + gate_part * (1.0 - sigmoid_gate))
        grad_up = grad_act * jax.nn.silu(gate_part)
        grad_gate_up = (
            jnp.stack([grad_gate, grad_up], axis=1)
            .astype(jnp.bfloat16)
            .reshape(seq_len, 2 * ff_local)
        )
        grad_gu_weight = inner_rows(rows_b, grad_gate_up).reshape(full_gu.shape)
        flat_gu = full_gu.reshape(full_gu.shape[0], 2 * ff_local)

        def back_mlp(row_start, row_count, source=grad_gate_up, weight=flat_gu):
            return inner_cols(source, weight)

        grad_normed_b = lax.psum_scatter(
            back_mlp(jnp.int32(0), local_rows * lax.axis_size("tensor")).astype(jnp.bfloat16),
            "tensor",
            scatter_dimension=0,
            tiled=True,
        ).astype(jnp.float32)
        grad_in_b, gain_b, shift_b = norm_back(
            grad_normed_b, scaled_b, inverse_b, norm_gain[layer_index, 1]
        )
        grad = grad + grad_in_b
        grad_rows_a = lax.all_gather(grad.astype(jnp.bfloat16), "tensor", axis=0, tiled=True)
        grad_out_weight = inner_rows(attended, grad_rows_a)
        grad_attended = inner_cols(grad_rows_a, full_out).astype(jnp.bfloat16)
        grad_attended = grad_attended.reshape(seq_len, heads_local, HD)
        grad_queries, grad_keys, grad_values = attend_back(
            queries, key_rows, values, positions, logsums, grad_attended, score_scale
        )
        grad_queries = rotate(grad_queries, cos_table, -sin_table)
        grad_keys = rotate(grad_keys, cos_table, -sin_table)
        grad_mixed = jnp.stack([grad_queries, grad_keys, grad_values], axis=1)
        grad_mixed = grad_mixed.reshape(seq_len, 3 * width_local).astype(jnp.bfloat16)
        qkv_shift_local = jnp.sum(grad_mixed, axis=0, dtype=jnp.float32).reshape(3, width_local)
        qkv_shift_rows[layer_index] = lax.dynamic_update_slice(
            jnp.zeros((3, b_qkv.shape[2]), jnp.float32),
            qkv_shift_local,
            (jnp.int32(0), tensor_rank * width_local),
        )
        grad_qkv_weight = inner_rows(rows_a, grad_mixed).reshape(full_qkv.shape)
        flat_qkv = full_qkv.reshape(full_qkv.shape[0], 3 * width_local)

        def back_attn(row_start, row_count, source=grad_mixed, weight=flat_qkv):
            return inner_cols(source, weight)

        grad_normed_a = lax.psum_scatter(
            back_attn(jnp.int32(0), local_rows * lax.axis_size("tensor")).astype(jnp.bfloat16),
            "tensor",
            scatter_dimension=0,
            tiled=True,
        ).astype(jnp.float32)
        grad_in_a, gain_a, shift_a = norm_back(
            grad_normed_a, scaled_a, inverse_a, norm_gain[layer_index, 0]
        )
        grad = grad + grad_in_a
        gain_rows[layer_index] = jnp.stack([gain_a, gain_b])
        shift_rows[layer_index] = jnp.stack([shift_a, shift_b])
        weight_parts[layer_index] = (
            lax.psum_scatter(
                grad_qkv_weight.astype(jnp.bfloat16), "dp", scatter_dimension=0, tiled=True
            ).astype(jnp.float32),
            lax.psum_scatter(
                grad_out_weight.astype(jnp.bfloat16), "dp", scatter_dimension=1, tiled=True
            ).astype(jnp.float32),
            lax.psum_scatter(
                grad_gu_weight.astype(jnp.bfloat16), "dp", scatter_dimension=0, tiled=True
            ).astype(jnp.float32),
            lax.psum_scatter(
                grad_down_weight.astype(jnp.bfloat16), "dp", scatter_dimension=1, tiled=True
            ).astype(jnp.float32),
        )
    stack_qkv = jnp.stack([weight_parts[number][0] for number in range(LAYERS)])
    stack_out = jnp.stack([weight_parts[number][1] for number in range(LAYERS)])
    stack_gu = jnp.stack([weight_parts[number][2] for number in range(LAYERS)])
    stack_down = jnp.stack([weight_parts[number][3] for number in range(LAYERS)])
    gain_grad, norm_bias_grad, qkv_bias_grad = lax.psum(
        (jnp.stack(gain_rows), jnp.stack(shift_rows), jnp.stack(qkv_shift_rows)), ("dp", "tensor")
    )
    return (
        activations,
        grad,
        gain_grad,
        norm_bias_grad,
        stack_qkv,
        qkv_bias_grad,
        stack_out,
        stack_gu,
        stack_down,
    )


def solution(mesh):
    in_specs = (
        P(("dp", "tensor"), None),
        P("dp"),
        P(),
        P(),
        P(None, "dp", None, "tensor"),
        P(),
        P(None, "tensor", "dp"),
        P(None, "dp", None, "tensor"),
        P(None, "tensor", "dp"),
        P(("dp", "tensor"), None),
    )
    out_specs = (
        P(("dp", "tensor"), None),
        P(("dp", "tensor"), None),
        P(),
        P(),
        P(None, "dp", None, "tensor"),
        P(),
        P(None, "tensor", "dp"),
        P(None, "dp", None, "tensor"),
        P(None, "tensor", "dp"),
    )
    def run(*operands):
        fits = operands[7].shape[3] % 128 == 0 and operands[4].shape[3] % PAIR == 0
        return (per_device if fits else per_device_plain)(*operands)

    return jax.shard_map(
        run, mesh=mesh, in_specs=in_specs, out_specs=out_specs, check_vma=False
    )
```

```python
import functools
import math

import jax
import jax.numpy as jnp
from jax import lax
from jax.experimental import pallas as pl
from jax.experimental.pallas import tpu as pltpu
from jax.sharding import PartitionSpec as P

HD = 64
ROT = 16
LAYERS = 2
PAIR = 2 * HD
MESH = pl.DeviceIdType.MESH
F32 = jnp.float32
BF16 = jnp.bfloat16
VMEM_LIMIT = 62 * 2**20
LAG = 6

norm_eps = 1e-05
theta_log = math.log(10000.0)
masked_score = -1e30
rows_rows = (((0,), (0,)), ((), ()))
cols_cols = (((1,), (1,)), ((), ()))
rows_cols = (((1,), (0,)), ((), ()))


def matmul(left, right, dims=rows_cols):
    return lax.dot_general(left, right, dims, preferred_element_type=F32)


def member_at(member, step):
    bit = 1
    while bit <= step:
        if step & bit:
            member = member + bit * (1 - 2 * ((member // bit) % 2))
        bit *= 2
    return member


class Whole:
    def __init__(self, held, size, send_sem, recv_sem):
        self.held, self.size, self.send_sem, self.recv_sem = held, size, send_sem, recv_sem
        self.member = lax.axis_index("dp")
        self.share = held.shape[0] // size
        self.evens = range(0, size, 2)

    def peers(self):
        return tuple(member_at(self.member, step) for step in self.evens if step) + (
            member_at(self.member, 1),
        )

    def rows(self, step):
        start = member_at(self.member, step) * self.share
        return pl.ds(pl.multiple_of(start, self.share), self.share)

    def hop(self, source_step, target_step, number):
        return pltpu.make_async_remote_copy(
            src_ref=self.held.at[self.rows(source_step)],
            dst_ref=self.held.at[self.rows(source_step)],
            send_sem=self.send_sem.at[number],
            recv_sem=self.recv_sem.at[number],
            device_id={"dp": member_at(self.member, target_step)},
            device_id_type=MESH,
        )

    def to_chips(self, step):
        return self.hop(0, step, step)

    def to_core(self, step):
        return self.hop(step, 1, step + 1)

    def start(self):
        for step in self.evens:
            if step:
                self.to_chips(step).start()
        self.to_core(0).start()

    def pass_on(self):
        for step in self.evens:
            if step:
                self.to_chips(step).wait_recv()
                self.to_core(step).start()

    def wait(self):
        for step in self.evens:
            self.to_core(step).wait_recv()

    def drain(self):
        for step in self.evens:
            if step:
                self.to_chips(step).wait_send()
            self.to_core(step).wait_send()


class Owned:
    def __init__(self, part, size, mine, swapped, landed, load_sem, sems):
        self.part, self.mine, self.swapped, self.landed = part, mine, swapped, landed
        self.load_sem, (self.swap_send, self.swap_recv, self.send_sem, self.recv_sem) = load_sem, sems
        self.member = lax.axis_index("dp")
        self.share = part.shape[0] // size
        self.chips = range(size // 2)

    def peers(self):
        return tuple(member_at(self.member, 2 * chip) for chip in self.chips if chip) + (
            member_at(self.member, 1),
        )

    def rows(self, step):
        return pl.ds(pl.multiple_of(member_at(self.member, step) * self.share, self.share), self.share)

    def load(self, chip):
        return pltpu.make_async_copy(
            self.part.at[self.rows(2 * chip)], self.mine.at[chip], self.load_sem.at[chip]
        )

    def swap(self, chip):
        return pltpu.make_async_remote_copy(
            src_ref=self.part.at[self.rows(2 * chip + 1)],
            dst_ref=self.swapped.at[chip],
            send_sem=self.swap_send.at[chip],
            recv_sem=self.swap_recv.at[chip],
            device_id={"dp": member_at(self.member, 1)},
            device_id_type=MESH,
        )

    def hop(self, chip):
        return pltpu.make_async_remote_copy(
            src_ref=self.mine.at[chip],
            dst_ref=self.landed.at[chip - 1],
            send_sem=self.send_sem.at[chip],
            recv_sem=self.recv_sem.at[chip],
            device_id={"dp": member_at(self.member, 2 * chip)},
            device_id_type=MESH,
        )

    def each_rows(self, run):
        def one(number, carry):
            run(pl.ds(pl.multiple_of(number * 16, 16), 16))
            return carry

        lax.fori_loop(0, self.share // 16, one, 0)

    def start(self):
        for chip in self.chips:
            self.swap(chip).start()
            self.load(chip).start()

    def across_chips(self, total):
        for chip in (*self.chips[1:], 0):
            self.load(chip).wait()
            self.swap(chip).wait_recv()

            def rows(at):
                both = self.mine[chip, at, :].astype(F32) + self.swapped[chip, at, :].astype(F32)
                if chip:
                    self.mine[chip, at, :] = both.astype(BF16)
                else:
                    total[at, :] = both

            self.each_rows(rows)
            if chip:
                self.hop(chip).start()

    def finish(self, total):
        for chip in self.chips[1:]:
            self.hop(chip).wait_recv()

        def rows(at):
            values = total[at, :]
            for chip in self.chips[1:]:
                values = values + self.landed[chip - 1, at, :].astype(F32)
            total[at, :] = values

        self.each_rows(rows)

    def drain(self):
        for chip in self.chips:
            self.swap(chip).wait_send()
            if chip:
                self.hop(chip).wait_send()


def line_barrier(place, count, others=()):
    barrier = pltpu.get_barrier_semaphore()
    for other in others:
        pl.semaphore_signal(barrier, inc=1, device_id={"dp": other}, device_id_type=MESH)

    @pl.when(place > 0)
    def _():
        pl.semaphore_signal(barrier, inc=1, device_id={"tensor": place - 1}, device_id_type=MESH)

    @pl.when(place < count - 1)
    def _():
        pl.semaphore_signal(barrier, inc=1, device_id={"tensor": place + 1}, device_id_type=MESH)

    middle = (place > 0) & (place < count - 1)

    @pl.when(middle)
    def _():
        pl.semaphore_wait(barrier, 2 + len(others))

    @pl.when(jnp.logical_not(middle))
    def _():
        pl.semaphore_wait(barrier, 1 + len(others))


def each_tile(width, tile, run):
    def one(number, carry):
        run(pl.multiple_of(number * tile, tile), tile)
        return carry

    lax.fori_loop(0, width // tile, one, 0)
    if width % tile:
        run(width // tile * tile, width % tile)


class Line:
    def __init__(self, count, pieces, shares, sending, arrived, sum_send, sum_recv, held, send_sem, recv_sem):
        self.count, self.pieces = count, pieces
        self.shares, self.sending, self.arrived = shares, sending, arrived
        self.sum_send, self.sum_recv = sum_send, sum_recv
        self.held, self.send_sem, self.recv_sem = held, send_sem, recv_sem
        self.place = lax.axis_index("tensor")
        self.rows = (held if held is not None else sending).shape[1] // pieces

    def at(self, piece):
        return pl.ds(pl.multiple_of(piece * self.rows, self.rows), self.rows)

    def sum_hop(self, piece, owner):
        right = owner > self.place
        target = jnp.where(right, self.place + 1, self.place - 1)
        slot = jnp.where(right | (owner != target), owner, self.count)
        return pltpu.make_async_remote_copy(
            src_ref=self.sending.at[owner, self.at(piece)],
            dst_ref=self.arrived.at[slot, self.at(piece)],
            send_sem=self.sum_send.at[owner, piece],
            recv_sem=self.sum_recv.at[slot, piece],
            device_id={"tensor": target},
            device_id_type=MESH,
        )

    def sum_landed(self, piece, slot):
        return pltpu.make_async_remote_copy(
            src_ref=self.sending.at[0, self.at(piece)],
            dst_ref=self.arrived.at[slot, self.at(piece)],
            send_sem=self.sum_send.at[0, piece],
            recv_sem=self.sum_recv.at[slot, piece],
            device_id={"tensor": self.place},
            device_id_type=MESH,
        )

    def row_hop(self, piece, block, right):
        return pltpu.make_async_remote_copy(
            src_ref=self.held.at[block, self.at(piece)],
            dst_ref=self.held.at[block, self.at(piece)],
            send_sem=self.send_sem.at[jnp.where(right, 0, 1), block, piece],
            recv_sem=self.recv_sem.at[block, piece],
            device_id={"tensor": jnp.where(right, self.place + 1, self.place - 1)},
            device_id_type=MESH,
        )

    def sides(self, away, run):
        def one(side, carry):
            block = jnp.where(side == 0, self.place + away, self.place - away)

            @pl.when((block >= 0) & (block < self.count))
            def _():
                run(block, side == 0)

            return carry

        lax.fori_loop(0, 2, one, 0)

    def chunks(self, run):
        chunk = min(16, self.rows)

        def one(number, carry):
            run(pl.multiple_of(number * chunk, chunk), chunk)
            return carry

        lax.fori_loop(0, self.rows // chunk, one, 0)

    def pass_on(self, piece, owner, right):
        first = pl.multiple_of(piece * self.rows, self.rows)
        onward = jnp.where(right, self.place > 0, self.place < self.count - 1)

        @pl.when(onward)
        def _():
            self.sum_landed(piece, owner).wait_recv()

            def rows(start, size):
                at = pl.ds(pl.multiple_of(first + start, size), size)
                self.sending[owner, at, :] = (
                    self.shares[owner, at, :]
                    + self.arrived[owner, at, :].astype(F32)
                ).astype(BF16)

            self.chunks(rows)

        @pl.when(jnp.logical_not(onward))
        def _():
            def rows(start, size):
                at = pl.ds(pl.multiple_of(first + start, size), size)
                self.sending[owner, at, :] = self.shares[owner, at, :].astype(BF16)

            self.chunks(rows)

        self.sum_hop(piece, owner).start()

    def collect(self, piece):
        first = pl.multiple_of(piece * self.rows, self.rows)

        def add(slot):
            self.sum_landed(piece, slot).wait_recv()

            def rows(start, size):
                at = pl.ds(pl.multiple_of(first + start, size), size)
                self.shares[self.place, at, :] = self.shares[self.place, at, :] + self.arrived[
                    slot, at, :
                ].astype(F32)

            self.chunks(rows)

        @pl.when(self.place > 0)
        def _():
            add(self.place)

        @pl.when(self.place < self.count - 1)
        def _():
            add(self.count)

    def own_rows(self, piece, run):
        first = pl.multiple_of(piece * self.rows, self.rows)

        def rows(start, size):
            at = pl.ds(pl.multiple_of(first + start, size), size)
            run(at, self.shares[self.place, at, :])

        self.chunks(rows)

    def run(self, term, finish, process, each_tick=None, delay=0):
        count, pieces, place = self.count, self.pieces, self.place
        scatter, gather = term is not None, process is not None
        lead = count - 1 if scatter else 0
        if scatter:
            term(0)

        def tick(number, carry):
            if each_tick is not None:
                each_tick(number)

            def valid(piece):
                return (piece >= 0) & (piece < pieces)

            if scatter:

                def sum_step(step, inner):
                    piece = number - step

                    @pl.when(valid(piece))
                    def _():
                        self.sides(
                            count - 1 - step,
                            lambda owner, right: self.pass_on(piece, owner, right),
                        )

                    return inner

                lax.fori_loop(0, count - 1, sum_step, 0)
            mine = number - lead

            @pl.when(valid(mine))
            def _():
                if scatter:
                    self.collect(mine)
                finish(mine)
                if gather:

                    @pl.when(place < count - 1)
                    def _():
                        self.row_hop(mine, place, True).start()

                    @pl.when(place > 0)
                    def _():
                        self.row_hop(mine, place, False).start()

            if gather:

                def row_step(step, inner):
                    piece = mine - step

                    def forward(block, right):
                        self.row_hop(piece, block, True).wait_recv()
                        onward = jnp.where(right, place > 0, place < count - 1)

                        @pl.when(onward)
                        def _():
                            self.row_hop(piece, block, jnp.logical_not(right)).start()

                    @pl.when(valid(piece))
                    def _():
                        self.sides(step, forward)

                    return inner

                lax.fori_loop(1, count, row_step, 0)
            if scatter:

                @pl.when(number + 1 < pieces)
                def _():
                    term(number + 1)

            if gather:

                @pl.when(valid(mine - (count - 1) - delay))
                def _():
                    process(mine - (count - 1) - delay)

            return carry

        lax.fori_loop(0, pieces + lead + (count - 1 + delay if gather else 0), tick, 0)

    def drain(self):
        def piece_sends(piece, carry):
            def owner_sends(owner, inner):
                if self.sending is not None:

                    @pl.when(owner != self.place)
                    def _():
                        self.sum_hop(piece, owner).wait_send()

                if self.held is not None:

                    @pl.when((owner <= self.place) & (self.place < self.count - 1))
                    def _():
                        self.row_hop(piece, owner, True).wait_send()

                    @pl.when((owner >= self.place) & (self.place > 0))
                    def _():
                        self.row_hop(piece, owner, False).wait_send()

                return inner

            lax.fori_loop(0, self.count, owner_sends, 0)
            return carry

        lax.fori_loop(0, self.pieces, piece_sends, 0)


def norm_rows(values):
    average = jnp.mean(values, axis=-1, keepdims=True)
    centred = values - average
    variance = jnp.mean(centred * centred, axis=-1, keepdims=True)
    inverse = lax.rsqrt(variance + norm_eps)
    return centred * inverse, inverse


def scatter_scratch(count, pieces, rows, width):
    return [
        pltpu.VMEM((count, rows, width), F32),
        pltpu.VMEM((count, rows, width), BF16),
        pltpu.VMEM((count + 1, rows, width), BF16),
        pltpu.SemaphoreType.DMA((count, pieces)),
        pltpu.SemaphoreType.DMA((count + 1, pieces)),
    ]


def gather_scratch(count, pieces, rows, width):
    return [
        pltpu.VMEM((count, rows, width), BF16),
        pltpu.SemaphoreType.DMA((2, count, pieces)),
        pltpu.SemaphoreType.DMA((count, pieces)),
    ]


vmem = pl.BlockSpec(memory_space=pltpu.VMEM)
hbm = pl.BlockSpec(memory_space=pl.ANY)


class Loads:
    def __init__(self, pairs, sems):
        self.copies = [
            pltpu.make_async_copy(source, target, sems.at[number])
            for number, (source, target) in enumerate(pairs)
        ]
        for copy in self.copies:
            copy.start()

    def wait(self, *numbers):
        for number in numbers:
            self.copies[number].wait()


class Saves:
    def __init__(self, pairs, sems, line):
        self.pairs, self.sems, self.line = pairs, sems, line

    def copy(self, number, piece):
        source, target = self.pairs[number]
        rows = self.line.at(piece)
        where = (slice(None),) * (len(source.shape) - 2) + (rows,)
        return pltpu.make_async_copy(
            source.at[where], target.at[where], self.sems.at[number, piece]
        )

    def start(self, piece):
        for number in range(len(self.pairs)):
            self.copy(number, piece).start()

    def wait(self):
        for number in range(len(self.pairs)):
            for piece in range(self.line.pieces):
                self.copy(number, piece).wait()


def flat_rows(ref, rows, columns=slice(None)):
    values = ref[:, rows, columns]
    return values.reshape(values.shape[0] * values.shape[1], values.shape[2])


def put_rows(ref, rows, columns, values):
    count = ref.shape[0]
    ref[:, rows, columns] = values.reshape(count, values.shape[0] // count, values.shape[1])


def line_call(body, out_shape, out_specs, in_specs, scratch, number, flops, moved):
    return pl.pallas_call(
        body,
        out_shape=out_shape,
        in_specs=in_specs,
        out_specs=out_specs,
        scratch_shapes=scratch,
        compiler_params=pltpu.CompilerParams(
            collective_id=number, has_side_effects=True, vmem_limit_bytes=VMEM_LIMIT
        ),
        cost_estimate=pl.CostEstimate(flops=flops, bytes_accessed=moved, transcendentals=0),
    )


def pieces_of(rows):
    return 4 if rows % 64 == 0 else 1


def query_key_value(line, weight, bias, tables, mixed):
    cos, sin_up, sin_down = tables
    width = mixed.shape[3]

    def factor(table, rows, size):
        return jnp.concatenate([flat_rows(table, rows)] * (size // PAIR), axis=1)

    def process(piece):
        rows = line.at(piece)

        def columns(kind):
            def run(start, size):
                source = pl.ds(pl.multiple_of(kind * width + start, 128), size)
                result = matmul(flat_rows(line.held, rows), weight[:, source]) + bias[:, source]
                if kind < 2:
                    result = (
                        result * factor(cos, rows, size)
                        + pltpu.roll(result, size - ROT // 2, 1) * factor(sin_up, rows, size)
                        + pltpu.roll(result, ROT // 2, 1) * factor(sin_down, rows, size)
                    )
                if kind == 0:
                    result = result * (1.0 / math.sqrt(HD))
                put_rows(mixed.at[kind], rows, pl.ds(start, size), result.astype(BF16))

            return run

        for kind in range(3):
            each_tile(width, min(256, width), columns(kind))

    return process


def gate_and_up(line, weight, act, slope, silu):
    width = act.shape[2]

    def process(piece):
        rows = line.at(piece)

        def run(start, size):
            at = pl.ds(start, size)
            own = flat_rows(line.held, rows)
            gate = matmul(own, weight[:, at])
            up = matmul(own, weight[:, pl.ds(pl.multiple_of(width + start, 128), size)])
            sigmoid = jax.nn.sigmoid(gate)
            soft = gate * sigmoid
            put_rows(act, rows, at, (soft * up).astype(BF16))
            put_rows(silu, rows, at, soft.astype(BF16))
            put_rows(slope, rows, at, (up * sigmoid * (1.0 + gate * (1.0 - sigmoid))).astype(BF16))

        each_tile(width, 256, run)

    return process


def grad_gate_and_up(line, weight, slope, silu, wide):
    width = slope.shape[2]

    def process(piece):
        rows = line.at(piece)

        def run(start, size):
            at = pl.ds(start, size)
            grad_act = matmul(flat_rows(line.held, rows), weight[at, :], cols_cols)
            put_rows(wide, rows, at, (grad_act * flat_rows(slope, rows, at).astype(F32)).astype(BF16))
            put_rows(
                wide,
                rows,
                pl.ds(pl.multiple_of(width + start, 128), size),
                (grad_act * flat_rows(silu, rows, at).astype(F32)).astype(BF16),
            )

        each_tile(width, 256, run)

    return process


def through_transposed(line, weight, result):
    def process(piece):
        rows = line.at(piece)

        def run(start, size):
            at = pl.ds(start, size)
            put_rows(
                result, rows, at, matmul(flat_rows(line.held, rows), weight[at, :], cols_cols).astype(BF16)
            )

        each_tile(result.shape[2], 256, run)

    return process


def share_of(line, source, weight):
    def term(piece):
        rows = line.at(piece)

        def run(start, size):
            at = pl.ds(start, size)
            put_rows(line.shares, rows, at, matmul(flat_rows(source, rows), weight[:, at]))

        each_tile(line.shares.shape[2], 256, run)

    return term


def share_transposed(line, sources, weight):
    width = sources[0].shape[2]

    def term(piece):
        rows = line.at(piece)

        def run(start, size):
            at = pl.ds(start, size)
            result = matmul(flat_rows(sources[0], rows), weight[at, :width], cols_cols)
            for number in range(1, len(sources)):
                result = result + matmul(
                    flat_rows(sources[number], rows),
                    weight[at, number * width : (number + 1) * width],
                    cols_cols,
                )
            put_rows(line.shares, rows, at, result)

        each_tile(line.shares.shape[2], 256, run)

    return term


def add_and_norm(line, before, gain, shift, after):
    def finish(piece):
        def rows(at, total):
            hidden = before[at, :].astype(F32) + total
            after[at, :] = hidden
            scaled, _ = norm_rows(hidden)
            line.held[line.place, at, :] = (scaled * gain[...] + shift[...]).astype(BF16)

        line.own_rows(piece, rows)

    return finish


def norm_backward(line, grad, hidden, gain, out, gain_sum, shift_sum):
    gain_sum[...] = jnp.zeros_like(gain_sum)
    shift_sum[...] = jnp.zeros_like(shift_sum)

    def finish(piece):
        def rows(at, grad_normed):
            scaled, inverse = norm_rows(hidden[at, :].astype(F32))
            weighted = grad_normed * gain[...]
            first = jnp.mean(weighted, axis=-1, keepdims=True)
            second = jnp.mean(weighted * scaled, axis=-1, keepdims=True)
            result = grad[at, :].astype(F32) + inverse * (weighted - first - scaled * second)
            out[at, :] = result
            if line.held is not None:
                line.held[line.place, at, :] = result.astype(BF16)
            gain_sum[...] += jnp.sum(grad_normed * scaled, axis=0, keepdims=True)
            shift_sum[...] += jnp.sum(grad_normed, axis=0, keepdims=True)

        line.own_rows(piece, rows)

    return finish


def split(refs, *sizes):
    parts, start = [], 0
    for size in sizes:
        parts.append(refs[start : start + size])
        start += size
    return parts


def first_kernel(count, pieces, size, *refs):
    (own, gain, shift, share, bias, *tables), outs, gather, rest = split(refs, 8, 3, 3, 6)
    rows_out, mixed_out, weight_out = outs
    weight_held, mixed, load_sem, save_sem, weight_send, weight_recv = rest
    line = Line(count, pieces, None, None, None, None, None, *gather)
    weight = Whole(weight_held, size, weight_send, weight_recv)
    load = pltpu.make_async_copy(share, weight_held.at[weight.rows(0)], load_sem.at[0])
    keep = pltpu.make_async_copy(weight_held, weight_out, load_sem.at[1])
    load.start()
    line_barrier(line.place, count, weight.peers())
    saves = Saves([(line.held, rows_out), (mixed, mixed_out)], save_sem, line)
    compute = query_key_value(line, weight_held, bias, tables, mixed)
    load.wait()
    weight.start()

    def finish(piece):
        first_row = pl.multiple_of(piece * line.rows, line.rows)

        def rows(start, size):
            at = pl.ds(pl.multiple_of(first_row + start, size), size)
            scaled, _ = norm_rows(own[at, :].astype(F32))
            line.held[line.place, at, :] = (scaled * gain[...] + shift[...]).astype(BF16)

        line.chunks(rows)

    def each_tick(number):
        @pl.when(number == count - 1)
        def _():
            weight.pass_on()

    def process(piece):
        @pl.when(piece == 0)
        def _():
            weight.wait()
            keep.start()

        compute(piece)
        saves.start(piece)

    line.run(None, finish, process, each_tick, 2)
    line.drain()
    weight.drain()
    keep.wait()
    saves.wait()


def first(count, own, gain, shift, share, bias, tables, width):
    rows, depth = own.shape
    pieces = pieces_of(rows)
    size = lax.axis_size("dp")
    return line_call(
        functools.partial(first_kernel, count, pieces, size),
        (
            jax.ShapeDtypeStruct((count, rows, depth), BF16),
            jax.ShapeDtypeStruct((3, count, rows, width), BF16),
            jax.ShapeDtypeStruct((depth, 3 * width), BF16),
        ),
        (hbm, hbm, hbm),
        [vmem, vmem, vmem, hbm, vmem, vmem, vmem, vmem],
        gather_scratch(count, pieces, rows, depth)
        + [
            pltpu.VMEM((depth, 3 * width), BF16),
            pltpu.VMEM((3, count, rows, width), BF16),
            pltpu.SemaphoreType.DMA((2,)),
            pltpu.SemaphoreType.DMA((2, pieces)),
            pltpu.SemaphoreType.DMA((size,)),
            pltpu.SemaphoreType.DMA((size,)),
        ],
        0,
        6 * count * rows * depth * width,
        depth * width * 6 + own.size * 2 * count * 4,
    )(own, gain, shift, share, bias, *tables)


def middle_kernel(count, pieces, lag, *refs):
    ins, outs, scatter, gather, rest = split(refs, 6, 5, 5, 3, 9)
    source, w_out, before, gain, shift, w_up = ins
    after, rows_out, act_out, slope_out, silu_out = outs
    source_held, out_held, up_held, act, slope, silu, load_sem, save_sem, turn = rest
    line = Line(count, pieces, *scatter, *gather)
    loads = Loads([(source, source_held), (w_out, out_held), (w_up, up_held)], load_sem)
    member = lax.axis_index("dp")
    core = member % 2
    partner = member + 1 - 2 * core
    line_barrier(line.place, count, (partner,) if lag else ())
    saves = Saves(
        [(line.held, rows_out), (act, act_out), (slope, slope_out), (silu, silu_out)], save_sem, line
    )
    compute = gate_and_up(line, up_held, act, slope, silu)

    def process(piece):
        @pl.when(piece == 0)
        def _():
            loads.wait(2)

        compute(piece)
        saves.start(piece)

    def signal(number):
        @pl.when((core == 0) & (number == lag))
        def _():
            pl.semaphore_signal(turn, inc=1, device_id={"dp": partner}, device_id_type=MESH)

    loads.wait(0, 1)
    if lag:

        @pl.when(core == 1)
        def _():
            pl.semaphore_wait(turn, 1)

    line.run(
        share_of(line, source_held, out_held),
        add_and_norm(line, before, gain, shift, after),
        process,
        signal if lag else None,
    )
    line.drain()
    saves.wait()


def middle(count, source, w_out, before, gain, shift, w_up, lag=0):
    rows, depth = before.shape
    pieces = pieces_of(rows)
    width = w_up.shape[1] // 2
    wide = jax.ShapeDtypeStruct((count, rows, width), BF16)
    return line_call(
        functools.partial(middle_kernel, count, pieces, lag),
        (
            jax.ShapeDtypeStruct((rows, depth), F32),
            jax.ShapeDtypeStruct((count, rows, depth), BF16),
            wide,
            wide,
            wide,
        ),
        (vmem, hbm, hbm, hbm, hbm),
        [hbm, hbm, vmem, vmem, vmem, hbm],
        scatter_scratch(count, pieces, rows, depth)
        + gather_scratch(count, pieces, rows, depth)
        + [
            pltpu.VMEM(source.shape, BF16),
            pltpu.VMEM(w_out.shape, BF16),
            pltpu.VMEM(w_up.shape, BF16),
            pltpu.VMEM(wide.shape, BF16),
            pltpu.VMEM(wide.shape, BF16),
            pltpu.VMEM(wide.shape, BF16),
            pltpu.SemaphoreType.DMA((3,)),
            pltpu.SemaphoreType.DMA((4, pieces)),
            pltpu.SemaphoreType.REGULAR,
        ],
        7 if lag else 1,
        2 * count * rows * (w_out.size + w_up.size),
        (w_out.size + w_up.size) * 2 + before.size * 60,
    )(source, w_out, before, gain, shift, w_up)


def between_kernel(count, pieces, *refs):
    ins, outs, scatter, gather, rest = split(refs, 10, 3, 5, 3, 6)
    source, w_down, before, gain, shift, weight, bias, *tables = ins
    after, rows_out, mixed_out = outs
    source_held, down_held, weight_held, mixed, load_sem, save_sem = rest
    line = Line(count, pieces, *scatter, *gather)
    loads = Loads([(source, source_held), (w_down, down_held), (weight, weight_held)], load_sem)
    line_barrier(line.place, count)
    saves = Saves([(line.held, rows_out), (mixed, mixed_out)], save_sem, line)
    compute = query_key_value(line, weight_held, bias, tables, mixed)

    def process(piece):
        @pl.when(piece == 0)
        def _():
            loads.wait(2)

        compute(piece)
        saves.start(piece)

    loads.wait(0, 1)
    line.run(
        share_of(line, source_held, down_held), add_and_norm(line, before, gain, shift, after), process
    )
    line.drain()
    saves.wait()


def between(count, source, w_down, before, gain, shift, weight, bias, tables):
    rows, depth = before.shape
    pieces = pieces_of(rows)
    mixed = (3, count, rows, weight.shape[1] // 3)
    return line_call(
        functools.partial(between_kernel, count, pieces),
        (
            jax.ShapeDtypeStruct((rows, depth), F32),
            jax.ShapeDtypeStruct((count, rows, depth), BF16),
            jax.ShapeDtypeStruct(mixed, BF16),
        ),
        (vmem, hbm, hbm),
        [hbm, hbm, vmem, vmem, vmem, hbm, vmem, vmem, vmem, vmem],
        scatter_scratch(count, pieces, rows, depth)
        + gather_scratch(count, pieces, rows, depth)
        + [
            pltpu.VMEM(source.shape, BF16),
            pltpu.VMEM(w_down.shape, BF16),
            pltpu.VMEM(weight.shape, BF16),
            pltpu.VMEM(mixed, BF16),
            pltpu.SemaphoreType.DMA((3,)),
            pltpu.SemaphoreType.DMA((2, pieces)),
        ],
        2,
        2 * count * rows * (w_down.size + weight.size),
        (w_down.size + weight.size) * 2 + before.size * 60,
    )(source, w_down, before, gain, shift, weight, bias, *tables)


def turn_kernel(count, pieces, *refs):
    ins, outs, scatter, gather, rest = split(refs, 6, 3, 5, 3, 7)
    source, w_down, before, own, slope_in, silu_in = ins
    after, rows_out, wide_out = outs
    source_held, down_held, slope, silu, wide, load_sem, save_sem = rest
    line = Line(count, pieces, *scatter, *gather)
    loads = Loads(
        [(source, source_held), (w_down, down_held), (slope_in, slope), (silu_in, silu)], load_sem
    )
    line_barrier(line.place, count)
    saves = Saves([(line.held, rows_out), (wide, wide_out)], save_sem, line)
    compute = grad_gate_and_up(line, down_held, slope, silu, wide)

    def finish(piece):
        def rows(at, total):
            after[at, :] = (before[at, :] + total).astype(BF16)
            line.held[line.place, at, :] = own[at, :]

        line.own_rows(piece, rows)

    def process(piece):
        @pl.when(piece == 0)
        def _():
            loads.wait(2, 3)

        compute(piece)
        saves.start(piece)

    loads.wait(0, 1)
    line.run(share_of(line, source_held, down_held), finish, process)
    line.drain()
    saves.wait()


def turn(count, source, w_down, before, own, slope, silu):
    rows, depth = before.shape
    pieces = pieces_of(rows)
    width = w_down.shape[0]
    return line_call(
        functools.partial(turn_kernel, count, pieces),
        (
            jax.ShapeDtypeStruct((rows, depth), BF16),
            jax.ShapeDtypeStruct((count, rows, depth), BF16),
            jax.ShapeDtypeStruct((count, rows, 2 * width), BF16),
        ),
        (vmem, hbm, hbm),
        [hbm, hbm, vmem, vmem, hbm, hbm],
        scatter_scratch(count, pieces, rows, depth)
        + gather_scratch(count, pieces, rows, depth)
        + [
            pltpu.VMEM(source.shape, BF16),
            pltpu.VMEM(w_down.shape, BF16),
            pltpu.VMEM(slope.shape, BF16),
            pltpu.VMEM(silu.shape, BF16),
            pltpu.VMEM((count, rows, 2 * width), BF16),
            pltpu.SemaphoreType.DMA((4,)),
            pltpu.SemaphoreType.DMA((2, pieces)),
        ],
        3,
        4 * count * rows * w_down.size,
        w_down.size * 2 + before.size * 60,
    )(source, w_down, before, own, slope, silu)


def middle_back_kernel(count, pieces, *refs):
    ins, outs, scatter, gather, rest = split(refs, 6, 5, 5, 3, 6)
    source, w_up, grad, hidden, gain, w_out = ins
    out, gain_sum, shift_sum, rows_out, result_out = outs
    source_held, up_held, out_held, result, load_sem, save_sem = rest
    line = Line(count, pieces, *scatter, *gather)
    loads = Loads([(source, source_held), (w_up, up_held), (w_out, out_held)], load_sem)
    line_barrier(line.place, count)
    saves = Saves([(line.held, rows_out), (result, result_out)], save_sem, line)
    compute = through_transposed(line, out_held, result)

    def process(piece):
        @pl.when(piece == 0)
        def _():
            loads.wait(2)

        compute(piece)
        saves.start(piece)

    loads.wait(0, 1)
    line.run(
        share_transposed(line, [source_held], up_held),
        norm_backward(line, grad, hidden, gain, out, gain_sum, shift_sum),
        process,
    )
    line.drain()
    saves.wait()


def middle_back(count, source, w_up, grad, hidden, gain, w_out):
    rows, depth = grad.shape
    pieces = pieces_of(rows)
    width = w_out.shape[0]
    return line_call(
        functools.partial(middle_back_kernel, count, pieces),
        (
            jax.ShapeDtypeStruct((rows, depth), F32),
            jax.ShapeDtypeStruct((1, depth), F32),
            jax.ShapeDtypeStruct((1, depth), F32),
            jax.ShapeDtypeStruct((count, rows, depth), BF16),
            jax.ShapeDtypeStruct((count, rows, width), BF16),
        ),
        (vmem, vmem, vmem, hbm, hbm),
        [hbm, hbm, vmem, vmem, vmem, hbm],
        scatter_scratch(count, pieces, rows, depth)
        + gather_scratch(count, pieces, rows, depth)
        + [
            pltpu.VMEM(source.shape, BF16),
            pltpu.VMEM(w_up.shape, BF16),
            pltpu.VMEM(w_out.shape, BF16),
            pltpu.VMEM((count, rows, width), BF16),
            pltpu.SemaphoreType.DMA((3,)),
            pltpu.SemaphoreType.DMA((2, pieces)),
        ],
        4 if grad.dtype == F32 else 8,
        2 * count * rows * (w_up.size + w_out.size),
        (w_up.size + w_out.size) * 2 + grad.size * 60,
    )(source, w_up, grad, hidden, gain, w_out)


def between_back_kernel(count, pieces, *refs):
    ins, outs, scatter, gather, rest = split(refs, 8, 5, 5, 3, 8)
    source, weight, grad, hidden, gain, w_down, slope_in, silu_in = ins
    out, gain_sum, shift_sum, rows_out, wide_out = outs
    source_held, weight_held, down_held, slope, silu, wide, load_sem, save_sem = rest
    line = Line(count, pieces, *scatter, *gather)
    loads = Loads(
        [
            (source, source_held),
            (weight, weight_held),
            (w_down, down_held),
            (slope_in, slope),
            (silu_in, silu),
        ],
        load_sem,
    )
    line_barrier(line.place, count)
    saves = Saves([(line.held, rows_out), (wide, wide_out)], save_sem, line)
    compute = grad_gate_and_up(line, down_held, slope, silu, wide)

    def process(piece):
        @pl.when(piece == 0)
        def _():
            loads.wait(2, 3, 4)

        compute(piece)
        saves.start(piece)

    loads.wait(0, 1)
    line.run(
        share_transposed(line, [source_held.at[kind] for kind in range(3)], weight_held),
        norm_backward(line, grad, hidden, gain, out, gain_sum, shift_sum),
        process,
    )
    line.drain()
    saves.wait()


def between_back(count, source, weight, grad, hidden, gain, w_down, slope, silu):
    rows, depth = grad.shape
    pieces = pieces_of(rows)
    width = w_down.shape[0]
    return line_call(
        functools.partial(between_back_kernel, count, pieces),
        (
            jax.ShapeDtypeStruct((rows, depth), F32),
            jax.ShapeDtypeStruct((1, depth), F32),
            jax.ShapeDtypeStruct((1, depth), F32),
            jax.ShapeDtypeStruct((count, rows, depth), BF16),
            jax.ShapeDtypeStruct((count, rows, 2 * width), BF16),
        ),
        (vmem, vmem, vmem, hbm, hbm),
        [hbm, hbm, vmem, vmem, vmem, hbm, hbm, hbm],
        scatter_scratch(count, pieces, rows, depth)
        + gather_scratch(count, pieces, rows, depth)
        + [
            pltpu.VMEM(source.shape, BF16),
            pltpu.VMEM(weight.shape, BF16),
            pltpu.VMEM(w_down.shape, BF16),
            pltpu.VMEM(slope.shape, BF16),
            pltpu.VMEM(silu.shape, BF16),
            pltpu.VMEM((count, rows, 2 * width), BF16),
            pltpu.SemaphoreType.DMA((5,)),
            pltpu.SemaphoreType.DMA((2, pieces)),
        ],
        5,
        2 * count * rows * (w_down.size + weight.size),
        (w_down.size + weight.size) * 2 + grad.size * 60,
    )(source, weight, grad, hidden, gain, w_down, slope, silu)


def last_kernel(count, pieces, size, *refs):
    ins, outs, scatter, rest = split(refs, 6, 4, 5, 11)
    source, weight, grad, hidden, gain, part = ins
    *outs, owned_out = outs
    source_held, weight_held, load_sem, mine, swapped, landed, part_sem, *sems = rest
    line = Line(count, pieces, *scatter, None, None, None)
    owned = Owned(part, size, mine, swapped, landed, part_sem, sems)
    loads = Loads([(source, source_held), (weight, weight_held)], load_sem)
    line_barrier(line.place, count, owned.peers())
    owned.start()

    def each_tick(number):
        @pl.when(number == 1)
        def _():
            owned.across_chips(owned_out)

    loads.wait(0, 1)
    line.run(
        share_transposed(line, [source_held.at[kind] for kind in range(3)], weight_held),
        norm_backward(line, grad, hidden, gain, *outs),
        None,
        each_tick,
    )
    line.drain()
    owned.finish(owned_out)
    owned.drain()


def last(count, source, weight, grad, hidden, gain, part):
    rows, depth = grad.shape
    pieces = pieces_of(rows)
    size = lax.axis_size("dp")
    share, width = part.shape[0] // size, part.shape[1]
    return line_call(
        functools.partial(last_kernel, count, pieces, size),
        (
            jax.ShapeDtypeStruct((rows, depth), F32),
            jax.ShapeDtypeStruct((1, depth), F32),
            jax.ShapeDtypeStruct((1, depth), F32),
            jax.ShapeDtypeStruct((share, width), F32),
        ),
        (vmem, vmem, vmem, vmem),
        [hbm, hbm, vmem, vmem, vmem, hbm],
        scatter_scratch(count, pieces, rows, depth)
        + [
            pltpu.VMEM(source.shape, BF16),
            pltpu.VMEM(weight.shape, BF16),
            pltpu.SemaphoreType.DMA((2,)),
            pltpu.VMEM((size // 2, share, width), BF16),
            pltpu.VMEM((size // 2, share, width), BF16),
            pltpu.VMEM((size // 2 - 1, share, width), BF16),
            pltpu.SemaphoreType.DMA((size // 2,)),
        ]
        + [pltpu.SemaphoreType.DMA((size // 2,))] * 4,
        6,
        2 * count * rows * weight.size,
        weight.size * 2 + grad.size * 20,
    )(source, weight, grad, hidden, gain, part)


def usable(first, start, keys, queries):
    key_index = lax.broadcasted_iota(jnp.int32, (keys, queries), 0)
    query_index = start + lax.broadcasted_iota(jnp.int32, (keys, queries), 1)
    return (key_index >= first) & (key_index <= query_index)


def head_lanes(values, head):
    lane = lax.broadcasted_iota(jnp.int32, values.shape, 1)
    return jnp.where((lane // HD) == head, values, jnp.zeros_like(values))


def attend_kernel(block, positions, queries, keys, values, attended, logsums):
    length = keys.shape[0]
    values_across = jnp.transpose(values[...])
    for start in range(0, length, block):
        seen = start + block
        at = slice(start, seen)
        own = queries[at, :]
        index = start + lax.broadcasted_iota(jnp.int32, (1, block), 1)
        allowed = usable(index - positions[:, at], start, seen, block)
        halves = []
        for head in range(2):
            scores = matmul(keys[:seen, :], head_lanes(own, head), cols_cols)
            scores = jnp.where(allowed, scores, masked_score)
            highest = jnp.max(scores, axis=0, keepdims=True)
            weights = jnp.exp(scores - highest)
            sums = jnp.sum(weights, axis=0, keepdims=True)
            result = matmul(values_across[:, :seen], weights.astype(BF16))
            halves.append(result[head * HD : (head + 1) * HD, :] / sums)
            logsums[head : head + 1, at] = highest + jnp.log(sums)
        attended[at, :] = jnp.transpose(jnp.concatenate(halves, axis=0)).astype(BF16)


def pair_spec(length, kind):
    return pl.BlockSpec((None, length, PAIR), lambda pair: (kind, 0, pair))


def attend(mixed, positions):
    _, length, width = mixed.shape
    pairs = width // PAIR
    block = min(256, length)
    return pl.pallas_call(
        functools.partial(attend_kernel, block),
        grid=(pairs,),
        out_shape=(
            jax.ShapeDtypeStruct((length, width), BF16),
            jax.ShapeDtypeStruct((pairs, 2, length), F32),
        ),
        in_specs=[
            pl.BlockSpec((1, length), lambda pair: (0, 0)),
            pair_spec(length, 0),
            pair_spec(length, 1),
            pair_spec(length, 2),
        ],
        out_specs=(
            pl.BlockSpec((length, PAIR), lambda pair: (0, pair)),
            pl.BlockSpec((None, 2, length), lambda pair: (pair, 0, 0)),
        ),
        compiler_params=pltpu.CompilerParams(vmem_limit_bytes=VMEM_LIMIT),
        cost_estimate=pl.CostEstimate(
            flops=8 * length * length * width,
            bytes_accessed=8 * length * width,
            transcendentals=length * length * width // HD,
        ),
    )(positions, mixed, mixed, mixed)


def unrotate(values, cos, sin_up, sin_down):
    return (
        values * cos
        - pltpu.roll(values, PAIR - ROT // 2, 1) * sin_up
        - pltpu.roll(values, ROT // 2, 1) * sin_down
    )


def attend_back_kernel(
    block, positions, queries, keys, values, attended, grad_attended, logsums,
    cos, sin_up, sin_down, grad_mixed, bias_sum, grad_keys, grad_values,
):
    length = keys.shape[0]
    keys_across = jnp.transpose(keys[...])
    grad_keys[...] = jnp.zeros_like(grad_keys)
    grad_values[...] = jnp.zeros_like(grad_values)
    bias_sum[...] = jnp.zeros_like(bias_sum)
    for start in range(0, length, block):
        seen = start + block
        at = slice(start, seen)
        own = queries[at, :]
        grad_own = grad_attended[at, :]
        inner = jnp.transpose(grad_own.astype(F32) * attended[at, :].astype(F32))
        index = start + lax.broadcasted_iota(jnp.int32, (1, block), 1)
        allowed = usable(index - positions[:, at], start, seen, block)
        halves = []
        for head in range(2):
            own_head = head_lanes(own, head)
            grad_head = head_lanes(grad_own, head)
            scores = matmul(keys[:seen, :], own_head, cols_cols)
            weights = jnp.where(allowed, jnp.exp(scores - logsums[head : head + 1, at]), 0.0)
            grad_weights = matmul(values[:seen, :], grad_head, cols_cols)
            row_inner = jnp.sum(inner[head * HD : (head + 1) * HD, :], axis=0, keepdims=True)
            grad_scores = (weights * (grad_weights - row_inner)).astype(BF16)
            grad_values[:seen, :] += matmul(weights.astype(BF16), grad_head)
            grad_keys[:seen, :] += matmul(grad_scores, own_head)
            result = matmul(keys_across[:, :seen], grad_scores)
            halves.append(result[head * HD : (head + 1) * HD, :])
        grad_own_queries = jnp.transpose(jnp.concatenate(halves, axis=0)) * (1.0 / math.sqrt(HD))
        low = unrotate(grad_own_queries, cos[at, :], sin_up[at, :], sin_down[at, :]).astype(BF16)
        grad_mixed[0, at, :] = low
        bias_sum[0:1, :] += jnp.sum(low.astype(F32), axis=0, keepdims=True)
    for start in range(0, length, block):
        at = slice(start, start + block)
        low = unrotate(grad_keys[at, :], cos[at, :], sin_up[at, :], sin_down[at, :]).astype(BF16)
        grad_mixed[1, at, :] = low
        bias_sum[1:2, :] += jnp.sum(low.astype(F32), axis=0, keepdims=True)
        low = grad_values[at, :].astype(BF16)
        grad_mixed[2, at, :] = low
        bias_sum[2:3, :] += jnp.sum(low.astype(F32), axis=0, keepdims=True)


def attend_backward(mixed, positions, attended, grad_attended, logsums, tables):
    _, length, width = mixed.shape
    pairs = width // PAIR
    block = min(256, length)
    across = pl.BlockSpec((length, PAIR), lambda pair: (0, pair))
    table = pl.BlockSpec((length, PAIR), lambda pair: (0, 0))
    return pl.pallas_call(
        functools.partial(attend_back_kernel, block),
        grid=(pairs,),
        out_shape=(
            jax.ShapeDtypeStruct((3, length, width), BF16),
            jax.ShapeDtypeStruct((3, width), F32),
        ),
        in_specs=[
            pl.BlockSpec((1, length), lambda pair: (0, 0)),
            pair_spec(length, 0),
            pair_spec(length, 1),
            pair_spec(length, 2),
            across,
            across,
            pl.BlockSpec((None, 2, length), lambda pair: (pair, 0, 0)),
            table,
            table,
            table,
        ],
        out_specs=(
            pl.BlockSpec((3, length, PAIR), lambda pair: (0, 0, pair)),
            pl.BlockSpec((3, PAIR), lambda pair: (0, pair)),
        ),
        scratch_shapes=[pltpu.VMEM((length, PAIR), F32), pltpu.VMEM((length, PAIR), F32)],
        compiler_params=pltpu.CompilerParams(vmem_limit_bytes=VMEM_LIMIT),
        cost_estimate=pl.CostEstimate(
            flops=20 * length * length * width,
            bytes_accessed=16 * length * width,
            transcendentals=length * length * width // HD,
        ),
    )(positions, mixed, mixed, mixed, attended, grad_attended, logsums, *tables)


def rotary_tables(positions):
    half_rot = ROT // 2
    lane = jnp.arange(PAIR, dtype=jnp.int32) % HD
    frequency = jnp.exp(-((lane % half_rot).astype(F32) * 2.0 / ROT) * theta_log)
    angles = positions.astype(F32)[:, None] * frequency[None, :]
    cos, sin = jnp.cos(angles), jnp.sin(angles)
    return (
        jnp.where(lane < ROT, cos, 1.0),
        jnp.where(lane < half_rot, -sin, 0.0),
        jnp.where((lane >= half_rot) & (lane < ROT), sin, 0.0),
    )


def all_sum(values, axes):
    for axis in axes:
        size = lax.axis_size(axis)
        if size & (size - 1):
            values = lax.psum(values, axis)
            continue
        step = 1
        while step < size:
            values = values + lax.ppermute(values, axis, [(i, i ^ step) for i in range(size)])
            step *= 2
    return values


def owner_sum(part, axis):
    return lax.psum_scatter(part, "dp", scatter_dimension=axis, tiled=True)


def after(values, *others):
    return lax.optimization_barrier((values, *others))


def per_device(
    tokens, positions, norm_gain, norm_bias, w_qkv, b_qkv, w_out, w_gate_up, w_down, cotangent
):
    count = lax.axis_size("tensor")
    tensor_rank = lax.axis_index("tensor")
    width = w_qkv.shape[3]
    ff_local = w_gate_up.shape[3]
    rows, depth = tokens.shape
    length = positions.shape[0]
    tables = rotary_tables(positions)
    positions_row = positions.reshape(1, length)

    def whole(weight, axis):
        return lax.all_gather(weight, "dp", axis=axis, tiled=True)

    flat = [
        [
            w_qkv[layer].reshape(-1, 3 * width),
            w_out[layer],
            w_gate_up[layer].reshape(-1, 2 * ff_local),
            w_down[layer],
        ]
        for layer in range(LAYERS)
    ]
    axes = (0, 1, 0, 1)
    gathered = [[None, whole(flat[0][1], axes[1]), whole(flat[0][2], axes[2]), None]]
    hidden = tokens
    block_tables = tuple(table.reshape(count, rows, -1) for table in tables)
    biases = [
        lax.dynamic_slice_in_dim(b_qkv[layer], tensor_rank * width, width, 1).reshape(1, 3 * width)
        for layer in range(LAYERS)
    ]
    rows_a, mixed, gathered[0][0] = first(
        count, tokens, norm_gain[0, 0:1], norm_bias[0, 0:1], flat[0][0], biases[0], block_tables, width
    )
    mixed, flat[0][3] = after(mixed, flat[0][3])
    gathered[0][3] = whole(flat[0][3], axes[3])
    kept = []
    for layer in range(LAYERS):
        mixed = mixed.reshape(3, length, width)
        attended, logsums = attend(mixed, positions_row)
        if layer + 1 < LAYERS:
            attended, *flat[layer + 1] = after(attended, *flat[layer + 1])
            gathered.append([whole(flat[layer + 1][kind], axes[kind]) for kind in range(4)])
        full_qkv, full_out, full_gu, full_down = gathered[layer]
        hidden_mid, rows_b, act, slope, silu = middle(
            count,
            attended.reshape(count, rows, width),
            full_out,
            hidden,
            norm_gain[layer, 1:2],
            norm_bias[layer, 1:2],
            full_gu,
            LAG if layer == 0 else 0,
        )
        kept.append((hidden, rows_a, mixed, attended, logsums, hidden_mid, rows_b, act, slope, silu))
        if layer + 1 < LAYERS:
            hidden, rows_a, mixed = between(
                count,
                act,
                full_down,
                hidden_mid,
                norm_gain[layer + 1, 0:1],
                norm_bias[layer + 1, 0:1],
                gathered[layer + 1][0],
                biases[layer + 1],
                block_tables,
            )
        else:
            activations, grad_rows_b, wide = turn(
                count, act, full_down, hidden_mid, cotangent, slope, silu
            )
    grad = cotangent
    scattered = [None] * LAYERS
    small = [None] * LAYERS
    for layer in reversed(range(LAYERS)):
        hidden, rows_a, mixed, attended, logsums, hidden_mid, rows_b, act, slope, silu = kept[layer]
        full_qkv, full_out, full_gu, full_down = gathered[layer]
        later = scattered[layer + 1] if layer + 1 < LAYERS else None
        gu_part = matmul(
            rows_b.reshape(length, depth), wide.reshape(length, 2 * ff_local), rows_rows
        ).astype(BF16)
        down_part = matmul(
            act.reshape(length, ff_local), grad_rows_b.reshape(length, depth), rows_rows
        ).astype(BF16)
        wide, down_part, gu_part = after(wide, down_part, gu_part)
        gu_grad, down_grad = owner_sum(gu_part, 0), owner_sum(down_part, 1)
        if later:
            wide, later[2] = after(wide, later[2])
        grad, gain_b, shift_b, grad_rows_a, grad_attended = middle_back(
            count, wide, full_gu, grad, hidden_mid, norm_gain[layer, 1:2], full_out
        )
        out_part = matmul(attended, grad_rows_a.reshape(length, depth), rows_rows).astype(BF16)
        grad_attended, out_part = after(grad_attended, out_part)
        out_grad = owner_sum(out_part, 1)
        if later:
            grad_attended, later[3] = after(grad_attended, later[3])
        grad_mixed, bias_sum = attend_backward(
            mixed, positions_row, attended, grad_attended.reshape(length, width), logsums, tables
        )
        flat_mixed = grad_mixed.transpose(1, 0, 2).reshape(length, 3 * width)
        qkv_part = matmul(rows_a.reshape(length, depth), flat_mixed, rows_rows).astype(BF16)
        grad_mixed, qkv_part = after(grad_mixed, qkv_part)
        if layer:
            qkv_grad = owner_sum(qkv_part, 0)
        if later:
            grad_mixed, later[0], later[1] = after(grad_mixed, later[0], later[1])
        source = grad_mixed.reshape(3, count, rows, width)
        if layer:
            below = kept[layer - 1]
            grad, gain_a, shift_a, grad_rows_b, wide = between_back(
                count,
                source,
                full_qkv,
                grad,
                hidden,
                norm_gain[layer, 0:1],
                gathered[layer - 1][3],
                below[8],
                below[9],
            )
        else:
            grad, gain_a, shift_a, qkv_grad = last(
                count, source, full_qkv, grad, hidden, norm_gain[layer, 0:1], qkv_part
            )
        bias_full = lax.dynamic_update_slice(
            jnp.zeros((3, b_qkv.shape[2]), F32), bias_sum, (jnp.int32(0), tensor_rank * width)
        )
        small[layer] = jnp.concatenate([gain_a, gain_b, shift_a, shift_b, bias_full], axis=0)
        scattered[layer] = [qkv_grad, out_grad, gu_grad, down_grad]
    sums = all_sum(jnp.stack(small), ("dp", "tensor"))
    shapes = ((-1, 3, width), (width, -1), (-1, 2, ff_local), (ff_local, -1))
    stacks = [
        jnp.stack([scattered[layer][kind].astype(F32).reshape(shape) for layer in range(LAYERS)])
        for kind, shape in enumerate(shapes)
    ]
    return (
        activations,
        grad,
        sums[:, 0:2],
        sums[:, 2:4],
        stacks[0],
        sums[:, 4:7],
        stacks[1],
        stacks[2],
        stacks[3],
    )


def norm_parts(hidden):
    average = jnp.mean(hidden, axis=-1, keepdims=True)
    centred = hidden - average
    variance = jnp.mean(centred * centred, axis=-1, keepdims=True)
    inverse = lax.rsqrt(variance + norm_eps)
    return (centred * inverse, inverse)


def norm_back(grad_normed, scaled, inverse, norm_weight):
    weighted = grad_normed * norm_weight
    first_mean = jnp.mean(weighted, axis=-1, keepdims=True)
    second_mean = jnp.mean(weighted * scaled, axis=-1, keepdims=True)
    grad_input = inverse * (weighted - first_mean - scaled * second_mean)
    return (grad_input, jnp.sum(grad_normed * scaled, axis=0), jnp.sum(grad_normed, axis=0))


def plain_tables(positions):
    half_rot = ROT // 2
    frequency = jnp.exp(-(jnp.arange(half_rot, dtype=jnp.float32) * 2.0 / ROT) * theta_log)
    angles = positions.astype(jnp.float32)[:, None] * frequency[None, :]
    return (jnp.cos(angles)[:, None, :], jnp.sin(angles)[:, None, :])


def rotate(values, cos_table, sin_table):
    half_rot = ROT // 2
    first_half = values[..., :half_rot]
    second_half = values[..., half_rot:ROT]
    return jnp.concatenate(
        [
            first_half * cos_table - second_half * sin_table,
            second_half * cos_table + first_half * sin_table,
            values[..., ROT:],
        ],
        axis=-1,
    )


def inner_rows(left, right):
    return lax.dot_general(left, right, rows_rows, preferred_element_type=jnp.float32)


def inner_cols(left, right):
    return lax.dot_general(left, right, cols_cols, preferred_element_type=jnp.float32)


def block_scores(queries, key_rows, positions, number, block_rows, score_scale):
    seq_len = key_rows.shape[0]
    row_start = number * block_rows
    query_block = lax.dynamic_slice_in_dim(queries, row_start, block_rows, 0)
    scores = (
        jnp.einsum("qhd,khd->hqk", query_block, key_rows, preferred_element_type=jnp.float32)
        * score_scale
    )
    row_index = row_start + jnp.arange(block_rows, dtype=jnp.int32)
    first_key = row_index - lax.dynamic_slice_in_dim(positions, row_start, block_rows, 0)
    columns = jnp.arange(seq_len, dtype=jnp.int32)
    allowed = (columns[None, :] <= row_index[:, None]) & (columns[None, :] >= first_key[:, None])
    return (query_block, allowed, jnp.where(allowed[None], scores, masked_score))


def attend_forward(queries, key_rows, values, positions, score_scale):
    seq_len = queries.shape[0]
    block_rows = min(512, seq_len)

    def one_block(number):
        query_block, allowed, scores = block_scores(
            queries, key_rows, positions, number, block_rows, score_scale
        )
        row_max = jnp.max(scores, axis=-1, keepdims=True)
        shifted = jnp.exp(scores - row_max)
        row_sum = jnp.sum(shifted, axis=-1, keepdims=True)
        weights_low = (shifted / row_sum).astype(jnp.bfloat16)
        block_out = jnp.einsum(
            "hqk,khd->qhd", weights_low, values, preferred_element_type=jnp.float32
        )
        return (block_out, row_max + jnp.log(row_sum))

    block_outs, logsums = lax.map(one_block, jnp.arange(seq_len // block_rows, dtype=jnp.int32))
    return (block_outs.reshape(seq_len, -1), logsums)


def attend_back(queries, key_rows, values, positions, logsums, grad_attended, score_scale):
    seq_len = queries.shape[0]
    block_rows = min(512, seq_len)

    def one_block(totals, inputs):
        grad_keys, grad_values = totals
        number, logsum = inputs
        query_block, allowed, scores = block_scores(
            queries, key_rows, positions, number, block_rows, score_scale
        )
        softmax_rows = jnp.exp(scores - logsum)
        grad_block = lax.dynamic_slice_in_dim(grad_attended, number * block_rows, block_rows, 0)
        grad_probs = jnp.einsum(
            "qhd,khd->hqk", grad_block, values, preferred_element_type=jnp.float32
        )
        grad_values = grad_values + jnp.einsum(
            "hqk,qhd->khd",
            softmax_rows.astype(jnp.bfloat16),
            grad_block,
            preferred_element_type=jnp.float32,
        )
        row_inner = jnp.sum(softmax_rows * grad_probs, axis=-1, keepdims=True)
        grad_scores = jnp.where(allowed[None], softmax_rows * (grad_probs - row_inner), 0.0).astype(
            jnp.bfloat16
        )
        grad_query = (
            jnp.einsum("hqk,khd->qhd", grad_scores, key_rows, preferred_element_type=jnp.float32)
            * score_scale
        )
        grad_keys = (
            grad_keys
            + jnp.einsum(
                "hqk,qhd->khd", grad_scores, query_block, preferred_element_type=jnp.float32
            )
            * score_scale
        )
        return ((grad_keys, grad_values), grad_query)

    empty_grad = jnp.zeros(key_rows.shape, jnp.float32)
    numbers = jnp.arange(seq_len // block_rows, dtype=jnp.int32)
    (grad_keys, grad_values), grad_queries = lax.scan(
        one_block, (empty_grad, empty_grad), (numbers, logsums)
    )
    return (grad_queries.reshape(queries.shape), grad_keys, grad_values)


def per_device_plain(
    tokens, positions, norm_gain, norm_bias, w_qkv, b_qkv, w_out, w_gate_up, w_down, cotangent
):
    tensor_rank = lax.axis_index("tensor")
    width_local = w_qkv.shape[3]
    heads_local = width_local // HD
    ff_local = w_gate_up.shape[3]
    local_rows = tokens.shape[0]
    seq_len = positions.shape[0]
    score_scale = 1.0 / math.sqrt(HD)
    cos_table, sin_table = plain_tables(positions)
    hidden = tokens.astype(jnp.float32)
    kept_state = []
    for layer_index in range(LAYERS):
        gathered = (
            lax.all_gather(w_qkv[layer_index], "dp", axis=0, tiled=True),
            lax.all_gather(w_out[layer_index], "dp", axis=1, tiled=True),
            lax.all_gather(w_gate_up[layer_index], "dp", axis=0, tiled=True),
            lax.all_gather(w_down[layer_index], "dp", axis=1, tiled=True),
        )
        full_qkv, full_out, full_gu, full_down = gathered
        scaled_a, inverse_a = norm_parts(hidden)
        normed_a = (scaled_a * norm_gain[layer_index, 0] + norm_bias[layer_index, 0]).astype(
            jnp.bfloat16
        )
        rows_a = lax.all_gather(normed_a, "tensor", axis=0, tiled=True)
        bias_local = lax.dynamic_slice_in_dim(
            b_qkv[layer_index], tensor_rank * width_local, width_local, 1
        )
        mixed = jnp.dot(
            rows_a,
            full_qkv.reshape(full_qkv.shape[0], 3 * width_local),
            preferred_element_type=jnp.float32,
        ) + bias_local.reshape(3 * width_local)
        mixed = mixed.reshape(seq_len, 3, heads_local, HD)
        queries = rotate(mixed[:, 0], cos_table, sin_table).astype(jnp.bfloat16)
        key_rows = rotate(mixed[:, 1], cos_table, sin_table).astype(jnp.bfloat16)
        values = mixed[:, 2].astype(jnp.bfloat16)
        attended, logsums = attend_forward(queries, key_rows, values, positions, score_scale)
        attended = attended.astype(jnp.bfloat16)

        def project_attn(row_start, row_count, source=attended, weight=full_out):
            return jnp.dot(source, weight, preferred_element_type=jnp.float32)

        branch_a = lax.psum_scatter(
            project_attn(jnp.int32(0), local_rows * lax.axis_size("tensor")).astype(jnp.bfloat16),
            "tensor",
            scatter_dimension=0,
            tiled=True,
        ).astype(jnp.float32)
        hidden_mid = hidden + branch_a
        scaled_b, inverse_b = norm_parts(hidden_mid)
        normed_b = (scaled_b * norm_gain[layer_index, 1] + norm_bias[layer_index, 1]).astype(
            jnp.bfloat16
        )
        rows_b = lax.all_gather(normed_b, "tensor", axis=0, tiled=True)
        gate_up = jnp.dot(
            rows_b,
            full_gu.reshape(full_gu.shape[0], 2 * ff_local),
            preferred_element_type=jnp.float32,
        ).reshape(seq_len, 2, ff_local)
        activated = (jax.nn.silu(gate_up[:, 0]) * gate_up[:, 1]).astype(jnp.bfloat16)

        def project_mlp(row_start, row_count, source=activated, weight=full_down):
            return jnp.dot(source, weight, preferred_element_type=jnp.float32)

        hidden = hidden_mid + lax.psum_scatter(
            project_mlp(jnp.int32(0), local_rows * lax.axis_size("tensor")).astype(jnp.bfloat16),
            "tensor",
            scatter_dimension=0,
            tiled=True,
        ).astype(jnp.float32)
        kept_state.append(
            (
                gathered,
                scaled_a,
                inverse_a,
                rows_a,
                queries,
                key_rows,
                values,
                logsums,
                attended,
                scaled_b,
                inverse_b,
                rows_b,
                gate_up,
                activated,
            )
        )
    activations = hidden.astype(jnp.bfloat16)
    grad = cotangent.astype(jnp.float32)
    weight_parts = [None] * LAYERS
    gain_rows = [None] * LAYERS
    shift_rows = [None] * LAYERS
    qkv_shift_rows = [None] * LAYERS
    for layer_index in reversed(range(LAYERS)):
        (
            gathered,
            scaled_a,
            inverse_a,
            rows_a,
            queries,
            key_rows,
            values,
            logsums,
            attended,
            scaled_b,
            inverse_b,
            rows_b,
            gate_up,
            activated,
        ) = kept_state[layer_index]
        full_qkv, full_out, full_gu, full_down = (
            lax.all_gather(w_qkv[layer_index], "dp", axis=0, tiled=True),
            lax.all_gather(w_out[layer_index], "dp", axis=1, tiled=True),
            lax.all_gather(w_gate_up[layer_index], "dp", axis=0, tiled=True),
            lax.all_gather(w_down[layer_index], "dp", axis=1, tiled=True),
        )
        grad_rows_b = lax.all_gather(grad.astype(jnp.bfloat16), "tensor", axis=0, tiled=True)
        grad_down_weight = inner_rows(activated, grad_rows_b)
        grad_act = inner_cols(grad_rows_b, full_down)
        gate_part = gate_up[:, 0]
        up_part = gate_up[:, 1]
        sigmoid_gate = jax.nn.sigmoid(gate_part)
        grad_gate = grad_act * up_part * sigmoid_gate * (1.0 + gate_part * (1.0 - sigmoid_gate))
        grad_up = grad_act * jax.nn.silu(gate_part)
        grad_gate_up = (
            jnp.stack([grad_gate, grad_up], axis=1)
            .astype(jnp.bfloat16)
            .reshape(seq_len, 2 * ff_local)
        )
        grad_gu_weight = inner_rows(rows_b, grad_gate_up).reshape(full_gu.shape)
        flat_gu = full_gu.reshape(full_gu.shape[0], 2 * ff_local)

        def back_mlp(row_start, row_count, source=grad_gate_up, weight=flat_gu):
            return inner_cols(source, weight)

        grad_normed_b = lax.psum_scatter(
            back_mlp(jnp.int32(0), local_rows * lax.axis_size("tensor")).astype(jnp.bfloat16),
            "tensor",
            scatter_dimension=0,
            tiled=True,
        ).astype(jnp.float32)
        grad_in_b, gain_b, shift_b = norm_back(
            grad_normed_b, scaled_b, inverse_b, norm_gain[layer_index, 1]
        )
        grad = grad + grad_in_b
        grad_rows_a = lax.all_gather(grad.astype(jnp.bfloat16), "tensor", axis=0, tiled=True)
        grad_out_weight = inner_rows(attended, grad_rows_a)
        grad_attended = inner_cols(grad_rows_a, full_out).astype(jnp.bfloat16)
        grad_attended = grad_attended.reshape(seq_len, heads_local, HD)
        grad_queries, grad_keys, grad_values = attend_back(
            queries, key_rows, values, positions, logsums, grad_attended, score_scale
        )
        grad_queries = rotate(grad_queries, cos_table, -sin_table)
        grad_keys = rotate(grad_keys, cos_table, -sin_table)
        grad_mixed = jnp.stack([grad_queries, grad_keys, grad_values], axis=1)
        grad_mixed = grad_mixed.reshape(seq_len, 3 * width_local).astype(jnp.bfloat16)
        qkv_shift_local = jnp.sum(grad_mixed, axis=0, dtype=jnp.float32).reshape(3, width_local)
        qkv_shift_rows[layer_index] = lax.dynamic_update_slice(
            jnp.zeros((3, b_qkv.shape[2]), jnp.float32),
            qkv_shift_local,
            (jnp.int32(0), tensor_rank * width_local),
        )
        grad_qkv_weight = inner_rows(rows_a, grad_mixed).reshape(full_qkv.shape)
        flat_qkv = full_qkv.reshape(full_qkv.shape[0], 3 * width_local)

        def back_attn(row_start, row_count, source=grad_mixed, weight=flat_qkv):
            return inner_cols(source, weight)

        grad_normed_a = lax.psum_scatter(
            back_attn(jnp.int32(0), local_rows * lax.axis_size("tensor")).astype(jnp.bfloat16),
            "tensor",
            scatter_dimension=0,
            tiled=True,
        ).astype(jnp.float32)
        grad_in_a, gain_a, shift_a = norm_back(
            grad_normed_a, scaled_a, inverse_a, norm_gain[layer_index, 0]
        )
        grad = grad + grad_in_a
        gain_rows[layer_index] = jnp.stack([gain_a, gain_b])
        shift_rows[layer_index] = jnp.stack([shift_a, shift_b])
        weight_parts[layer_index] = (
            lax.psum_scatter(
                grad_qkv_weight.astype(jnp.bfloat16), "dp", scatter_dimension=0, tiled=True
            ).astype(jnp.float32),
            lax.psum_scatter(
                grad_out_weight.astype(jnp.bfloat16), "dp", scatter_dimension=1, tiled=True
            ).astype(jnp.float32),
            lax.psum_scatter(
                grad_gu_weight.astype(jnp.bfloat16), "dp", scatter_dimension=0, tiled=True
            ).astype(jnp.float32),
            lax.psum_scatter(
                grad_down_weight.astype(jnp.bfloat16), "dp", scatter_dimension=1, tiled=True
            ).astype(jnp.float32),
        )
    stack_qkv = jnp.stack([weight_parts[number][0] for number in range(LAYERS)])
    stack_out = jnp.stack([weight_parts[number][1] for number in range(LAYERS)])
    stack_gu = jnp.stack([weight_parts[number][2] for number in range(LAYERS)])
    stack_down = jnp.stack([weight_parts[number][3] for number in range(LAYERS)])
    gain_grad, norm_bias_grad, qkv_bias_grad = lax.psum(
        (jnp.stack(gain_rows), jnp.stack(shift_rows), jnp.stack(qkv_shift_rows)), ("dp", "tensor")
    )
    return (
        activations,
        grad,
        gain_grad,
        norm_bias_grad,
        stack_qkv,
        qkv_bias_grad,
        stack_out,
        stack_gu,
        stack_down,
    )


def solution(mesh):
    in_specs = (
        P(("dp", "tensor"), None),
        P("dp"),
        P(),
        P(),
        P(None, "dp", None, "tensor"),
        P(),
        P(None, "tensor", "dp"),
        P(None, "dp", None, "tensor"),
        P(None, "tensor", "dp"),
        P(("dp", "tensor"), None),
    )
    out_specs = (
        P(("dp", "tensor"), None),
        P(("dp", "tensor"), None),
        P(),
        P(),
        P(None, "dp", None, "tensor"),
        P(),
        P(None, "tensor", "dp"),
        P(None, "dp", None, "tensor"),
        P(None, "tensor", "dp"),
    )
    def run(*operands):
        fits = operands[7].shape[3] % 128 == 0 and operands[4].shape[3] % PAIR == 0
        return (per_device if fits else per_device_plain)(*operands)

    return jax.shard_map(
        run, mesh=mesh, in_specs=in_specs, out_specs=out_specs, check_vma=False
    )
```

```python
import functools
import math

import jax
import jax.numpy as jnp
from jax import lax
from jax.experimental import pallas as pl
from jax.experimental.pallas import tpu as pltpu
from jax.sharding import PartitionSpec as P

HD = 64
ROT = 16
LAYERS = 2
PAIR = 2 * HD
MESH = pl.DeviceIdType.MESH
F32 = jnp.float32
BF16 = jnp.bfloat16
VMEM_LIMIT = 62 * 2**20
LAG = 6

norm_eps = 1e-05
theta_log = math.log(10000.0)
masked_score = -1e30
rows_rows = (((0,), (0,)), ((), ()))
cols_cols = (((1,), (1,)), ((), ()))
rows_cols = (((1,), (0,)), ((), ()))


def matmul(left, right, dims=rows_cols):
    return lax.dot_general(left, right, dims, preferred_element_type=F32)


def member_at(member, step):
    bit = 1
    while bit <= step:
        if step & bit:
            member = member + bit * (1 - 2 * ((member // bit) % 2))
        bit *= 2
    return member


class Whole:
    def __init__(self, held, size, send_sem, recv_sem):
        self.held, self.size, self.send_sem, self.recv_sem = held, size, send_sem, recv_sem
        self.member = lax.axis_index("dp")
        self.share = held.shape[0] // size
        self.evens = range(0, size, 2)

    def peers(self):
        return tuple(member_at(self.member, step) for step in self.evens if step) + (
            member_at(self.member, 1),
        )

    def rows(self, step):
        start = member_at(self.member, step) * self.share
        return pl.ds(pl.multiple_of(start, self.share), self.share)

    def hop(self, source_step, target_step, number):
        return pltpu.make_async_remote_copy(
            src_ref=self.held.at[self.rows(source_step)],
            dst_ref=self.held.at[self.rows(source_step)],
            send_sem=self.send_sem.at[number],
            recv_sem=self.recv_sem.at[number],
            device_id={"dp": member_at(self.member, target_step)},
            device_id_type=MESH,
        )

    def to_chips(self, step):
        return self.hop(0, step, step)

    def to_core(self, step):
        return self.hop(step, 1, step + 1)

    def start(self):
        for step in self.evens:
            if step:
                self.to_chips(step).start()
        self.to_core(0).start()

    def pass_on(self):
        for step in self.evens:
            if step:
                self.to_chips(step).wait_recv()
                self.to_core(step).start()

    def wait(self):
        for step in self.evens:
            self.to_core(step).wait_recv()

    def drain(self):
        for step in self.evens:
            if step:
                self.to_chips(step).wait_send()
            self.to_core(step).wait_send()


def line_barrier(place, count, others=()):
    barrier = pltpu.get_barrier_semaphore()
    for other in others:
        pl.semaphore_signal(barrier, inc=1, device_id={"dp": other}, device_id_type=MESH)

    @pl.when(place > 0)
    def _():
        pl.semaphore_signal(barrier, inc=1, device_id={"tensor": place - 1}, device_id_type=MESH)

    @pl.when(place < count - 1)
    def _():
        pl.semaphore_signal(barrier, inc=1, device_id={"tensor": place + 1}, device_id_type=MESH)

    middle = (place > 0) & (place < count - 1)

    @pl.when(middle)
    def _():
        pl.semaphore_wait(barrier, 2 + len(others))

    @pl.when(jnp.logical_not(middle))
    def _():
        pl.semaphore_wait(barrier, 1 + len(others))


def each_tile(width, tile, run):
    def one(number, carry):
        run(pl.multiple_of(number * tile, tile), tile)
        return carry

    lax.fori_loop(0, width // tile, one, 0)
    if width % tile:
        run(width // tile * tile, width % tile)


class Line:
    def __init__(self, count, pieces, shares, sending, arrived, sum_send, sum_recv, held, send_sem, recv_sem):
        self.count, self.pieces = count, pieces
        self.shares, self.sending, self.arrived = shares, sending, arrived
        self.sum_send, self.sum_recv = sum_send, sum_recv
        self.held, self.send_sem, self.recv_sem = held, send_sem, recv_sem
        self.place = lax.axis_index("tensor")
        self.rows = (held if held is not None else sending).shape[1] // pieces

    def at(self, piece):
        return pl.ds(pl.multiple_of(piece * self.rows, self.rows), self.rows)

    def sum_hop(self, piece, owner):
        right = owner > self.place
        target = jnp.where(right, self.place + 1, self.place - 1)
        slot = jnp.where(right | (owner != target), owner, self.count)
        return pltpu.make_async_remote_copy(
            src_ref=self.sending.at[owner, self.at(piece)],
            dst_ref=self.arrived.at[slot, self.at(piece)],
            send_sem=self.sum_send.at[owner, piece],
            recv_sem=self.sum_recv.at[slot, piece],
            device_id={"tensor": target},
            device_id_type=MESH,
        )

    def sum_landed(self, piece, slot):
        return pltpu.make_async_remote_copy(
            src_ref=self.sending.at[0, self.at(piece)],
            dst_ref=self.arrived.at[slot, self.at(piece)],
            send_sem=self.sum_send.at[0, piece],
            recv_sem=self.sum_recv.at[slot, piece],
            device_id={"tensor": self.place},
            device_id_type=MESH,
        )

    def row_hop(self, piece, block, right):
        return pltpu.make_async_remote_copy(
            src_ref=self.held.at[block, self.at(piece)],
            dst_ref=self.held.at[block, self.at(piece)],
            send_sem=self.send_sem.at[jnp.where(right, 0, 1), block, piece],
            recv_sem=self.recv_sem.at[block, piece],
            device_id={"tensor": jnp.where(right, self.place + 1, self.place - 1)},
            device_id_type=MESH,
        )

    def sides(self, away, run):
        def one(side, carry):
            block = jnp.where(side == 0, self.place + away, self.place - away)

            @pl.when((block >= 0) & (block < self.count))
            def _():
                run(block, side == 0)

            return carry

        lax.fori_loop(0, 2, one, 0)

    def chunks(self, run):
        chunk = min(16, self.rows)

        def one(number, carry):
            run(pl.multiple_of(number * chunk, chunk), chunk)
            return carry

        lax.fori_loop(0, self.rows // chunk, one, 0)

    def pass_on(self, piece, owner, right):
        first = pl.multiple_of(piece * self.rows, self.rows)
        onward = jnp.where(right, self.place > 0, self.place < self.count - 1)

        @pl.when(onward)
        def _():
            self.sum_landed(piece, owner).wait_recv()

            def rows(start, size):
                at = pl.ds(pl.multiple_of(first + start, size), size)
                self.sending[owner, at, :] = (
                    self.shares[owner, at, :]
                    + self.arrived[owner, at, :].astype(F32)
                ).astype(BF16)

            self.chunks(rows)

        @pl.when(jnp.logical_not(onward))
        def _():
            def rows(start, size):
                at = pl.ds(pl.multiple_of(first + start, size), size)
                self.sending[owner, at, :] = self.shares[owner, at, :].astype(BF16)

            self.chunks(rows)

        self.sum_hop(piece, owner).start()

    def collect(self, piece):
        first = pl.multiple_of(piece * self.rows, self.rows)

        def add(slot):
            self.sum_landed(piece, slot).wait_recv()

            def rows(start, size):
                at = pl.ds(pl.multiple_of(first + start, size), size)
                self.shares[self.place, at, :] = self.shares[self.place, at, :] + self.arrived[
                    slot, at, :
                ].astype(F32)

            self.chunks(rows)

        @pl.when(self.place > 0)
        def _():
            add(self.place)

        @pl.when(self.place < self.count - 1)
        def _():
            add(self.count)

    def own_rows(self, piece, run):
        first = pl.multiple_of(piece * self.rows, self.rows)

        def rows(start, size):
            at = pl.ds(pl.multiple_of(first + start, size), size)
            run(at, self.shares[self.place, at, :])

        self.chunks(rows)

    def run(self, term, finish, process, each_tick=None, delay=0):
        count, pieces, place = self.count, self.pieces, self.place
        scatter, gather = term is not None, process is not None
        lead = count - 1 if scatter else 0
        if scatter:
            term(0)

        def tick(number, carry):
            if each_tick is not None:
                each_tick(number)

            def valid(piece):
                return (piece >= 0) & (piece < pieces)

            if scatter:

                def sum_step(step, inner):
                    piece = number - step

                    @pl.when(valid(piece))
                    def _():
                        self.sides(
                            count - 1 - step,
                            lambda owner, right: self.pass_on(piece, owner, right),
                        )

                    return inner

                lax.fori_loop(0, count - 1, sum_step, 0)
            mine = number - lead

            @pl.when(valid(mine))
            def _():
                if scatter:
                    self.collect(mine)
                finish(mine)
                if gather:

                    @pl.when(place < count - 1)
                    def _():
                        self.row_hop(mine, place, True).start()

                    @pl.when(place > 0)
                    def _():
                        self.row_hop(mine, place, False).start()

            if gather:

                def row_step(step, inner):
                    piece = mine - step

                    def forward(block, right):
                        self.row_hop(piece, block, True).wait_recv()
                        onward = jnp.where(right, place > 0, place < count - 1)

                        @pl.when(onward)
                        def _():
                            self.row_hop(piece, block, jnp.logical_not(right)).start()

                    @pl.when(valid(piece))
                    def _():
                        self.sides(step, forward)

                    return inner

                lax.fori_loop(1, count, row_step, 0)
            if scatter:

                @pl.when(number + 1 < pieces)
                def _():
                    term(number + 1)

            if gather:

                @pl.when(valid(mine - (count - 1) - delay))
                def _():
                    process(mine - (count - 1) - delay)

            return carry

        lax.fori_loop(0, pieces + lead + (count - 1 + delay if gather else 0), tick, 0)

    def drain(self):
        def piece_sends(piece, carry):
            def owner_sends(owner, inner):
                if self.sending is not None:

                    @pl.when(owner != self.place)
                    def _():
                        self.sum_hop(piece, owner).wait_send()

                if self.held is not None:

                    @pl.when((owner <= self.place) & (self.place < self.count - 1))
                    def _():
                        self.row_hop(piece, owner, True).wait_send()

                    @pl.when((owner >= self.place) & (self.place > 0))
                    def _():
                        self.row_hop(piece, owner, False).wait_send()

                return inner

            lax.fori_loop(0, self.count, owner_sends, 0)
            return carry

        lax.fori_loop(0, self.pieces, piece_sends, 0)


def norm_rows(values):
    average = jnp.mean(values, axis=-1, keepdims=True)
    centred = values - average
    variance = jnp.mean(centred * centred, axis=-1, keepdims=True)
    inverse = lax.rsqrt(variance + norm_eps)
    return centred * inverse, inverse


def scatter_scratch(count, pieces, rows, width):
    return [
        pltpu.VMEM((count, rows, width), F32),
        pltpu.VMEM((count, rows, width), BF16),
        pltpu.VMEM((count + 1, rows, width), BF16),
        pltpu.SemaphoreType.DMA((count, pieces)),
        pltpu.SemaphoreType.DMA((count + 1, pieces)),
    ]


def gather_scratch(count, pieces, rows, width):
    return [
        pltpu.VMEM((count, rows, width), BF16),
        pltpu.SemaphoreType.DMA((2, count, pieces)),
        pltpu.SemaphoreType.DMA((count, pieces)),
    ]


vmem = pl.BlockSpec(memory_space=pltpu.VMEM)
hbm = pl.BlockSpec(memory_space=pl.ANY)


class Loads:
    def __init__(self, pairs, sems):
        self.copies = [
            pltpu.make_async_copy(source, target, sems.at[number])
            for number, (source, target) in enumerate(pairs)
        ]
        for copy in self.copies:
            copy.start()

    def wait(self, *numbers):
        for number in numbers:
            self.copies[number].wait()


class Tiles:
    def __init__(self, source, target, axis, sems):
        self.source, self.target, self.axis, self.sems = source, target, axis, sems
        self.size = min(256, target.shape[axis])
        for number in range(target.shape[axis] // self.size):
            self.copy(number).start()

    def copy(self, number):
        at = pl.ds(pl.multiple_of(number * self.size, self.size), self.size)
        where = (at,) if self.axis == 0 else (slice(None), at)
        return pltpu.make_async_copy(
            self.source.at[where], self.target.at[where], self.sems.at[number]
        )

    def need(self, piece, start):
        @pl.when(piece == 0)
        def _():
            self.copy(start // self.size).wait()


class Saves:
    def __init__(self, pairs, sems, line):
        self.pairs, self.sems, self.line = pairs, sems, line

    def copy(self, number, piece):
        source, target = self.pairs[number]
        rows = self.line.at(piece)
        where = (slice(None),) * (len(source.shape) - 2) + (rows,)
        return pltpu.make_async_copy(
            source.at[where], target.at[where], self.sems.at[number, piece]
        )

    def start(self, piece):
        for number in range(len(self.pairs)):
            self.copy(number, piece).start()

    def wait(self):
        for number in range(len(self.pairs)):
            for piece in range(self.line.pieces):
                self.copy(number, piece).wait()


def flat_rows(ref, rows, columns=slice(None)):
    values = ref[:, rows, columns]
    return values.reshape(values.shape[0] * values.shape[1], values.shape[2])


def put_rows(ref, rows, columns, values):
    count = ref.shape[0]
    ref[:, rows, columns] = values.reshape(count, values.shape[0] // count, values.shape[1])


def line_call(body, out_shape, out_specs, in_specs, scratch, number, flops, moved):
    return pl.pallas_call(
        body,
        out_shape=out_shape,
        in_specs=in_specs,
        out_specs=out_specs,
        scratch_shapes=scratch,
        compiler_params=pltpu.CompilerParams(
            collective_id=number, has_side_effects=True, vmem_limit_bytes=VMEM_LIMIT
        ),
        cost_estimate=pl.CostEstimate(flops=flops, bytes_accessed=moved, transcendentals=0),
    )


def pieces_of(rows):
    return 4 if rows % 64 == 0 else 1


def query_key_value(line, weight, bias, tables, mixed):
    cos, sin_up, sin_down = tables
    width = mixed.shape[3]

    def factor(table, rows, size):
        return jnp.concatenate([flat_rows(table, rows)] * (size // PAIR), axis=1)

    def process(piece):
        rows = line.at(piece)

        def columns(kind):
            def run(start, size):
                source = pl.ds(pl.multiple_of(kind * width + start, 128), size)
                result = matmul(flat_rows(line.held, rows), weight[:, source]) + bias[:, source]
                if kind < 2:
                    result = (
                        result * factor(cos, rows, size)
                        + pltpu.roll(result, size - ROT // 2, 1) * factor(sin_up, rows, size)
                        + pltpu.roll(result, ROT // 2, 1) * factor(sin_down, rows, size)
                    )
                if kind == 0:
                    result = result * (1.0 / math.sqrt(HD))
                put_rows(mixed.at[kind], rows, pl.ds(start, size), result.astype(BF16))

            return run

        for kind in range(3):
            each_tile(width, min(256, width), columns(kind))

    return process


def gate_and_up(line, weight, act, slope, silu):
    width = act.shape[2]

    def process(piece):
        rows = line.at(piece)

        def run(start, size):
            at = pl.ds(start, size)
            own = flat_rows(line.held, rows)
            gate = matmul(own, weight[:, at])
            up = matmul(own, weight[:, pl.ds(pl.multiple_of(width + start, 128), size)])
            sigmoid = jax.nn.sigmoid(gate)
            soft = gate * sigmoid
            put_rows(act, rows, at, (soft * up).astype(BF16))
            put_rows(silu, rows, at, soft.astype(BF16))
            put_rows(slope, rows, at, (up * sigmoid * (1.0 + gate * (1.0 - sigmoid))).astype(BF16))

        each_tile(width, 256, run)

    return process


def grad_gate_and_up(line, weight, slope, silu, wide):
    width = slope.shape[2]

    def process(piece):
        rows = line.at(piece)

        def run(start, size):
            at = pl.ds(start, size)
            grad_act = matmul(flat_rows(line.held, rows), weight[at, :], cols_cols)
            put_rows(wide, rows, at, (grad_act * flat_rows(slope, rows, at).astype(F32)).astype(BF16))
            put_rows(
                wide,
                rows,
                pl.ds(pl.multiple_of(width + start, 128), size),
                (grad_act * flat_rows(silu, rows, at).astype(F32)).astype(BF16),
            )

        each_tile(width, 256, run)

    return process


def through_transposed(line, weight, result):
    def process(piece):
        rows = line.at(piece)

        def run(start, size):
            at = pl.ds(start, size)
            put_rows(
                result, rows, at, matmul(flat_rows(line.held, rows), weight[at, :], cols_cols).astype(BF16)
            )

        each_tile(result.shape[2], 256, run)

    return process


def share_of(line, source, weight, tiles):
    def term(piece):
        rows = line.at(piece)

        def run(start, size):
            tiles.need(piece, start)
            at = pl.ds(start, size)
            put_rows(line.shares, rows, at, matmul(flat_rows(source, rows), weight[:, at]))

        each_tile(line.shares.shape[2], 256, run)

    return term


def share_transposed(line, sources, weight, tiles):
    width = sources[0].shape[2]

    def term(piece):
        rows = line.at(piece)

        def run(start, size):
            tiles.need(piece, start)
            at = pl.ds(start, size)
            result = matmul(flat_rows(sources[0], rows), weight[at, :width], cols_cols)
            for number in range(1, len(sources)):
                result = result + matmul(
                    flat_rows(sources[number], rows),
                    weight[at, number * width : (number + 1) * width],
                    cols_cols,
                )
            put_rows(line.shares, rows, at, result)

        each_tile(line.shares.shape[2], 256, run)

    return term


def add_and_norm(line, before, gain, shift, after):
    def finish(piece):
        def rows(at, total):
            hidden = before[at, :].astype(F32) + total
            after[at, :] = hidden
            scaled, _ = norm_rows(hidden)
            line.held[line.place, at, :] = (scaled * gain[...] + shift[...]).astype(BF16)

        line.own_rows(piece, rows)

    return finish


def norm_backward(line, grad, hidden, gain, out, gain_sum, shift_sum):
    gain_sum[...] = jnp.zeros_like(gain_sum)
    shift_sum[...] = jnp.zeros_like(shift_sum)

    def finish(piece):
        def rows(at, grad_normed):
            scaled, inverse = norm_rows(hidden[at, :].astype(F32))
            weighted = grad_normed * gain[...]
            first = jnp.mean(weighted, axis=-1, keepdims=True)
            second = jnp.mean(weighted * scaled, axis=-1, keepdims=True)
            result = grad[at, :].astype(F32) + inverse * (weighted - first - scaled * second)
            out[at, :] = result
            if line.held is not None:
                line.held[line.place, at, :] = result.astype(BF16)
            gain_sum[...] += jnp.sum(grad_normed * scaled, axis=0, keepdims=True)
            shift_sum[...] += jnp.sum(grad_normed, axis=0, keepdims=True)

        line.own_rows(piece, rows)

    return finish


def split(refs, *sizes):
    parts, start = [], 0
    for size in sizes:
        parts.append(refs[start : start + size])
        start += size
    return parts


def first_kernel(count, pieces, size, *refs):
    (own, gain, shift, share, bias, *tables), outs, gather, rest = split(refs, 8, 3, 3, 6)
    rows_out, mixed_out, weight_out = outs
    weight_held, mixed, load_sem, save_sem, weight_send, weight_recv = rest
    line = Line(count, pieces, None, None, None, None, None, *gather)
    weight = Whole(weight_held, size, weight_send, weight_recv)
    load = pltpu.make_async_copy(share, weight_held.at[weight.rows(0)], load_sem.at[0])
    keep = pltpu.make_async_copy(weight_held, weight_out, load_sem.at[1])
    load.start()
    line_barrier(line.place, count, weight.peers())
    saves = Saves([(line.held, rows_out), (mixed, mixed_out)], save_sem, line)
    compute = query_key_value(line, weight_held, bias, tables, mixed)
    load.wait()
    weight.start()

    def finish(piece):
        first_row = pl.multiple_of(piece * line.rows, line.rows)

        def rows(start, size):
            at = pl.ds(pl.multiple_of(first_row + start, size), size)
            scaled, _ = norm_rows(own[at, :].astype(F32))
            line.held[line.place, at, :] = (scaled * gain[...] + shift[...]).astype(BF16)

        line.chunks(rows)

    def each_tick(number):
        @pl.when(number == count - 1)
        def _():
            weight.pass_on()

    def process(piece):
        @pl.when(piece == 0)
        def _():
            weight.wait()
            keep.start()

        compute(piece)
        saves.start(piece)

    line.run(None, finish, process, each_tick, 2)
    line.drain()
    weight.drain()
    keep.wait()
    saves.wait()


def first(count, own, gain, shift, share, bias, tables, width):
    rows, depth = own.shape
    pieces = pieces_of(rows)
    size = lax.axis_size("dp")
    return line_call(
        functools.partial(first_kernel, count, pieces, size),
        (
            jax.ShapeDtypeStruct((count, rows, depth), BF16),
            jax.ShapeDtypeStruct((3, count, rows, width), BF16),
            jax.ShapeDtypeStruct((depth, 3 * width), BF16),
        ),
        (hbm, hbm, hbm),
        [vmem, vmem, vmem, hbm, vmem, vmem, vmem, vmem],
        gather_scratch(count, pieces, rows, depth)
        + [
            pltpu.VMEM((depth, 3 * width), BF16),
            pltpu.VMEM((3, count, rows, width), BF16),
            pltpu.SemaphoreType.DMA((2,)),
            pltpu.SemaphoreType.DMA((2, pieces)),
            pltpu.SemaphoreType.DMA((size,)),
            pltpu.SemaphoreType.DMA((size,)),
        ],
        0,
        6 * count * rows * depth * width,
        depth * width * 6 + own.size * 2 * count * 4,
    )(own, gain, shift, share, bias, *tables)


def middle_kernel(count, pieces, lag, *refs):
    ins, outs, scatter, gather, rest = split(refs, 6, 5, 5, 3, 10)
    source, w_out, before, gain, shift, w_up = ins
    after, rows_out, act_out, slope_out, silu_out = outs
    source_held, out_held, up_held, act, slope, silu, load_sem, tile_sem, save_sem, turn = rest
    line = Line(count, pieces, *scatter, *gather)
    loads = Loads([(source, source_held), (w_up, up_held)], load_sem)
    member = lax.axis_index("dp")
    core = member % 2
    partner = member + 1 - 2 * core
    tiles = Tiles(w_out, out_held, 1, tile_sem)
    line_barrier(line.place, count, (partner,) if lag else ())
    saves = Saves(
        [(line.held, rows_out), (act, act_out), (slope, slope_out), (silu, silu_out)], save_sem, line
    )
    compute = gate_and_up(line, up_held, act, slope, silu)

    def process(piece):
        @pl.when(piece == 0)
        def _():
            loads.wait(1)

        compute(piece)
        saves.start(piece)

    def signal(number):
        @pl.when((core == 0) & (number == lag))
        def _():
            pl.semaphore_signal(turn, inc=1, device_id={"dp": partner}, device_id_type=MESH)

    loads.wait(0)
    if lag:

        @pl.when(core == 1)
        def _():
            pl.semaphore_wait(turn, 1)

    line.run(
        share_of(line, source_held, out_held, tiles),
        add_and_norm(line, before, gain, shift, after),
        process,
        signal if lag else None,
    )
    line.drain()
    saves.wait()


def middle(count, source, w_out, before, gain, shift, w_up, lag=0):
    rows, depth = before.shape
    pieces = pieces_of(rows)
    width = w_up.shape[1] // 2
    wide = jax.ShapeDtypeStruct((count, rows, width), BF16)
    return line_call(
        functools.partial(middle_kernel, count, pieces, lag),
        (
            jax.ShapeDtypeStruct((rows, depth), F32),
            jax.ShapeDtypeStruct((count, rows, depth), BF16),
            wide,
            wide,
            wide,
        ),
        (vmem, hbm, hbm, hbm, hbm),
        [hbm, hbm, vmem, vmem, vmem, hbm],
        scatter_scratch(count, pieces, rows, depth)
        + gather_scratch(count, pieces, rows, depth)
        + [
            pltpu.VMEM(source.shape, BF16),
            pltpu.VMEM(w_out.shape, BF16),
            pltpu.VMEM(w_up.shape, BF16),
            pltpu.VMEM(wide.shape, BF16),
            pltpu.VMEM(wide.shape, BF16),
            pltpu.VMEM(wide.shape, BF16),
            pltpu.SemaphoreType.DMA((2,)),
            pltpu.SemaphoreType.DMA((max(1, depth // 256),)),
            pltpu.SemaphoreType.DMA((4, pieces)),
            pltpu.SemaphoreType.REGULAR,
        ],
        7 if lag else 1,
        2 * count * rows * (w_out.size + w_up.size),
        (w_out.size + w_up.size) * 2 + before.size * 60,
    )(source, w_out, before, gain, shift, w_up)


def between_kernel(count, pieces, *refs):
    ins, outs, scatter, gather, rest = split(refs, 10, 3, 5, 3, 7)
    source, w_down, before, gain, shift, weight, bias, *tables = ins
    after, rows_out, mixed_out = outs
    source_held, down_held, weight_held, mixed, load_sem, tile_sem, save_sem = rest
    line = Line(count, pieces, *scatter, *gather)
    loads = Loads([(source, source_held), (weight, weight_held)], load_sem)
    tiles = Tiles(w_down, down_held, 1, tile_sem)
    line_barrier(line.place, count)
    saves = Saves([(line.held, rows_out), (mixed, mixed_out)], save_sem, line)
    compute = query_key_value(line, weight_held, bias, tables, mixed)

    def process(piece):
        @pl.when(piece == 0)
        def _():
            loads.wait(1)

        compute(piece)
        saves.start(piece)

    loads.wait(0)
    line.run(
        share_of(line, source_held, down_held, tiles), add_and_norm(line, before, gain, shift, after), process
    )
    line.drain()
    saves.wait()


def between(count, source, w_down, before, gain, shift, weight, bias, tables):
    rows, depth = before.shape
    pieces = pieces_of(rows)
    mixed = (3, count, rows, weight.shape[1] // 3)
    return line_call(
        functools.partial(between_kernel, count, pieces),
        (
            jax.ShapeDtypeStruct((rows, depth), F32),
            jax.ShapeDtypeStruct((count, rows, depth), BF16),
            jax.ShapeDtypeStruct(mixed, BF16),
        ),
        (vmem, hbm, hbm),
        [hbm, hbm, vmem, vmem, vmem, hbm, vmem, vmem, vmem, vmem],
        scatter_scratch(count, pieces, rows, depth)
        + gather_scratch(count, pieces, rows, depth)
        + [
            pltpu.VMEM(source.shape, BF16),
            pltpu.VMEM(w_down.shape, BF16),
            pltpu.VMEM(weight.shape, BF16),
            pltpu.VMEM(mixed, BF16),
            pltpu.SemaphoreType.DMA((2,)),
            pltpu.SemaphoreType.DMA((max(1, depth // 256),)),
            pltpu.SemaphoreType.DMA((2, pieces)),
        ],
        2,
        2 * count * rows * (w_down.size + weight.size),
        (w_down.size + weight.size) * 2 + before.size * 60,
    )(source, w_down, before, gain, shift, weight, bias, *tables)


def turn_kernel(count, pieces, *refs):
    ins, outs, scatter, gather, rest = split(refs, 6, 3, 5, 3, 8)
    source, w_down, before, own, slope_in, silu_in = ins
    after, rows_out, wide_out = outs
    source_held, down_held, slope, silu, wide, load_sem, tile_sem, save_sem = rest
    line = Line(count, pieces, *scatter, *gather)
    loads = Loads(
        [(source, source_held), (slope_in, slope), (silu_in, silu)], load_sem
    )
    tiles = Tiles(w_down, down_held, 1, tile_sem)
    line_barrier(line.place, count)
    saves = Saves([(line.held, rows_out), (wide, wide_out)], save_sem, line)
    compute = grad_gate_and_up(line, down_held, slope, silu, wide)

    def finish(piece):
        def rows(at, total):
            after[at, :] = (before[at, :] + total).astype(BF16)
            line.held[line.place, at, :] = own[at, :]

        line.own_rows(piece, rows)

    def process(piece):
        @pl.when(piece == 0)
        def _():
            loads.wait(1, 2)

        compute(piece)
        saves.start(piece)

    loads.wait(0)
    line.run(share_of(line, source_held, down_held, tiles), finish, process)
    line.drain()
    saves.wait()


def turn(count, source, w_down, before, own, slope, silu):
    rows, depth = before.shape
    pieces = pieces_of(rows)
    width = w_down.shape[0]
    return line_call(
        functools.partial(turn_kernel, count, pieces),
        (
            jax.ShapeDtypeStruct((rows, depth), BF16),
            jax.ShapeDtypeStruct((count, rows, depth), BF16),
            jax.ShapeDtypeStruct((count, rows, 2 * width), BF16),
        ),
        (vmem, hbm, hbm),
        [hbm, hbm, vmem, vmem, hbm, hbm],
        scatter_scratch(count, pieces, rows, depth)
        + gather_scratch(count, pieces, rows, depth)
        + [
            pltpu.VMEM(source.shape, BF16),
            pltpu.VMEM(w_down.shape, BF16),
            pltpu.VMEM(slope.shape, BF16),
            pltpu.VMEM(silu.shape, BF16),
            pltpu.VMEM((count, rows, 2 * width), BF16),
            pltpu.SemaphoreType.DMA((3,)),
            pltpu.SemaphoreType.DMA((max(1, depth // 256),)),
            pltpu.SemaphoreType.DMA((2, pieces)),
        ],
        3,
        4 * count * rows * w_down.size,
        w_down.size * 2 + before.size * 60,
    )(source, w_down, before, own, slope, silu)


def middle_back_kernel(count, pieces, *refs):
    ins, outs, scatter, gather, rest = split(refs, 6, 5, 5, 3, 7)
    source, w_up, grad, hidden, gain, w_out = ins
    out, gain_sum, shift_sum, rows_out, result_out = outs
    source_held, up_held, out_held, result, load_sem, tile_sem, save_sem = rest
    line = Line(count, pieces, *scatter, *gather)
    loads = Loads([(source, source_held), (w_out, out_held)], load_sem)
    tiles = Tiles(w_up, up_held, 0, tile_sem)
    line_barrier(line.place, count)
    saves = Saves([(line.held, rows_out), (result, result_out)], save_sem, line)
    compute = through_transposed(line, out_held, result)

    def process(piece):
        @pl.when(piece == 0)
        def _():
            loads.wait(1)

        compute(piece)
        saves.start(piece)

    loads.wait(0)
    line.run(
        share_transposed(line, [source_held], up_held, tiles),
        norm_backward(line, grad, hidden, gain, out, gain_sum, shift_sum),
        process,
    )
    line.drain()
    saves.wait()


def middle_back(count, source, w_up, grad, hidden, gain, w_out):
    rows, depth = grad.shape
    pieces = pieces_of(rows)
    width = w_out.shape[0]
    return line_call(
        functools.partial(middle_back_kernel, count, pieces),
        (
            jax.ShapeDtypeStruct((rows, depth), F32),
            jax.ShapeDtypeStruct((1, depth), F32),
            jax.ShapeDtypeStruct((1, depth), F32),
            jax.ShapeDtypeStruct((count, rows, depth), BF16),
            jax.ShapeDtypeStruct((count, rows, width), BF16),
        ),
        (vmem, vmem, vmem, hbm, hbm),
        [hbm, hbm, vmem, vmem, vmem, hbm],
        scatter_scratch(count, pieces, rows, depth)
        + gather_scratch(count, pieces, rows, depth)
        + [
            pltpu.VMEM(source.shape, BF16),
            pltpu.VMEM(w_up.shape, BF16),
            pltpu.VMEM(w_out.shape, BF16),
            pltpu.VMEM((count, rows, width), BF16),
            pltpu.SemaphoreType.DMA((2,)),
            pltpu.SemaphoreType.DMA((max(1, depth // 256),)),
            pltpu.SemaphoreType.DMA((2, pieces)),
        ],
        4 if grad.dtype == F32 else 8,
        2 * count * rows * (w_up.size + w_out.size),
        (w_up.size + w_out.size) * 2 + grad.size * 60,
    )(source, w_up, grad, hidden, gain, w_out)


def between_back_kernel(count, pieces, *refs):
    ins, outs, scatter, gather, rest = split(refs, 8, 5, 5, 3, 9)
    source, weight, grad, hidden, gain, w_down, slope_in, silu_in = ins
    out, gain_sum, shift_sum, rows_out, wide_out = outs
    source_held, weight_held, down_held, slope, silu, wide, load_sem, tile_sem, save_sem = rest
    line = Line(count, pieces, *scatter, *gather)
    loads = Loads(
        [
            (source, source_held),
            (w_down, down_held),
            (slope_in, slope),
            (silu_in, silu),
        ],
        load_sem,
    )
    tiles = Tiles(weight, weight_held, 0, tile_sem)
    line_barrier(line.place, count)
    saves = Saves([(line.held, rows_out), (wide, wide_out)], save_sem, line)
    compute = grad_gate_and_up(line, down_held, slope, silu, wide)

    def process(piece):
        @pl.when(piece == 0)
        def _():
            loads.wait(1, 2, 3)

        compute(piece)
        saves.start(piece)

    loads.wait(0)
    line.run(
        share_transposed(line, [source_held.at[kind] for kind in range(3)], weight_held, tiles),
        norm_backward(line, grad, hidden, gain, out, gain_sum, shift_sum),
        process,
    )
    line.drain()
    saves.wait()


def between_back(count, source, weight, grad, hidden, gain, w_down, slope, silu):
    rows, depth = grad.shape
    pieces = pieces_of(rows)
    width = w_down.shape[0]
    return line_call(
        functools.partial(between_back_kernel, count, pieces),
        (
            jax.ShapeDtypeStruct((rows, depth), F32),
            jax.ShapeDtypeStruct((1, depth), F32),
            jax.ShapeDtypeStruct((1, depth), F32),
            jax.ShapeDtypeStruct((count, rows, depth), BF16),
            jax.ShapeDtypeStruct((count, rows, 2 * width), BF16),
        ),
        (vmem, vmem, vmem, hbm, hbm),
        [hbm, hbm, vmem, vmem, vmem, hbm, hbm, hbm],
        scatter_scratch(count, pieces, rows, depth)
        + gather_scratch(count, pieces, rows, depth)
        + [
            pltpu.VMEM(source.shape, BF16),
            pltpu.VMEM(weight.shape, BF16),
            pltpu.VMEM(w_down.shape, BF16),
            pltpu.VMEM(slope.shape, BF16),
            pltpu.VMEM(silu.shape, BF16),
            pltpu.VMEM((count, rows, 2 * width), BF16),
            pltpu.SemaphoreType.DMA((4,)),
            pltpu.SemaphoreType.DMA((max(1, depth // 256),)),
            pltpu.SemaphoreType.DMA((2, pieces)),
        ],
        5,
        2 * count * rows * (w_down.size + weight.size),
        (w_down.size + weight.size) * 2 + grad.size * 60,
    )(source, weight, grad, hidden, gain, w_down, slope, silu)


def last_kernel(count, pieces, *refs):
    ins, outs, scatter, rest = split(refs, 5, 3, 5, 4)
    source, weight, grad, hidden, gain = ins
    source_held, weight_held, load_sem, tile_sem = rest
    line = Line(count, pieces, *scatter, None, None, None)
    loads = Loads([(source, source_held), ], load_sem)
    tiles = Tiles(weight, weight_held, 0, tile_sem)
    line_barrier(line.place, count)
    loads.wait(0)
    line.run(
        share_transposed(line, [source_held.at[kind] for kind in range(3)], weight_held, tiles),
        norm_backward(line, grad, hidden, gain, *outs),
        None,
    )
    line.drain()


def last(count, source, weight, grad, hidden, gain):
    rows, depth = grad.shape
    pieces = pieces_of(rows)
    return line_call(
        functools.partial(last_kernel, count, pieces),
        (
            jax.ShapeDtypeStruct((rows, depth), F32),
            jax.ShapeDtypeStruct((1, depth), F32),
            jax.ShapeDtypeStruct((1, depth), F32),
        ),
        (vmem, vmem, vmem),
        [hbm, hbm, vmem, vmem, vmem],
        scatter_scratch(count, pieces, rows, depth)
        + [
            pltpu.VMEM(source.shape, BF16),
            pltpu.VMEM(weight.shape, BF16),
            pltpu.SemaphoreType.DMA((1,)),
            pltpu.SemaphoreType.DMA((max(1, depth // 256),)),
        ],
        6,
        2 * count * rows * weight.size,
        weight.size * 2 + grad.size * 20,
    )(source, weight, grad, hidden, gain)


def usable(first, start, keys, queries):
    key_index = lax.broadcasted_iota(jnp.int32, (keys, queries), 0)
    query_index = start + lax.broadcasted_iota(jnp.int32, (keys, queries), 1)
    return (key_index >= first) & (key_index <= query_index)


def head_lanes(values, head):
    lane = lax.broadcasted_iota(jnp.int32, values.shape, 1)
    return jnp.where((lane // HD) == head, values, jnp.zeros_like(values))


def attend_kernel(block, positions, queries, keys, values, attended, logsums):
    length = keys.shape[0]
    values_across = jnp.transpose(values[...])
    for start in range(0, length, block):
        seen = start + block
        at = slice(start, seen)
        own = queries[at, :]
        index = start + lax.broadcasted_iota(jnp.int32, (1, block), 1)
        allowed = usable(index - positions[:, at], start, seen, block)
        halves = []
        for head in range(2):
            scores = matmul(keys[:seen, :], head_lanes(own, head), cols_cols)
            scores = jnp.where(allowed, scores, masked_score)
            highest = jnp.max(scores, axis=0, keepdims=True)
            weights = jnp.exp(scores - highest)
            sums = jnp.sum(weights, axis=0, keepdims=True)
            result = matmul(values_across[:, :seen], weights.astype(BF16))
            halves.append(result[head * HD : (head + 1) * HD, :] / sums)
            logsums[head : head + 1, at] = highest + jnp.log(sums)
        attended[at, :] = jnp.transpose(jnp.concatenate(halves, axis=0)).astype(BF16)


def pair_spec(length, kind):
    return pl.BlockSpec((None, length, PAIR), lambda pair: (kind, 0, pair))


def attend(mixed, positions):
    _, length, width = mixed.shape
    pairs = width // PAIR
    block = min(256, length)
    return pl.pallas_call(
        functools.partial(attend_kernel, block),
        grid=(pairs,),
        out_shape=(
            jax.ShapeDtypeStruct((length, width), BF16),
            jax.ShapeDtypeStruct((pairs, 2, length), F32),
        ),
        in_specs=[
            pl.BlockSpec((1, length), lambda pair: (0, 0)),
            pair_spec(length, 0),
            pair_spec(length, 1),
            pair_spec(length, 2),
        ],
        out_specs=(
            pl.BlockSpec((length, PAIR), lambda pair: (0, pair)),
            pl.BlockSpec((None, 2, length), lambda pair: (pair, 0, 0)),
        ),
        compiler_params=pltpu.CompilerParams(vmem_limit_bytes=VMEM_LIMIT),
        cost_estimate=pl.CostEstimate(
            flops=8 * length * length * width,
            bytes_accessed=8 * length * width,
            transcendentals=length * length * width // HD,
        ),
    )(positions, mixed, mixed, mixed)


def unrotate(values, cos, sin_up, sin_down):
    return (
        values * cos
        - pltpu.roll(values, PAIR - ROT // 2, 1) * sin_up
        - pltpu.roll(values, ROT // 2, 1) * sin_down
    )


def attend_back_kernel(
    block, positions, queries, keys, values, attended, grad_attended, logsums,
    cos, sin_up, sin_down, grad_mixed, bias_sum, grad_keys, grad_values,
):
    length = keys.shape[0]
    keys_across = jnp.transpose(keys[...])
    grad_keys[...] = jnp.zeros_like(grad_keys)
    grad_values[...] = jnp.zeros_like(grad_values)
    bias_sum[...] = jnp.zeros_like(bias_sum)
    for start in range(0, length, block):
        seen = start + block
        at = slice(start, seen)
        own = queries[at, :]
        grad_own = grad_attended[at, :]
        inner = jnp.transpose(grad_own.astype(F32) * attended[at, :].astype(F32))
        index = start + lax.broadcasted_iota(jnp.int32, (1, block), 1)
        allowed = usable(index - positions[:, at], start, seen, block)
        halves = []
        for head in range(2):
            own_head = head_lanes(own, head)
            grad_head = head_lanes(grad_own, head)
            scores = matmul(keys[:seen, :], own_head, cols_cols)
            weights = jnp.where(allowed, jnp.exp(scores - logsums[head : head + 1, at]), 0.0)
            grad_weights = matmul(values[:seen, :], grad_head, cols_cols)
            row_inner = jnp.sum(inner[head * HD : (head + 1) * HD, :], axis=0, keepdims=True)
            grad_scores = (weights * (grad_weights - row_inner)).astype(BF16)
            grad_values[:seen, :] += matmul(weights.astype(BF16), grad_head)
            grad_keys[:seen, :] += matmul(grad_scores, own_head)
            result = matmul(keys_across[:, :seen], grad_scores)
            halves.append(result[head * HD : (head + 1) * HD, :])
        grad_own_queries = jnp.transpose(jnp.concatenate(halves, axis=0)) * (1.0 / math.sqrt(HD))
        low = unrotate(grad_own_queries, cos[at, :], sin_up[at, :], sin_down[at, :]).astype(BF16)
        grad_mixed[0, at, :] = low
        bias_sum[0:1, :] += jnp.sum(low.astype(F32), axis=0, keepdims=True)
    for start in range(0, length, block):
        at = slice(start, start + block)
        low = unrotate(grad_keys[at, :], cos[at, :], sin_up[at, :], sin_down[at, :]).astype(BF16)
        grad_mixed[1, at, :] = low
        bias_sum[1:2, :] += jnp.sum(low.astype(F32), axis=0, keepdims=True)
        low = grad_values[at, :].astype(BF16)
        grad_mixed[2, at, :] = low
        bias_sum[2:3, :] += jnp.sum(low.astype(F32), axis=0, keepdims=True)


def attend_backward(mixed, positions, attended, grad_attended, logsums, tables):
    _, length, width = mixed.shape
    pairs = width // PAIR
    block = min(256, length)
    across = pl.BlockSpec((length, PAIR), lambda pair: (0, pair))
    table = pl.BlockSpec((length, PAIR), lambda pair: (0, 0))
    return pl.pallas_call(
        functools.partial(attend_back_kernel, block),
        grid=(pairs,),
        out_shape=(
            jax.ShapeDtypeStruct((3, length, width), BF16),
            jax.ShapeDtypeStruct((3, width), F32),
        ),
        in_specs=[
            pl.BlockSpec((1, length), lambda pair: (0, 0)),
            pair_spec(length, 0),
            pair_spec(length, 1),
            pair_spec(length, 2),
            across,
            across,
            pl.BlockSpec((None, 2, length), lambda pair: (pair, 0, 0)),
            table,
            table,
            table,
        ],
        out_specs=(
            pl.BlockSpec((3, length, PAIR), lambda pair: (0, 0, pair)),
            pl.BlockSpec((3, PAIR), lambda pair: (0, pair)),
        ),
        scratch_shapes=[pltpu.VMEM((length, PAIR), F32), pltpu.VMEM((length, PAIR), F32)],
        compiler_params=pltpu.CompilerParams(vmem_limit_bytes=VMEM_LIMIT),
        cost_estimate=pl.CostEstimate(
            flops=20 * length * length * width,
            bytes_accessed=16 * length * width,
            transcendentals=length * length * width // HD,
        ),
    )(positions, mixed, mixed, mixed, attended, grad_attended, logsums, *tables)


def weight_grad_kernel(groups, tile, *refs):
    ins, (out,), rest = split(refs, 2 * groups, 1, 2 * groups + 6)
    held, (across, stages, tail, load_sem, out_sem, tail_sem) = split(rest, 2 * groups, 6)
    loads = Loads(list(zip(ins, held)), load_sem)
    depth, length = across.shape
    chunk = min(1024, depth)

    def save(slot, column):
        return pltpu.make_async_copy(
            stages.at[slot], out.at[:, pl.ds(pl.multiple_of(column, 128), tile)], out_sem.at[slot]
        )

    column, done = 0, 0
    for group in range(groups):
        left, right = held[2 * group], held[2 * group + 1]
        loads.wait(2 * group)

        def turn_over(number, carry, left=left):
            at = pl.ds(pl.multiple_of(number * 256, 256), 256)
            across[at, :] = jnp.transpose(left[:, at])
            return carry

        lax.fori_loop(0, depth // 256, turn_over, 0)
        loads.wait(2 * group + 1)
        kinds, _, width = right.shape
        full, short = width // tile, width % tile
        for kind in range(kinds):

            def fill(target, start, size, kind=kind, right=right):
                def rows(number, carry):
                    at = pl.ds(pl.multiple_of(number * chunk, chunk), chunk)
                    target[at, :] = matmul(across[at, :], right[kind, :, pl.ds(start, size)]).astype(BF16)
                    return carry

                lax.fori_loop(0, depth // chunk, rows, 0)

            def one(number, carry, fill=fill, column=column, done=done):
                slot = (done + number) % 2

                @pl.when(done + number >= 2)
                def _():
                    save(slot, 0).wait()

                start = pl.multiple_of(number * tile, tile)
                fill(stages.at[slot], start, tile)
                save(slot, column + start).start()
                return carry

            lax.fori_loop(0, full, one, 0)
            done += full
            if short:
                fill(tail, full * tile, short)
                copy = pltpu.make_async_copy(
                    tail, out.at[:, column + full * tile : column + width], tail_sem
                )
                copy.start()
                copy.wait()
            column += width
    for slot in range(min(2, done)):
        save(slot, 0).wait()


def weight_grad(*pairs):
    length, depth = pairs[0][0].shape
    total = sum(right.shape[0] * right.shape[2] for _, right in pairs)
    tile = min(256, *(right.shape[2] for _, right in pairs))
    short = max(right.shape[2] % tile for _, right in pairs)
    arrays = [array for pair in pairs for array in pair]
    return pl.pallas_call(
        functools.partial(weight_grad_kernel, len(pairs), tile),
        out_shape=jax.ShapeDtypeStruct((depth, total), BF16),
        in_specs=[hbm] * len(arrays),
        out_specs=hbm,
        scratch_shapes=[pltpu.VMEM(array.shape, BF16) for array in arrays]
        + [
            pltpu.VMEM((depth, length), BF16),
            pltpu.VMEM((2, depth, tile), BF16),
            pltpu.VMEM((depth, short or 128), BF16),
            pltpu.SemaphoreType.DMA((len(arrays),)),
            pltpu.SemaphoreType.DMA((2,)),
            pltpu.SemaphoreType.DMA,
        ],
        compiler_params=pltpu.CompilerParams(vmem_limit_bytes=VMEM_LIMIT),
        cost_estimate=pl.CostEstimate(
            flops=2 * length * depth * total, bytes_accessed=4 * depth * total, transcendentals=0
        ),
    )(*arrays)


def rotary_tables(positions):
    half_rot = ROT // 2
    lane = jnp.arange(PAIR, dtype=jnp.int32) % HD
    frequency = jnp.exp(-((lane % half_rot).astype(F32) * 2.0 / ROT) * theta_log)
    angles = positions.astype(F32)[:, None] * frequency[None, :]
    cos, sin = jnp.cos(angles), jnp.sin(angles)
    return (
        jnp.where(lane < ROT, cos, 1.0),
        jnp.where(lane < half_rot, -sin, 0.0),
        jnp.where((lane >= half_rot) & (lane < ROT), sin, 0.0),
    )


def all_sum(values, axes, beside):
    beside, made = list(beside), []
    for axis in axes:
        size = lax.axis_size(axis)
        if size & (size - 1):
            values = lax.psum(values, axis)
            continue
        step = 1
        while step < size:
            moved = lax.ppermute(values, axis, [(i, i ^ step) for i in range(size)])
            if beside:
                moved, array = lax.optimization_barrier((moved, beside.pop(0)))
                made.append(array)
            values = values + moved
            step *= 2
    return values, made + beside


def owner_sum(part, axis):
    return lax.psum_scatter(part, "dp", scatter_dimension=axis, tiled=True)


def after(values, *others):
    return lax.optimization_barrier((values, *others))


def per_device(
    tokens, positions, norm_gain, norm_bias, w_qkv, b_qkv, w_out, w_gate_up, w_down, cotangent
):
    count = lax.axis_size("tensor")
    tensor_rank = lax.axis_index("tensor")
    width = w_qkv.shape[3]
    ff_local = w_gate_up.shape[3]
    rows, depth = tokens.shape
    length = positions.shape[0]
    tables = rotary_tables(positions)
    positions_row = positions.reshape(1, length)

    def whole(weight, axis):
        return lax.all_gather(weight, "dp", axis=axis, tiled=True)

    flat = [
        [
            w_qkv[layer].reshape(-1, 3 * width),
            w_out[layer],
            w_gate_up[layer].reshape(-1, 2 * ff_local),
            w_down[layer],
        ]
        for layer in range(LAYERS)
    ]
    axes = (0, 1, 0, 1)
    gathered = [[None, whole(flat[0][1], axes[1]), whole(flat[0][2], axes[2]), None]]
    hidden = tokens
    block_tables = tuple(table.reshape(count, rows, -1) for table in tables)
    biases = [
        lax.dynamic_slice_in_dim(b_qkv[layer], tensor_rank * width, width, 1).reshape(1, 3 * width)
        for layer in range(LAYERS)
    ]
    rows_a, mixed, gathered[0][0] = first(
        count, tokens, norm_gain[0, 0:1], norm_bias[0, 0:1], flat[0][0], biases[0], block_tables, width
    )
    mixed, flat[0][3] = after(mixed, flat[0][3])
    gathered[0][3] = whole(flat[0][3], axes[3])
    kept = []
    for layer in range(LAYERS):
        mixed = mixed.reshape(3, length, width)
        attended, logsums = attend(mixed, positions_row)
        if layer + 1 < LAYERS:
            attended, *flat[layer + 1] = after(attended, *flat[layer + 1])
            gathered.append([whole(flat[layer + 1][kind], axes[kind]) for kind in range(4)])
        full_qkv, full_out, full_gu, full_down = gathered[layer]
        hidden_mid, rows_b, act, slope, silu = middle(
            count,
            attended.reshape(count, rows, width),
            full_out,
            hidden,
            norm_gain[layer, 1:2],
            norm_bias[layer, 1:2],
            full_gu,
            LAG if layer == 0 else 0,
        )
        kept.append((hidden, rows_a, mixed, attended, logsums, hidden_mid, rows_b, act, slope, silu))
        if layer + 1 < LAYERS:
            hidden, rows_a, mixed = between(
                count,
                act,
                full_down,
                hidden_mid,
                norm_gain[layer + 1, 0:1],
                norm_bias[layer + 1, 0:1],
                gathered[layer + 1][0],
                biases[layer + 1],
                block_tables,
            )
        else:
            activations, grad_rows_b, wide = turn(
                count, act, full_down, hidden_mid, cotangent, slope, silu
            )
    grad = cotangent
    scattered = [None] * LAYERS
    small = [None] * LAYERS
    for layer in reversed(range(LAYERS)):
        hidden, rows_a, mixed, attended, logsums, hidden_mid, rows_b, act, slope, silu = kept[layer]
        full_qkv, full_out, full_gu, full_down = gathered[layer]
        later = scattered[layer + 1] if layer + 1 < LAYERS else None
        feed_part = weight_grad(
            (rows_b.reshape(length, depth), wide.reshape(1, length, 2 * ff_local)),
            (grad_rows_b.reshape(length, depth), act.reshape(1, length, ff_local)),
        )
        wide, feed_part = after(wide, feed_part)
        feed_grad = owner_sum(feed_part, 0)
        if later:
            wide, later[1] = after(wide, later[1])
        grad, gain_b, shift_b, grad_rows_a, grad_attended = middle_back(
            count, wide, full_gu, grad, hidden_mid, norm_gain[layer, 1:2], full_out
        )
        if later:
            grad_attended, later[0] = after(grad_attended, later[0])
        grad_mixed, bias_sum = attend_backward(
            mixed, positions_row, attended, grad_attended.reshape(length, width), logsums, tables
        )
        attend_part = weight_grad(
            (rows_a.reshape(length, depth), grad_mixed),
            (grad_rows_a.reshape(length, depth), attended.reshape(1, length, width)),
        )
        grad_mixed, attend_part = after(grad_mixed, attend_part)
        attend_grad = owner_sum(attend_part, 0)
        source = grad_mixed.reshape(3, count, rows, width)
        if layer:
            below = kept[layer - 1]
            grad, gain_a, shift_a, grad_rows_b, wide = between_back(
                count,
                source,
                full_qkv,
                grad,
                hidden,
                norm_gain[layer, 0:1],
                gathered[layer - 1][3],
                below[8],
                below[9],
            )
        else:
            grad, gain_a, shift_a = last(count, source, full_qkv, grad, hidden, norm_gain[layer, 0:1])
        bias_full = lax.dynamic_update_slice(
            jnp.zeros((3, b_qkv.shape[2]), F32), bias_sum, (jnp.int32(0), tensor_rank * width)
        )
        small[layer] = jnp.concatenate([gain_a, gain_b, shift_a, shift_b, bias_full], axis=0)
        scattered[layer] = [attend_grad, feed_grad]
    cuts = (
        lambda each: each[0][:, : 3 * width].reshape(-1, 3, width),
        lambda each: each[0][:, 3 * width :].T,
        lambda each: each[1][:, : 2 * ff_local].reshape(-1, 2, ff_local),
        lambda each: each[1][:, 2 * ff_local :].T,
    )
    stacks = [jnp.stack([cut(each).astype(F32) for each in scattered]) for cut in cuts]
    sums, made = all_sum(jnp.stack(small), ("dp", "tensor"), stacks[2:] + stacks[:2])
    stacks = made[2:] + made[:2]
    return (
        activations,
        grad,
        sums[:, 0:2],
        sums[:, 2:4],
        stacks[0],
        sums[:, 4:7],
        stacks[1],
        stacks[2],
        stacks[3],
    )


def norm_parts(hidden):
    average = jnp.mean(hidden, axis=-1, keepdims=True)
    centred = hidden - average
    variance = jnp.mean(centred * centred, axis=-1, keepdims=True)
    inverse = lax.rsqrt(variance + norm_eps)
    return (centred * inverse, inverse)


def norm_back(grad_normed, scaled, inverse, norm_weight):
    weighted = grad_normed * norm_weight
    first_mean = jnp.mean(weighted, axis=-1, keepdims=True)
    second_mean = jnp.mean(weighted * scaled, axis=-1, keepdims=True)
    grad_input = inverse * (weighted - first_mean - scaled * second_mean)
    return (grad_input, jnp.sum(grad_normed * scaled, axis=0), jnp.sum(grad_normed, axis=0))


def plain_tables(positions):
    half_rot = ROT // 2
    frequency = jnp.exp(-(jnp.arange(half_rot, dtype=jnp.float32) * 2.0 / ROT) * theta_log)
    angles = positions.astype(jnp.float32)[:, None] * frequency[None, :]
    return (jnp.cos(angles)[:, None, :], jnp.sin(angles)[:, None, :])


def rotate(values, cos_table, sin_table):
    half_rot = ROT // 2
    first_half = values[..., :half_rot]
    second_half = values[..., half_rot:ROT]
    return jnp.concatenate(
        [
            first_half * cos_table - second_half * sin_table,
            second_half * cos_table + first_half * sin_table,
            values[..., ROT:],
        ],
        axis=-1,
    )


def inner_rows(left, right):
    return lax.dot_general(left, right, rows_rows, preferred_element_type=jnp.float32)


def inner_cols(left, right):
    return lax.dot_general(left, right, cols_cols, preferred_element_type=jnp.float32)


def block_scores(queries, key_rows, positions, number, block_rows, score_scale):
    seq_len = key_rows.shape[0]
    row_start = number * block_rows
    query_block = lax.dynamic_slice_in_dim(queries, row_start, block_rows, 0)
    scores = (
        jnp.einsum("qhd,khd->hqk", query_block, key_rows, preferred_element_type=jnp.float32)
        * score_scale
    )
    row_index = row_start + jnp.arange(block_rows, dtype=jnp.int32)
    first_key = row_index - lax.dynamic_slice_in_dim(positions, row_start, block_rows, 0)
    columns = jnp.arange(seq_len, dtype=jnp.int32)
    allowed = (columns[None, :] <= row_index[:, None]) & (columns[None, :] >= first_key[:, None])
    return (query_block, allowed, jnp.where(allowed[None], scores, masked_score))


def attend_forward(queries, key_rows, values, positions, score_scale):
    seq_len = queries.shape[0]
    block_rows = min(512, seq_len)

    def one_block(number):
        query_block, allowed, scores = block_scores(
            queries, key_rows, positions, number, block_rows, score_scale
        )
        row_max = jnp.max(scores, axis=-1, keepdims=True)
        shifted = jnp.exp(scores - row_max)
        row_sum = jnp.sum(shifted, axis=-1, keepdims=True)
        weights_low = (shifted / row_sum).astype(jnp.bfloat16)
        block_out = jnp.einsum(
            "hqk,khd->qhd", weights_low, values, preferred_element_type=jnp.float32
        )
        return (block_out, row_max + jnp.log(row_sum))

    block_outs, logsums = lax.map(one_block, jnp.arange(seq_len // block_rows, dtype=jnp.int32))
    return (block_outs.reshape(seq_len, -1), logsums)


def attend_back(queries, key_rows, values, positions, logsums, grad_attended, score_scale):
    seq_len = queries.shape[0]
    block_rows = min(512, seq_len)

    def one_block(totals, inputs):
        grad_keys, grad_values = totals
        number, logsum = inputs
        query_block, allowed, scores = block_scores(
            queries, key_rows, positions, number, block_rows, score_scale
        )
        softmax_rows = jnp.exp(scores - logsum)
        grad_block = lax.dynamic_slice_in_dim(grad_attended, number * block_rows, block_rows, 0)
        grad_probs = jnp.einsum(
            "qhd,khd->hqk", grad_block, values, preferred_element_type=jnp.float32
        )
        grad_values = grad_values + jnp.einsum(
            "hqk,qhd->khd",
            softmax_rows.astype(jnp.bfloat16),
            grad_block,
            preferred_element_type=jnp.float32,
        )
        row_inner = jnp.sum(softmax_rows * grad_probs, axis=-1, keepdims=True)
        grad_scores = jnp.where(allowed[None], softmax_rows * (grad_probs - row_inner), 0.0).astype(
            jnp.bfloat16
        )
        grad_query = (
            jnp.einsum("hqk,khd->qhd", grad_scores, key_rows, preferred_element_type=jnp.float32)
            * score_scale
        )
        grad_keys = (
            grad_keys
            + jnp.einsum(
                "hqk,qhd->khd", grad_scores, query_block, preferred_element_type=jnp.float32
            )
            * score_scale
        )
        return ((grad_keys, grad_values), grad_query)

    empty_grad = jnp.zeros(key_rows.shape, jnp.float32)
    numbers = jnp.arange(seq_len // block_rows, dtype=jnp.int32)
    (grad_keys, grad_values), grad_queries = lax.scan(
        one_block, (empty_grad, empty_grad), (numbers, logsums)
    )
    return (grad_queries.reshape(queries.shape), grad_keys, grad_values)


def per_device_plain(
    tokens, positions, norm_gain, norm_bias, w_qkv, b_qkv, w_out, w_gate_up, w_down, cotangent
):
    tensor_rank = lax.axis_index("tensor")
    width_local = w_qkv.shape[3]
    heads_local = width_local // HD
    ff_local = w_gate_up.shape[3]
    local_rows = tokens.shape[0]
    seq_len = positions.shape[0]
    score_scale = 1.0 / math.sqrt(HD)
    cos_table, sin_table = plain_tables(positions)
    hidden = tokens.astype(jnp.float32)
    kept_state = []
    for layer_index in range(LAYERS):
        gathered = (
            lax.all_gather(w_qkv[layer_index], "dp", axis=0, tiled=True),
            lax.all_gather(w_out[layer_index], "dp", axis=1, tiled=True),
            lax.all_gather(w_gate_up[layer_index], "dp", axis=0, tiled=True),
            lax.all_gather(w_down[layer_index], "dp", axis=1, tiled=True),
        )
        full_qkv, full_out, full_gu, full_down = gathered
        scaled_a, inverse_a = norm_parts(hidden)
        normed_a = (scaled_a * norm_gain[layer_index, 0] + norm_bias[layer_index, 0]).astype(
            jnp.bfloat16
        )
        rows_a = lax.all_gather(normed_a, "tensor", axis=0, tiled=True)
        bias_local = lax.dynamic_slice_in_dim(
            b_qkv[layer_index], tensor_rank * width_local, width_local, 1
        )
        mixed = jnp.dot(
            rows_a,
            full_qkv.reshape(full_qkv.shape[0], 3 * width_local),
            preferred_element_type=jnp.float32,
        ) + bias_local.reshape(3 * width_local)
        mixed = mixed.reshape(seq_len, 3, heads_local, HD)
        queries = rotate(mixed[:, 0], cos_table, sin_table).astype(jnp.bfloat16)
        key_rows = rotate(mixed[:, 1], cos_table, sin_table).astype(jnp.bfloat16)
        values = mixed[:, 2].astype(jnp.bfloat16)
        attended, logsums = attend_forward(queries, key_rows, values, positions, score_scale)
        attended = attended.astype(jnp.bfloat16)

        def project_attn(row_start, row_count, source=attended, weight=full_out):
            return jnp.dot(source, weight, preferred_element_type=jnp.float32)

        branch_a = lax.psum_scatter(
            project_attn(jnp.int32(0), local_rows * lax.axis_size("tensor")).astype(jnp.bfloat16),
            "tensor",
            scatter_dimension=0,
            tiled=True,
        ).astype(jnp.float32)
        hidden_mid = hidden + branch_a
        scaled_b, inverse_b = norm_parts(hidden_mid)
        normed_b = (scaled_b * norm_gain[layer_index, 1] + norm_bias[layer_index, 1]).astype(
            jnp.bfloat16
        )
        rows_b = lax.all_gather(normed_b, "tensor", axis=0, tiled=True)
        gate_up = jnp.dot(
            rows_b,
            full_gu.reshape(full_gu.shape[0], 2 * ff_local),
            preferred_element_type=jnp.float32,
        ).reshape(seq_len, 2, ff_local)
        activated = (jax.nn.silu(gate_up[:, 0]) * gate_up[:, 1]).astype(jnp.bfloat16)

        def project_mlp(row_start, row_count, source=activated, weight=full_down):
            return jnp.dot(source, weight, preferred_element_type=jnp.float32)

        hidden = hidden_mid + lax.psum_scatter(
            project_mlp(jnp.int32(0), local_rows * lax.axis_size("tensor")).astype(jnp.bfloat16),
            "tensor",
            scatter_dimension=0,
            tiled=True,
        ).astype(jnp.float32)
        kept_state.append(
            (
                gathered,
                scaled_a,
                inverse_a,
                rows_a,
                queries,
                key_rows,
                values,
                logsums,
                attended,
                scaled_b,
                inverse_b,
                rows_b,
                gate_up,
                activated,
            )
        )
    activations = hidden.astype(jnp.bfloat16)
    grad = cotangent.astype(jnp.float32)
    weight_parts = [None] * LAYERS
    gain_rows = [None] * LAYERS
    shift_rows = [None] * LAYERS
    qkv_shift_rows = [None] * LAYERS
    for layer_index in reversed(range(LAYERS)):
        (
            gathered,
            scaled_a,
            inverse_a,
            rows_a,
            queries,
            key_rows,
            values,
            logsums,
            attended,
            scaled_b,
            inverse_b,
            rows_b,
            gate_up,
            activated,
        ) = kept_state[layer_index]
        full_qkv, full_out, full_gu, full_down = (
            lax.all_gather(w_qkv[layer_index], "dp", axis=0, tiled=True),
            lax.all_gather(w_out[layer_index], "dp", axis=1, tiled=True),
            lax.all_gather(w_gate_up[layer_index], "dp", axis=0, tiled=True),
            lax.all_gather(w_down[layer_index], "dp", axis=1, tiled=True),
        )
        grad_rows_b = lax.all_gather(grad.astype(jnp.bfloat16), "tensor", axis=0, tiled=True)
        grad_down_weight = inner_rows(activated, grad_rows_b)
        grad_act = inner_cols(grad_rows_b, full_down)
        gate_part = gate_up[:, 0]
        up_part = gate_up[:, 1]
        sigmoid_gate = jax.nn.sigmoid(gate_part)
        grad_gate = grad_act * up_part * sigmoid_gate * (1.0 + gate_part * (1.0 - sigmoid_gate))
        grad_up = grad_act * jax.nn.silu(gate_part)
        grad_gate_up = (
            jnp.stack([grad_gate, grad_up], axis=1)
            .astype(jnp.bfloat16)
            .reshape(seq_len, 2 * ff_local)
        )
        grad_gu_weight = inner_rows(rows_b, grad_gate_up).reshape(full_gu.shape)
        flat_gu = full_gu.reshape(full_gu.shape[0], 2 * ff_local)

        def back_mlp(row_start, row_count, source=grad_gate_up, weight=flat_gu):
            return inner_cols(source, weight)

        grad_normed_b = lax.psum_scatter(
            back_mlp(jnp.int32(0), local_rows * lax.axis_size("tensor")).astype(jnp.bfloat16),
            "tensor",
            scatter_dimension=0,
            tiled=True,
        ).astype(jnp.float32)
        grad_in_b, gain_b, shift_b = norm_back(
            grad_normed_b, scaled_b, inverse_b, norm_gain[layer_index, 1]
        )
        grad = grad + grad_in_b
        grad_rows_a = lax.all_gather(grad.astype(jnp.bfloat16), "tensor", axis=0, tiled=True)
        grad_out_weight = inner_rows(attended, grad_rows_a)
        grad_attended = inner_cols(grad_rows_a, full_out).astype(jnp.bfloat16)
        grad_attended = grad_attended.reshape(seq_len, heads_local, HD)
        grad_queries, grad_keys, grad_values = attend_back(
            queries, key_rows, values, positions, logsums, grad_attended, score_scale
        )
        grad_queries = rotate(grad_queries, cos_table, -sin_table)
        grad_keys = rotate(grad_keys, cos_table, -sin_table)
        grad_mixed = jnp.stack([grad_queries, grad_keys, grad_values], axis=1)
        grad_mixed = grad_mixed.reshape(seq_len, 3 * width_local).astype(jnp.bfloat16)
        qkv_shift_local = jnp.sum(grad_mixed, axis=0, dtype=jnp.float32).reshape(3, width_local)
        qkv_shift_rows[layer_index] = lax.dynamic_update_slice(
            jnp.zeros((3, b_qkv.shape[2]), jnp.float32),
            qkv_shift_local,
            (jnp.int32(0), tensor_rank * width_local),
        )
        grad_qkv_weight = inner_rows(rows_a, grad_mixed).reshape(full_qkv.shape)
        flat_qkv = full_qkv.reshape(full_qkv.shape[0], 3 * width_local)

        def back_attn(row_start, row_count, source=grad_mixed, weight=flat_qkv):
            return inner_cols(source, weight)

        grad_normed_a = lax.psum_scatter(
            back_attn(jnp.int32(0), local_rows * lax.axis_size("tensor")).astype(jnp.bfloat16),
            "tensor",
            scatter_dimension=0,
            tiled=True,
        ).astype(jnp.float32)
        grad_in_a, gain_a, shift_a = norm_back(
            grad_normed_a, scaled_a, inverse_a, norm_gain[layer_index, 0]
        )
        grad = grad + grad_in_a
        gain_rows[layer_index] = jnp.stack([gain_a, gain_b])
        shift_rows[layer_index] = jnp.stack([shift_a, shift_b])
        weight_parts[layer_index] = (
            lax.psum_scatter(
                grad_qkv_weight.astype(jnp.bfloat16), "dp", scatter_dimension=0, tiled=True
            ).astype(jnp.float32),
            lax.psum_scatter(
                grad_out_weight.astype(jnp.bfloat16), "dp", scatter_dimension=1, tiled=True
            ).astype(jnp.float32),
            lax.psum_scatter(
                grad_gu_weight.astype(jnp.bfloat16), "dp", scatter_dimension=0, tiled=True
            ).astype(jnp.float32),
            lax.psum_scatter(
                grad_down_weight.astype(jnp.bfloat16), "dp", scatter_dimension=1, tiled=True
            ).astype(jnp.float32),
        )
    stack_qkv = jnp.stack([weight_parts[number][0] for number in range(LAYERS)])
    stack_out = jnp.stack([weight_parts[number][1] for number in range(LAYERS)])
    stack_gu = jnp.stack([weight_parts[number][2] for number in range(LAYERS)])
    stack_down = jnp.stack([weight_parts[number][3] for number in range(LAYERS)])
    gain_grad, norm_bias_grad, qkv_bias_grad = lax.psum(
        (jnp.stack(gain_rows), jnp.stack(shift_rows), jnp.stack(qkv_shift_rows)), ("dp", "tensor")
    )
    return (
        activations,
        grad,
        gain_grad,
        norm_bias_grad,
        stack_qkv,
        qkv_bias_grad,
        stack_out,
        stack_gu,
        stack_down,
    )


def solution(mesh):
    in_specs = (
        P(("dp", "tensor"), None),
        P("dp"),
        P(),
        P(),
        P(None, "dp", None, "tensor"),
        P(),
        P(None, "tensor", "dp"),
        P(None, "dp", None, "tensor"),
        P(None, "tensor", "dp"),
        P(("dp", "tensor"), None),
    )
    out_specs = (
        P(("dp", "tensor"), None),
        P(("dp", "tensor"), None),
        P(),
        P(),
        P(None, "dp", None, "tensor"),
        P(),
        P(None, "tensor", "dp"),
        P(None, "dp", None, "tensor"),
        P(None, "tensor", "dp"),
    )
    def run(*operands):
        fits = operands[7].shape[3] % 128 == 0 and operands[4].shape[3] % PAIR == 0
        return (per_device if fits else per_device_plain)(*operands)

    return jax.shard_map(
        run, mesh=mesh, in_specs=in_specs, out_specs=out_specs, check_vma=False
    )
```

```python
import functools
import math

import jax
import jax.numpy as jnp
from jax import lax
from jax.experimental import pallas as pl
from jax.experimental.pallas import tpu as pltpu
from jax.sharding import PartitionSpec as P

HD = 64
ROT = 16
LAYERS = 2
PAIR = 2 * HD
MESH = pl.DeviceIdType.MESH
F32 = jnp.float32
BF16 = jnp.bfloat16
VMEM_LIMIT = 62 * 2**20
LAG = 6

norm_eps = 1e-05
theta_log = math.log(10000.0)
masked_score = -1e30
rows_rows = (((0,), (0,)), ((), ()))
cols_cols = (((1,), (1,)), ((), ()))
rows_cols = (((1,), (0,)), ((), ()))


def matmul(left, right, dims=rows_cols):
    return lax.dot_general(left, right, dims, preferred_element_type=F32)


def member_at(member, step):
    bit = 1
    while bit <= step:
        if step & bit:
            member = member + bit * (1 - 2 * ((member // bit) % 2))
        bit *= 2
    return member


class Whole:
    def __init__(self, held, size, send_sem, recv_sem):
        self.held, self.size, self.send_sem, self.recv_sem = held, size, send_sem, recv_sem
        self.member = lax.axis_index("dp")
        self.share = held.shape[0] // size
        self.evens = range(0, size, 2)

    def peers(self):
        return tuple(member_at(self.member, step) for step in self.evens if step) + (
            member_at(self.member, 1),
        )

    def rows(self, step):
        start = member_at(self.member, step) * self.share
        return pl.ds(pl.multiple_of(start, self.share), self.share)

    def hop(self, source_step, target_step, number):
        return pltpu.make_async_remote_copy(
            src_ref=self.held.at[self.rows(source_step)],
            dst_ref=self.held.at[self.rows(source_step)],
            send_sem=self.send_sem.at[number],
            recv_sem=self.recv_sem.at[number],
            device_id={"dp": member_at(self.member, target_step)},
            device_id_type=MESH,
        )

    def to_chips(self, step):
        return self.hop(0, step, step)

    def to_core(self, step):
        return self.hop(step, 1, step + 1)

    def start(self):
        for step in self.evens:
            if step:
                self.to_chips(step).start()
        self.to_core(0).start()

    def pass_on(self):
        for step in self.evens:
            if step:
                self.to_chips(step).wait_recv()
                self.to_core(step).start()

    def wait(self):
        for step in self.evens:
            self.to_core(step).wait_recv()

    def drain(self):
        for step in self.evens:
            if step:
                self.to_chips(step).wait_send()
            self.to_core(step).wait_send()


def line_barrier(place, count, others=()):
    barrier = pltpu.get_barrier_semaphore()
    for other in others:
        pl.semaphore_signal(barrier, inc=1, device_id={"dp": other}, device_id_type=MESH)

    @pl.when(place > 0)
    def _():
        pl.semaphore_signal(barrier, inc=1, device_id={"tensor": place - 1}, device_id_type=MESH)

    @pl.when(place < count - 1)
    def _():
        pl.semaphore_signal(barrier, inc=1, device_id={"tensor": place + 1}, device_id_type=MESH)

    middle = (place > 0) & (place < count - 1)

    @pl.when(middle)
    def _():
        pl.semaphore_wait(barrier, 2 + len(others))

    @pl.when(jnp.logical_not(middle))
    def _():
        pl.semaphore_wait(barrier, 1 + len(others))


def each_tile(width, tile, run):
    def one(number, carry):
        run(pl.multiple_of(number * tile, tile), tile)
        return carry

    lax.fori_loop(0, width // tile, one, 0)
    if width % tile:
        run(width // tile * tile, width % tile)


class Line:
    def __init__(self, count, pieces, shares, sending, arrived, sum_send, sum_recv, held, send_sem, recv_sem):
        self.count, self.pieces = count, pieces
        self.shares, self.sending, self.arrived = shares, sending, arrived
        self.sum_send, self.sum_recv = sum_send, sum_recv
        self.held, self.send_sem, self.recv_sem = held, send_sem, recv_sem
        self.place = lax.axis_index("tensor")
        self.rows = (held if held is not None else sending).shape[1] // pieces

    def at(self, piece):
        return pl.ds(pl.multiple_of(piece * self.rows, self.rows), self.rows)

    def sum_hop(self, piece, owner):
        right = owner > self.place
        target = jnp.where(right, self.place + 1, self.place - 1)
        slot = jnp.where(right | (owner != target), owner, self.count)
        return pltpu.make_async_remote_copy(
            src_ref=self.sending.at[owner, self.at(piece)],
            dst_ref=self.arrived.at[slot, self.at(piece)],
            send_sem=self.sum_send.at[owner, piece],
            recv_sem=self.sum_recv.at[slot, piece],
            device_id={"tensor": target},
            device_id_type=MESH,
        )

    def sum_landed(self, piece, slot):
        return pltpu.make_async_remote_copy(
            src_ref=self.sending.at[0, self.at(piece)],
            dst_ref=self.arrived.at[slot, self.at(piece)],
            send_sem=self.sum_send.at[0, piece],
            recv_sem=self.sum_recv.at[slot, piece],
            device_id={"tensor": self.place},
            device_id_type=MESH,
        )

    def row_hop(self, piece, block, right):
        return pltpu.make_async_remote_copy(
            src_ref=self.held.at[block, self.at(piece)],
            dst_ref=self.held.at[block, self.at(piece)],
            send_sem=self.send_sem.at[jnp.where(right, 0, 1), block, piece],
            recv_sem=self.recv_sem.at[block, piece],
            device_id={"tensor": jnp.where(right, self.place + 1, self.place - 1)},
            device_id_type=MESH,
        )

    def sides(self, away, run):
        def one(side, carry):
            block = jnp.where(side == 0, self.place + away, self.place - away)

            @pl.when((block >= 0) & (block < self.count))
            def _():
                run(block, side == 0)

            return carry

        lax.fori_loop(0, 2, one, 0)

    def chunks(self, run):
        chunk = min(16, self.rows)

        def one(number, carry):
            run(pl.multiple_of(number * chunk, chunk), chunk)
            return carry

        lax.fori_loop(0, self.rows // chunk, one, 0)

    def pass_on(self, piece, owner, right):
        first = pl.multiple_of(piece * self.rows, self.rows)
        onward = jnp.where(right, self.place > 0, self.place < self.count - 1)

        @pl.when(onward)
        def _():
            self.sum_landed(piece, owner).wait_recv()

            def rows(start, size):
                at = pl.ds(pl.multiple_of(first + start, size), size)
                self.sending[owner, at, :] = (
                    self.shares[owner, at, :]
                    + self.arrived[owner, at, :].astype(F32)
                ).astype(BF16)

            self.chunks(rows)

        @pl.when(jnp.logical_not(onward))
        def _():
            def rows(start, size):
                at = pl.ds(pl.multiple_of(first + start, size), size)
                self.sending[owner, at, :] = self.shares[owner, at, :].astype(BF16)

            self.chunks(rows)

        self.sum_hop(piece, owner).start()

    def collect(self, piece):
        first = pl.multiple_of(piece * self.rows, self.rows)

        def add(slot):
            self.sum_landed(piece, slot).wait_recv()

            def rows(start, size):
                at = pl.ds(pl.multiple_of(first + start, size), size)
                self.shares[self.place, at, :] = self.shares[self.place, at, :] + self.arrived[
                    slot, at, :
                ].astype(F32)

            self.chunks(rows)

        @pl.when(self.place > 0)
        def _():
            add(self.place)

        @pl.when(self.place < self.count - 1)
        def _():
            add(self.count)

    def own_rows(self, piece, run):
        first = pl.multiple_of(piece * self.rows, self.rows)

        def rows(start, size):
            at = pl.ds(pl.multiple_of(first + start, size), size)
            run(at, self.shares[self.place, at, :])

        self.chunks(rows)

    def run(self, term, finish, process, each_tick=None, delay=0):
        count, pieces, place = self.count, self.pieces, self.place
        scatter, gather = term is not None, process is not None
        lead = count - 1 if scatter else 0
        if scatter:
            term(0)

        def tick(number, carry):
            if each_tick is not None:
                each_tick(number)

            def valid(piece):
                return (piece >= 0) & (piece < pieces)

            if scatter:

                def sum_step(step, inner):
                    piece = number - step

                    @pl.when(valid(piece))
                    def _():
                        self.sides(
                            count - 1 - step,
                            lambda owner, right: self.pass_on(piece, owner, right),
                        )

                    return inner

                lax.fori_loop(0, count - 1, sum_step, 0)
            mine = number - lead

            @pl.when(valid(mine))
            def _():
                if scatter:
                    self.collect(mine)
                finish(mine)
                if gather:

                    @pl.when(place < count - 1)
                    def _():
                        self.row_hop(mine, place, True).start()

                    @pl.when(place > 0)
                    def _():
                        self.row_hop(mine, place, False).start()

            if gather:

                def row_step(step, inner):
                    piece = mine - step

                    def forward(block, right):
                        self.row_hop(piece, block, True).wait_recv()
                        onward = jnp.where(right, place > 0, place < count - 1)

                        @pl.when(onward)
                        def _():
                            self.row_hop(piece, block, jnp.logical_not(right)).start()

                    @pl.when(valid(piece))
                    def _():
                        self.sides(step, forward)

                    return inner

                lax.fori_loop(1, count, row_step, 0)
            if scatter:

                @pl.when(number + 1 < pieces)
                def _():
                    term(number + 1)

            if gather:

                @pl.when(valid(mine - (count - 1) - delay))
                def _():
                    process(mine - (count - 1) - delay)

            return carry

        lax.fori_loop(0, pieces + lead + (count - 1 + delay if gather else 0), tick, 0)

    def drain(self):
        def piece_sends(piece, carry):
            def owner_sends(owner, inner):
                if self.sending is not None:

                    @pl.when(owner != self.place)
                    def _():
                        self.sum_hop(piece, owner).wait_send()

                if self.held is not None:

                    @pl.when((owner <= self.place) & (self.place < self.count - 1))
                    def _():
                        self.row_hop(piece, owner, True).wait_send()

                    @pl.when((owner >= self.place) & (self.place > 0))
                    def _():
                        self.row_hop(piece, owner, False).wait_send()

                return inner

            lax.fori_loop(0, self.count, owner_sends, 0)
            return carry

        lax.fori_loop(0, self.pieces, piece_sends, 0)


def norm_rows(values):
    average = jnp.mean(values, axis=-1, keepdims=True)
    centred = values - average
    variance = jnp.mean(centred * centred, axis=-1, keepdims=True)
    inverse = lax.rsqrt(variance + norm_eps)
    return centred * inverse, inverse


def scatter_scratch(count, pieces, rows, width):
    return [
        pltpu.VMEM((count, rows, width), F32),
        pltpu.VMEM((count, rows, width), BF16),
        pltpu.VMEM((count + 1, rows, width), BF16),
        pltpu.SemaphoreType.DMA((count, pieces)),
        pltpu.SemaphoreType.DMA((count + 1, pieces)),
    ]


def gather_scratch(count, pieces, rows, width):
    return [
        pltpu.VMEM((count, rows, width), BF16),
        pltpu.SemaphoreType.DMA((2, count, pieces)),
        pltpu.SemaphoreType.DMA((count, pieces)),
    ]


vmem = pl.BlockSpec(memory_space=pltpu.VMEM)
hbm = pl.BlockSpec(memory_space=pl.ANY)


class Loads:
    def __init__(self, pairs, sems):
        self.copies = [
            pltpu.make_async_copy(source, target, sems.at[number])
            for number, (source, target) in enumerate(pairs)
        ]
        for copy in self.copies:
            copy.start()

    def wait(self, *numbers):
        for number in numbers:
            self.copies[number].wait()


class Tiles:
    def __init__(self, source, target, axis, sems):
        self.source, self.target, self.axis, self.sems = source, target, axis, sems
        self.size = min(256, target.shape[axis])
        for number in range(target.shape[axis] // self.size):
            self.copy(number).start()

    def copy(self, number):
        at = pl.ds(pl.multiple_of(number * self.size, self.size), self.size)
        where = (at,) if self.axis == 0 else (slice(None), at)
        return pltpu.make_async_copy(
            self.source.at[where], self.target.at[where], self.sems.at[number]
        )

    def need(self, piece, start):
        @pl.when(piece == 0)
        def _():
            self.copy(start // self.size).wait()


class Saves:
    def __init__(self, pairs, sems, line):
        self.pairs, self.sems, self.line = pairs, sems, line

    def copy(self, number, piece):
        source, target = self.pairs[number]
        rows = self.line.at(piece)
        where = (slice(None),) * (len(source.shape) - 2) + (rows,)
        return pltpu.make_async_copy(
            source.at[where], target.at[where], self.sems.at[number, piece]
        )

    def start(self, piece):
        for number in range(len(self.pairs)):
            self.copy(number, piece).start()

    def wait(self):
        for number in range(len(self.pairs)):
            for piece in range(self.line.pieces):
                self.copy(number, piece).wait()


def flat_rows(ref, rows, columns=slice(None)):
    values = ref[:, rows, columns]
    return values.reshape(values.shape[0] * values.shape[1], values.shape[2])


def put_rows(ref, rows, columns, values):
    count = ref.shape[0]
    ref[:, rows, columns] = values.reshape(count, values.shape[0] // count, values.shape[1])


def line_call(body, out_shape, out_specs, in_specs, scratch, number, flops, moved):
    return pl.pallas_call(
        body,
        out_shape=out_shape,
        in_specs=in_specs,
        out_specs=out_specs,
        scratch_shapes=scratch,
        compiler_params=pltpu.CompilerParams(
            collective_id=number, has_side_effects=True, vmem_limit_bytes=VMEM_LIMIT
        ),
        cost_estimate=pl.CostEstimate(flops=flops, bytes_accessed=moved, transcendentals=0),
    )


def pieces_of(rows):
    return 4 if rows % 64 == 0 else 1


def query_key_value(line, weight, bias, tables, mixed):
    cos, sin_up, sin_down = tables
    width = mixed.shape[3]

    def factor(table, rows, size):
        return jnp.concatenate([flat_rows(table, rows)] * (size // PAIR), axis=1)

    def process(piece):
        rows = line.at(piece)

        def columns(kind):
            def run(start, size):
                source = pl.ds(pl.multiple_of(kind * width + start, 128), size)
                result = matmul(flat_rows(line.held, rows), weight[:, source]) + bias[:, source]
                if kind < 2:
                    result = (
                        result * factor(cos, rows, size)
                        + pltpu.roll(result, size - ROT // 2, 1) * factor(sin_up, rows, size)
                        + pltpu.roll(result, ROT // 2, 1) * factor(sin_down, rows, size)
                    )
                if kind == 0:
                    result = result * (1.0 / math.sqrt(HD))
                put_rows(mixed.at[kind], rows, pl.ds(start, size), result.astype(BF16))

            return run

        for kind in range(3):
            each_tile(width, min(256, width), columns(kind))

    return process


def gate_and_up(line, weight, act, slope, silu):
    width = act.shape[2]

    def process(piece):
        rows = line.at(piece)

        def run(start, size):
            at = pl.ds(start, size)
            own = flat_rows(line.held, rows)
            gate = matmul(own, weight[:, at])
            up = matmul(own, weight[:, pl.ds(pl.multiple_of(width + start, 128), size)])
            sigmoid = jax.nn.sigmoid(gate)
            soft = gate * sigmoid
            put_rows(act, rows, at, (soft * up).astype(BF16))
            put_rows(silu, rows, at, soft.astype(BF16))
            put_rows(slope, rows, at, (up * sigmoid * (1.0 + gate * (1.0 - sigmoid))).astype(BF16))

        each_tile(width, 256, run)

    return process


def grad_gate_and_up(line, weight, slope, silu, wide):
    width = slope.shape[2]

    def process(piece):
        rows = line.at(piece)

        def run(start, size):
            at = pl.ds(start, size)
            grad_act = matmul(flat_rows(line.held, rows), weight[at, :], cols_cols)
            put_rows(wide, rows, at, (grad_act * flat_rows(slope, rows, at).astype(F32)).astype(BF16))
            put_rows(
                wide,
                rows,
                pl.ds(pl.multiple_of(width + start, 128), size),
                (grad_act * flat_rows(silu, rows, at).astype(F32)).astype(BF16),
            )

        each_tile(width, 256, run)

    return process


def through_transposed(line, weight, result):
    def process(piece):
        rows = line.at(piece)

        def run(start, size):
            at = pl.ds(start, size)
            put_rows(
                result, rows, at, matmul(flat_rows(line.held, rows), weight[at, :], cols_cols).astype(BF16)
            )

        each_tile(result.shape[2], 256, run)

    return process


def share_of(line, source, weight, tiles):
    def term(piece):
        rows = line.at(piece)

        def run(start, size):
            tiles.need(piece, start)
            at = pl.ds(start, size)
            put_rows(line.shares, rows, at, matmul(flat_rows(source, rows), weight[:, at]))

        each_tile(line.shares.shape[2], 256, run)

    return term


def share_transposed(line, sources, weight, tiles):
    width = sources[0].shape[2]

    def term(piece):
        rows = line.at(piece)

        def run(start, size):
            tiles.need(piece, start)
            at = pl.ds(start, size)
            result = matmul(flat_rows(sources[0], rows), weight[at, :width], cols_cols)
            for number in range(1, len(sources)):
                result = result + matmul(
                    flat_rows(sources[number], rows),
                    weight[at, number * width : (number + 1) * width],
                    cols_cols,
                )
            put_rows(line.shares, rows, at, result)

        each_tile(line.shares.shape[2], 256, run)

    return term


def add_and_norm(line, before, gain, shift, after):
    def finish(piece):
        def rows(at, total):
            hidden = before[at, :].astype(F32) + total
            after[at, :] = hidden
            scaled, _ = norm_rows(hidden)
            line.held[line.place, at, :] = (scaled * gain[...] + shift[...]).astype(BF16)

        line.own_rows(piece, rows)

    return finish


def norm_backward(line, grad, hidden, gain, out, gain_sum, shift_sum):
    gain_sum[...] = jnp.zeros_like(gain_sum)
    shift_sum[...] = jnp.zeros_like(shift_sum)

    def finish(piece):
        def rows(at, grad_normed):
            scaled, inverse = norm_rows(hidden[at, :].astype(F32))
            weighted = grad_normed * gain[...]
            first = jnp.mean(weighted, axis=-1, keepdims=True)
            second = jnp.mean(weighted * scaled, axis=-1, keepdims=True)
            result = grad[at, :].astype(F32) + inverse * (weighted - first - scaled * second)
            out[at, :] = result
            if line.held is not None:
                line.held[line.place, at, :] = result.astype(BF16)
            gain_sum[...] += jnp.sum(grad_normed * scaled, axis=0, keepdims=True)
            shift_sum[...] += jnp.sum(grad_normed, axis=0, keepdims=True)

        line.own_rows(piece, rows)

    return finish


def split(refs, *sizes):
    parts, start = [], 0
    for size in sizes:
        parts.append(refs[start : start + size])
        start += size
    return parts


def first_kernel(count, pieces, size, *refs):
    (own, gain, shift, share, bias, *tables), outs, gather, rest = split(refs, 8, 3, 3, 6)
    rows_out, mixed_out, weight_out = outs
    weight_held, mixed, load_sem, save_sem, weight_send, weight_recv = rest
    line = Line(count, pieces, None, None, None, None, None, *gather)
    weight = Whole(weight_held, size, weight_send, weight_recv)
    load = pltpu.make_async_copy(share, weight_held.at[weight.rows(0)], load_sem.at[0])
    keep = pltpu.make_async_copy(weight_held, weight_out, load_sem.at[1])
    load.start()
    line_barrier(line.place, count, weight.peers())
    saves = Saves([(line.held, rows_out), (mixed, mixed_out)], save_sem, line)
    compute = query_key_value(line, weight_held, bias, tables, mixed)
    load.wait()
    weight.start()

    def finish(piece):
        first_row = pl.multiple_of(piece * line.rows, line.rows)

        def rows(start, size):
            at = pl.ds(pl.multiple_of(first_row + start, size), size)
            scaled, _ = norm_rows(own[at, :].astype(F32))
            line.held[line.place, at, :] = (scaled * gain[...] + shift[...]).astype(BF16)

        line.chunks(rows)

    def each_tick(number):
        @pl.when(number == count - 1)
        def _():
            weight.pass_on()

    def process(piece):
        @pl.when(piece == 0)
        def _():
            weight.wait()
            keep.start()

        compute(piece)
        saves.start(piece)

    line.run(None, finish, process, each_tick, 2)
    line.drain()
    weight.drain()
    keep.wait()
    saves.wait()


def first(count, own, gain, shift, share, bias, tables, width):
    rows, depth = own.shape
    pieces = pieces_of(rows)
    size = lax.axis_size("dp")
    return line_call(
        functools.partial(first_kernel, count, pieces, size),
        (
            jax.ShapeDtypeStruct((count, rows, depth), BF16),
            jax.ShapeDtypeStruct((3, count, rows, width), BF16),
            jax.ShapeDtypeStruct((depth, 3 * width), BF16),
        ),
        (hbm, hbm, hbm),
        [vmem, vmem, vmem, hbm, vmem, vmem, vmem, vmem],
        gather_scratch(count, pieces, rows, depth)
        + [
            pltpu.VMEM((depth, 3 * width), BF16),
            pltpu.VMEM((3, count, rows, width), BF16),
            pltpu.SemaphoreType.DMA((2,)),
            pltpu.SemaphoreType.DMA((2, pieces)),
            pltpu.SemaphoreType.DMA((size,)),
            pltpu.SemaphoreType.DMA((size,)),
        ],
        0,
        6 * count * rows * depth * width,
        depth * width * 6 + own.size * 2 * count * 4,
    )(own, gain, shift, share, bias, *tables)


def middle_kernel(count, pieces, lag, *refs):
    ins, outs, scatter, gather, rest = split(refs, 6, 5, 5, 3, 10)
    source, w_out, before, gain, shift, w_up = ins
    after, rows_out, act_out, slope_out, silu_out = outs
    source_held, out_held, up_held, act, slope, silu, load_sem, tile_sem, save_sem, turn = rest
    line = Line(count, pieces, *scatter, *gather)
    loads = Loads([(source, source_held), (w_up, up_held)], load_sem)
    member = lax.axis_index("dp")
    core = member % 2
    partner = member + 1 - 2 * core
    tiles = Tiles(w_out, out_held, 1, tile_sem)
    line_barrier(line.place, count, (partner,) if lag else ())
    saves = Saves(
        [(line.held, rows_out), (act, act_out), (slope, slope_out), (silu, silu_out)], save_sem, line
    )
    compute = gate_and_up(line, up_held, act, slope, silu)

    def process(piece):
        @pl.when(piece == 0)
        def _():
            loads.wait(1)

        compute(piece)
        saves.start(piece)

    def signal(number):
        @pl.when((core == 0) & (number == lag))
        def _():
            pl.semaphore_signal(turn, inc=1, device_id={"dp": partner}, device_id_type=MESH)

    loads.wait(0)
    if lag:

        @pl.when(core == 1)
        def _():
            pl.semaphore_wait(turn, 1)

    line.run(
        share_of(line, source_held, out_held, tiles),
        add_and_norm(line, before, gain, shift, after),
        process,
        signal if lag else None,
    )
    line.drain()
    saves.wait()


def middle(count, source, w_out, before, gain, shift, w_up, lag=0):
    rows, depth = before.shape
    pieces = pieces_of(rows)
    width = w_up.shape[1] // 2
    wide = jax.ShapeDtypeStruct((count, rows, width), BF16)
    return line_call(
        functools.partial(middle_kernel, count, pieces, lag),
        (
            jax.ShapeDtypeStruct((rows, depth), F32),
            jax.ShapeDtypeStruct((count, rows, depth), BF16),
            wide,
            wide,
            wide,
        ),
        (vmem, hbm, hbm, hbm, hbm),
        [hbm, hbm, vmem, vmem, vmem, hbm],
        scatter_scratch(count, pieces, rows, depth)
        + gather_scratch(count, pieces, rows, depth)
        + [
            pltpu.VMEM(source.shape, BF16),
            pltpu.VMEM(w_out.shape, BF16),
            pltpu.VMEM(w_up.shape, BF16),
            pltpu.VMEM(wide.shape, BF16),
            pltpu.VMEM(wide.shape, BF16),
            pltpu.VMEM(wide.shape, BF16),
            pltpu.SemaphoreType.DMA((2,)),
            pltpu.SemaphoreType.DMA((max(1, depth // 256),)),
            pltpu.SemaphoreType.DMA((4, pieces)),
            pltpu.SemaphoreType.REGULAR,
        ],
        7 if lag else 1,
        2 * count * rows * (w_out.size + w_up.size),
        (w_out.size + w_up.size) * 2 + before.size * 60,
    )(source, w_out, before, gain, shift, w_up)


def between_kernel(count, pieces, *refs):
    ins, outs, scatter, gather, rest = split(refs, 10, 3, 5, 3, 7)
    source, w_down, before, gain, shift, weight, bias, *tables = ins
    after, rows_out, mixed_out = outs
    source_held, down_held, weight_held, mixed, load_sem, tile_sem, save_sem = rest
    line = Line(count, pieces, *scatter, *gather)
    loads = Loads([(source, source_held), (weight, weight_held)], load_sem)
    tiles = Tiles(w_down, down_held, 1, tile_sem)
    line_barrier(line.place, count)
    saves = Saves([(line.held, rows_out), (mixed, mixed_out)], save_sem, line)
    compute = query_key_value(line, weight_held, bias, tables, mixed)

    def process(piece):
        @pl.when(piece == 0)
        def _():
            loads.wait(1)

        compute(piece)
        saves.start(piece)

    loads.wait(0)
    line.run(
        share_of(line, source_held, down_held, tiles), add_and_norm(line, before, gain, shift, after), process
    )
    line.drain()
    saves.wait()


def between(count, source, w_down, before, gain, shift, weight, bias, tables):
    rows, depth = before.shape
    pieces = pieces_of(rows)
    mixed = (3, count, rows, weight.shape[1] // 3)
    return line_call(
        functools.partial(between_kernel, count, pieces),
        (
            jax.ShapeDtypeStruct((rows, depth), F32),
            jax.ShapeDtypeStruct((count, rows, depth), BF16),
            jax.ShapeDtypeStruct(mixed, BF16),
        ),
        (vmem, hbm, hbm),
        [hbm, hbm, vmem, vmem, vmem, hbm, vmem, vmem, vmem, vmem],
        scatter_scratch(count, pieces, rows, depth)
        + gather_scratch(count, pieces, rows, depth)
        + [
            pltpu.VMEM(source.shape, BF16),
            pltpu.VMEM(w_down.shape, BF16),
            pltpu.VMEM(weight.shape, BF16),
            pltpu.VMEM(mixed, BF16),
            pltpu.SemaphoreType.DMA((2,)),
            pltpu.SemaphoreType.DMA((max(1, depth // 256),)),
            pltpu.SemaphoreType.DMA((2, pieces)),
        ],
        2,
        2 * count * rows * (w_down.size + weight.size),
        (w_down.size + weight.size) * 2 + before.size * 60,
    )(source, w_down, before, gain, shift, weight, bias, *tables)


def turn_kernel(count, pieces, *refs):
    ins, outs, scatter, gather, rest = split(refs, 6, 3, 5, 3, 8)
    source, w_down, before, own, slope_in, silu_in = ins
    after, rows_out, wide_out = outs
    source_held, down_held, slope, silu, wide, load_sem, tile_sem, save_sem = rest
    line = Line(count, pieces, *scatter, *gather)
    loads = Loads(
        [(source, source_held), (slope_in, slope), (silu_in, silu)], load_sem
    )
    tiles = Tiles(w_down, down_held, 1, tile_sem)
    line_barrier(line.place, count)
    saves = Saves([(line.held, rows_out), (wide, wide_out)], save_sem, line)
    compute = grad_gate_and_up(line, down_held, slope, silu, wide)

    def finish(piece):
        def rows(at, total):
            after[at, :] = (before[at, :] + total).astype(BF16)
            line.held[line.place, at, :] = own[at, :]

        line.own_rows(piece, rows)

    def process(piece):
        @pl.when(piece == 0)
        def _():
            loads.wait(1, 2)

        compute(piece)
        saves.start(piece)

    loads.wait(0)
    line.run(share_of(line, source_held, down_held, tiles), finish, process)
    line.drain()
    saves.wait()


def turn(count, source, w_down, before, own, slope, silu):
    rows, depth = before.shape
    pieces = pieces_of(rows)
    width = w_down.shape[0]
    return line_call(
        functools.partial(turn_kernel, count, pieces),
        (
            jax.ShapeDtypeStruct((rows, depth), BF16),
            jax.ShapeDtypeStruct((count, rows, depth), BF16),
            jax.ShapeDtypeStruct((count, rows, 2 * width), BF16),
        ),
        (vmem, hbm, hbm),
        [hbm, hbm, vmem, vmem, hbm, hbm],
        scatter_scratch(count, pieces, rows, depth)
        + gather_scratch(count, pieces, rows, depth)
        + [
            pltpu.VMEM(source.shape, BF16),
            pltpu.VMEM(w_down.shape, BF16),
            pltpu.VMEM(slope.shape, BF16),
            pltpu.VMEM(silu.shape, BF16),
            pltpu.VMEM((count, rows, 2 * width), BF16),
            pltpu.SemaphoreType.DMA((3,)),
            pltpu.SemaphoreType.DMA((max(1, depth // 256),)),
            pltpu.SemaphoreType.DMA((2, pieces)),
        ],
        3,
        4 * count * rows * w_down.size,
        w_down.size * 2 + before.size * 60,
    )(source, w_down, before, own, slope, silu)


def middle_back_kernel(count, pieces, *refs):
    ins, outs, scatter, gather, rest = split(refs, 6, 5, 5, 3, 7)
    source, w_up, grad, hidden, gain, w_out = ins
    out, gain_sum, shift_sum, rows_out, result_out = outs
    source_held, up_held, out_held, result, load_sem, tile_sem, save_sem = rest
    line = Line(count, pieces, *scatter, *gather)
    loads = Loads([(source, source_held), (w_out, out_held)], load_sem)
    tiles = Tiles(w_up, up_held, 0, tile_sem)
    line_barrier(line.place, count)
    saves = Saves([(line.held, rows_out), (result, result_out)], save_sem, line)
    compute = through_transposed(line, out_held, result)

    def process(piece):
        @pl.when(piece == 0)
        def _():
            loads.wait(1)

        compute(piece)
        saves.start(piece)

    loads.wait(0)
    line.run(
        share_transposed(line, [source_held], up_held, tiles),
        norm_backward(line, grad, hidden, gain, out, gain_sum, shift_sum),
        process,
    )
    line.drain()
    saves.wait()


def middle_back(count, source, w_up, grad, hidden, gain, w_out):
    rows, depth = grad.shape
    pieces = pieces_of(rows)
    width = w_out.shape[0]
    return line_call(
        functools.partial(middle_back_kernel, count, pieces),
        (
            jax.ShapeDtypeStruct((rows, depth), F32),
            jax.ShapeDtypeStruct((1, depth), F32),
            jax.ShapeDtypeStruct((1, depth), F32),
            jax.ShapeDtypeStruct((count, rows, depth), BF16),
            jax.ShapeDtypeStruct((count, rows, width), BF16),
        ),
        (vmem, vmem, vmem, hbm, hbm),
        [hbm, hbm, vmem, vmem, vmem, hbm],
        scatter_scratch(count, pieces, rows, depth)
        + gather_scratch(count, pieces, rows, depth)
        + [
            pltpu.VMEM(source.shape, BF16),
            pltpu.VMEM(w_up.shape, BF16),
            pltpu.VMEM(w_out.shape, BF16),
            pltpu.VMEM((count, rows, width), BF16),
            pltpu.SemaphoreType.DMA((2,)),
            pltpu.SemaphoreType.DMA((max(1, depth // 256),)),
            pltpu.SemaphoreType.DMA((2, pieces)),
        ],
        4 if grad.dtype == F32 else 8,
        2 * count * rows * (w_up.size + w_out.size),
        (w_up.size + w_out.size) * 2 + grad.size * 60,
    )(source, w_up, grad, hidden, gain, w_out)


def between_back_kernel(count, pieces, *refs):
    ins, outs, scatter, gather, rest = split(refs, 8, 5, 5, 3, 9)
    source, weight, grad, hidden, gain, w_down, slope_in, silu_in = ins
    out, gain_sum, shift_sum, rows_out, wide_out = outs
    source_held, weight_held, down_held, slope, silu, wide, load_sem, tile_sem, save_sem = rest
    line = Line(count, pieces, *scatter, *gather)
    loads = Loads(
        [
            (source, source_held),
            (w_down, down_held),
            (slope_in, slope),
            (silu_in, silu),
        ],
        load_sem,
    )
    tiles = Tiles(weight, weight_held, 0, tile_sem)
    line_barrier(line.place, count)
    saves = Saves([(line.held, rows_out), (wide, wide_out)], save_sem, line)
    compute = grad_gate_and_up(line, down_held, slope, silu, wide)

    def process(piece):
        @pl.when(piece == 0)
        def _():
            loads.wait(1, 2, 3)

        compute(piece)
        saves.start(piece)

    loads.wait(0)
    line.run(
        share_transposed(line, [source_held.at[kind] for kind in range(3)], weight_held, tiles),
        norm_backward(line, grad, hidden, gain, out, gain_sum, shift_sum),
        process,
    )
    line.drain()
    saves.wait()


def between_back(count, source, weight, grad, hidden, gain, w_down, slope, silu):
    rows, depth = grad.shape
    pieces = pieces_of(rows)
    width = w_down.shape[0]
    return line_call(
        functools.partial(between_back_kernel, count, pieces),
        (
            jax.ShapeDtypeStruct((rows, depth), F32),
            jax.ShapeDtypeStruct((1, depth), F32),
            jax.ShapeDtypeStruct((1, depth), F32),
            jax.ShapeDtypeStruct((count, rows, depth), BF16),
            jax.ShapeDtypeStruct((count, rows, 2 * width), BF16),
        ),
        (vmem, vmem, vmem, hbm, hbm),
        [hbm, hbm, vmem, vmem, vmem, hbm, hbm, hbm],
        scatter_scratch(count, pieces, rows, depth)
        + gather_scratch(count, pieces, rows, depth)
        + [
            pltpu.VMEM(source.shape, BF16),
            pltpu.VMEM(weight.shape, BF16),
            pltpu.VMEM(w_down.shape, BF16),
            pltpu.VMEM(slope.shape, BF16),
            pltpu.VMEM(silu.shape, BF16),
            pltpu.VMEM((count, rows, 2 * width), BF16),
            pltpu.SemaphoreType.DMA((4,)),
            pltpu.SemaphoreType.DMA((max(1, depth // 256),)),
            pltpu.SemaphoreType.DMA((2, pieces)),
        ],
        5,
        2 * count * rows * (w_down.size + weight.size),
        (w_down.size + weight.size) * 2 + grad.size * 60,
    )(source, weight, grad, hidden, gain, w_down, slope, silu)


def last_kernel(count, pieces, *refs):
    ins, outs, scatter, rest = split(refs, 5, 3, 5, 4)
    source, weight, grad, hidden, gain = ins
    source_held, weight_held, load_sem, tile_sem = rest
    line = Line(count, pieces, *scatter, None, None, None)
    loads = Loads([(source, source_held), ], load_sem)
    tiles = Tiles(weight, weight_held, 0, tile_sem)
    line_barrier(line.place, count)
    loads.wait(0)
    line.run(
        share_transposed(line, [source_held.at[kind] for kind in range(3)], weight_held, tiles),
        norm_backward(line, grad, hidden, gain, *outs),
        None,
    )
    line.drain()


def last(count, source, weight, grad, hidden, gain):
    rows, depth = grad.shape
    pieces = pieces_of(rows)
    return line_call(
        functools.partial(last_kernel, count, pieces),
        (
            jax.ShapeDtypeStruct((rows, depth), F32),
            jax.ShapeDtypeStruct((1, depth), F32),
            jax.ShapeDtypeStruct((1, depth), F32),
        ),
        (vmem, vmem, vmem),
        [hbm, hbm, vmem, vmem, vmem],
        scatter_scratch(count, pieces, rows, depth)
        + [
            pltpu.VMEM(source.shape, BF16),
            pltpu.VMEM(weight.shape, BF16),
            pltpu.SemaphoreType.DMA((1,)),
            pltpu.SemaphoreType.DMA((max(1, depth // 256),)),
        ],
        6,
        2 * count * rows * weight.size,
        weight.size * 2 + grad.size * 20,
    )(source, weight, grad, hidden, gain)


def key_parts(first, start, seen):
    size = seen - start
    parts = []
    if start:
        key_index = lax.broadcasted_iota(jnp.int32, (start, size), 0)
        parts.append((slice(0, start), key_index >= first))
    key_index = start + lax.broadcasted_iota(jnp.int32, (size, size), 0)
    query_index = start + lax.broadcasted_iota(jnp.int32, (size, size), 1)
    parts.append((slice(start, seen), (key_index >= first) & (key_index <= query_index)))
    return parts


def head_lanes(values, head):
    lane = lax.broadcasted_iota(jnp.int32, values.shape, 1)
    return jnp.where((lane // HD) == head, values, jnp.zeros_like(values))


def attend_kernel(block, positions, queries, keys, values, attended, logsums):
    length = keys.shape[0]
    values_across = jnp.transpose(values[...])
    for start in range(0, length, block):
        seen = start + block
        at = slice(start, seen)
        own = queries[at, :]
        index = start + lax.broadcasted_iota(jnp.int32, (1, block), 1)
        parts = key_parts(index - positions[:, at], start, seen)
        halves = []
        for head in range(2):
            own_head = head_lanes(own, head)
            scores = [
                jnp.where(allowed, matmul(keys[part, :], own_head, cols_cols), masked_score)
                for part, allowed in parts
            ]
            highest = functools.reduce(
                jnp.maximum, [jnp.max(each, axis=0, keepdims=True) for each in scores]
            )
            sums, result = 0.0, 0.0
            for (part, _), each in zip(parts, scores):
                weights = jnp.exp(each - highest)
                sums = sums + jnp.sum(weights, axis=0, keepdims=True)
                result = result + matmul(values_across[:, part], weights.astype(BF16))
            halves.append(result[head * HD : (head + 1) * HD, :] / sums)
            logsums[head : head + 1, at] = highest + jnp.log(sums)
        attended[at, :] = jnp.transpose(jnp.concatenate(halves, axis=0)).astype(BF16)


def pair_spec(length, kind):
    return pl.BlockSpec((None, length, PAIR), lambda pair: (kind, 0, pair))


def attend(mixed, positions):
    _, length, width = mixed.shape
    pairs = width // PAIR
    block = min(256, length)
    return pl.pallas_call(
        functools.partial(attend_kernel, block),
        grid=(pairs,),
        out_shape=(
            jax.ShapeDtypeStruct((length, width), BF16),
            jax.ShapeDtypeStruct((pairs, 2, length), F32),
        ),
        in_specs=[
            pl.BlockSpec((1, length), lambda pair: (0, 0)),
            pair_spec(length, 0),
            pair_spec(length, 1),
            pair_spec(length, 2),
        ],
        out_specs=(
            pl.BlockSpec((length, PAIR), lambda pair: (0, pair)),
            pl.BlockSpec((None, 2, length), lambda pair: (pair, 0, 0)),
        ),
        compiler_params=pltpu.CompilerParams(vmem_limit_bytes=VMEM_LIMIT),
        cost_estimate=pl.CostEstimate(
            flops=8 * length * length * width,
            bytes_accessed=8 * length * width,
            transcendentals=length * length * width // HD,
        ),
    )(positions, mixed, mixed, mixed)


def unrotate(values, cos, sin_up, sin_down):
    return (
        values * cos
        - pltpu.roll(values, PAIR - ROT // 2, 1) * sin_up
        - pltpu.roll(values, ROT // 2, 1) * sin_down
    )


def attend_back_kernel(
    block, positions, queries, keys, values, attended, grad_attended, logsums,
    cos, sin_up, sin_down, grad_mixed, bias_sum, grad_keys, grad_values,
):
    length = keys.shape[0]
    keys_across = jnp.transpose(keys[...])
    grad_keys[...] = jnp.zeros_like(grad_keys)
    grad_values[...] = jnp.zeros_like(grad_values)
    bias_sum[...] = jnp.zeros_like(bias_sum)
    for start in range(0, length, block):
        seen = start + block
        at = slice(start, seen)
        own = queries[at, :]
        grad_own = grad_attended[at, :]
        inner = jnp.transpose(grad_own.astype(F32) * attended[at, :].astype(F32))
        index = start + lax.broadcasted_iota(jnp.int32, (1, block), 1)
        parts = key_parts(index - positions[:, at], start, seen)
        halves = []
        for head in range(2):
            own_head = head_lanes(own, head)
            grad_head = head_lanes(grad_own, head)
            row_inner = jnp.sum(inner[head * HD : (head + 1) * HD, :], axis=0, keepdims=True)
            result = 0.0
            for part, allowed in parts:
                scores = matmul(keys[part, :], own_head, cols_cols)
                weights = jnp.where(allowed, jnp.exp(scores - logsums[head : head + 1, at]), 0.0)
                grad_weights = matmul(values[part, :], grad_head, cols_cols)
                grad_scores = (weights * (grad_weights - row_inner)).astype(BF16)
                grad_values[part, :] += matmul(weights.astype(BF16), grad_head)
                grad_keys[part, :] += matmul(grad_scores, own_head)
                result = result + matmul(keys_across[:, part], grad_scores)
            halves.append(result[head * HD : (head + 1) * HD, :])
        grad_own_queries = jnp.transpose(jnp.concatenate(halves, axis=0)) * (1.0 / math.sqrt(HD))
        low = unrotate(grad_own_queries, cos[at, :], sin_up[at, :], sin_down[at, :]).astype(BF16)
        grad_mixed[0, at, :] = low
        bias_sum[0:1, :] += jnp.sum(low.astype(F32), axis=0, keepdims=True)
    for start in range(0, length, block):
        at = slice(start, start + block)
        low = unrotate(grad_keys[at, :], cos[at, :], sin_up[at, :], sin_down[at, :]).astype(BF16)
        grad_mixed[1, at, :] = low
        bias_sum[1:2, :] += jnp.sum(low.astype(F32), axis=0, keepdims=True)
        low = grad_values[at, :].astype(BF16)
        grad_mixed[2, at, :] = low
        bias_sum[2:3, :] += jnp.sum(low.astype(F32), axis=0, keepdims=True)


def attend_backward(mixed, positions, attended, grad_attended, logsums, tables):
    _, length, width = mixed.shape
    pairs = width // PAIR
    block = min(256, length)
    across = pl.BlockSpec((length, PAIR), lambda pair: (0, pair))
    table = pl.BlockSpec((length, PAIR), lambda pair: (0, 0))
    return pl.pallas_call(
        functools.partial(attend_back_kernel, block),
        grid=(pairs,),
        out_shape=(
            jax.ShapeDtypeStruct((3, length, width), BF16),
            jax.ShapeDtypeStruct((3, width), F32),
        ),
        in_specs=[
            pl.BlockSpec((1, length), lambda pair: (0, 0)),
            pair_spec(length, 0),
            pair_spec(length, 1),
            pair_spec(length, 2),
            across,
            across,
            pl.BlockSpec((None, 2, length), lambda pair: (pair, 0, 0)),
            table,
            table,
            table,
        ],
        out_specs=(
            pl.BlockSpec((3, length, PAIR), lambda pair: (0, 0, pair)),
            pl.BlockSpec((3, PAIR), lambda pair: (0, pair)),
        ),
        scratch_shapes=[pltpu.VMEM((length, PAIR), F32), pltpu.VMEM((length, PAIR), F32)],
        compiler_params=pltpu.CompilerParams(vmem_limit_bytes=VMEM_LIMIT),
        cost_estimate=pl.CostEstimate(
            flops=20 * length * length * width,
            bytes_accessed=16 * length * width,
            transcendentals=length * length * width // HD,
        ),
    )(positions, mixed, mixed, mixed, attended, grad_attended, logsums, *tables)


def weight_grad_kernel(groups, tile, *refs):
    ins, (out,), rest = split(refs, 2 * groups, 1, 2 * groups + 6)
    held, (across, stages, tail, load_sem, out_sem, tail_sem) = split(rest, 2 * groups, 6)
    loads = Loads(list(zip(ins, held)), load_sem)
    depth, length = across.shape
    chunk = min(1024, depth)

    def save(slot, column):
        return pltpu.make_async_copy(
            stages.at[slot], out.at[:, pl.ds(pl.multiple_of(column, 128), tile)], out_sem.at[slot]
        )

    column, done = 0, 0
    for group in range(groups):
        left, right = held[2 * group], held[2 * group + 1]
        loads.wait(2 * group)

        def turn_over(number, carry, left=left):
            at = pl.ds(pl.multiple_of(number * 256, 256), 256)
            across[at, :] = jnp.transpose(left[:, at])
            return carry

        lax.fori_loop(0, depth // 256, turn_over, 0)
        loads.wait(2 * group + 1)
        kinds, _, width = right.shape
        full, short = width // tile, width % tile
        for kind in range(kinds):

            def fill(target, start, size, kind=kind, right=right):
                def rows(number, carry):
                    at = pl.ds(pl.multiple_of(number * chunk, chunk), chunk)
                    target[at, :] = matmul(across[at, :], right[kind, :, pl.ds(start, size)]).astype(BF16)
                    return carry

                lax.fori_loop(0, depth // chunk, rows, 0)

            def one(number, carry, fill=fill, column=column, done=done):
                slot = (done + number) % 2

                @pl.when(done + number >= 2)
                def _():
                    save(slot, 0).wait()

                start = pl.multiple_of(number * tile, tile)
                fill(stages.at[slot], start, tile)
                save(slot, column + start).start()
                return carry

            lax.fori_loop(0, full, one, 0)
            done += full
            if short:
                fill(tail, full * tile, short)
                copy = pltpu.make_async_copy(
                    tail, out.at[:, column + full * tile : column + width], tail_sem
                )
                copy.start()
                copy.wait()
            column += width
    for slot in range(min(2, done)):
        save(slot, 0).wait()


def weight_grad(*pairs):
    length, depth = pairs[0][0].shape
    total = sum(right.shape[0] * right.shape[2] for _, right in pairs)
    tile = min(256, *(right.shape[2] for _, right in pairs))
    short = max(right.shape[2] % tile for _, right in pairs)
    arrays = [array for pair in pairs for array in pair]
    return pl.pallas_call(
        functools.partial(weight_grad_kernel, len(pairs), tile),
        out_shape=jax.ShapeDtypeStruct((depth, total), BF16),
        in_specs=[hbm] * len(arrays),
        out_specs=hbm,
        scratch_shapes=[pltpu.VMEM(array.shape, BF16) for array in arrays]
        + [
            pltpu.VMEM((depth, length), BF16),
            pltpu.VMEM((2, depth, tile), BF16),
            pltpu.VMEM((depth, short or 128), BF16),
            pltpu.SemaphoreType.DMA((len(arrays),)),
            pltpu.SemaphoreType.DMA((2,)),
            pltpu.SemaphoreType.DMA,
        ],
        compiler_params=pltpu.CompilerParams(vmem_limit_bytes=VMEM_LIMIT),
        cost_estimate=pl.CostEstimate(
            flops=2 * length * depth * total, bytes_accessed=4 * depth * total, transcendentals=0
        ),
    )(*arrays)


def rotary_tables(positions):
    half_rot = ROT // 2
    lane = jnp.arange(PAIR, dtype=jnp.int32) % HD
    frequency = jnp.exp(-((lane % half_rot).astype(F32) * 2.0 / ROT) * theta_log)
    angles = positions.astype(F32)[:, None] * frequency[None, :]
    cos, sin = jnp.cos(angles), jnp.sin(angles)
    return (
        jnp.where(lane < ROT, cos, 1.0),
        jnp.where(lane < half_rot, -sin, 0.0),
        jnp.where((lane >= half_rot) & (lane < ROT), sin, 0.0),
    )


def all_sum(values, axes, beside):
    beside, made = list(beside), []
    for axis in axes:
        size = lax.axis_size(axis)
        if size & (size - 1):
            values = lax.psum(values, axis)
            continue
        step = 1
        while step < size:
            moved = lax.ppermute(values, axis, [(i, i ^ step) for i in range(size)])
            if beside:
                moved, array = lax.optimization_barrier((moved, beside.pop(0)))
                made.append(array)
            values = values + moved
            step *= 2
    return values, made + beside


def owner_sum(part, axis):
    return lax.psum_scatter(part, "dp", scatter_dimension=axis, tiled=True)


def after(values, *others):
    return lax.optimization_barrier((values, *others))


def per_device(
    tokens, positions, norm_gain, norm_bias, w_qkv, b_qkv, w_out, w_gate_up, w_down, cotangent
):
    count = lax.axis_size("tensor")
    tensor_rank = lax.axis_index("tensor")
    width = w_qkv.shape[3]
    ff_local = w_gate_up.shape[3]
    rows, depth = tokens.shape
    length = positions.shape[0]
    tables = rotary_tables(positions)
    positions_row = positions.reshape(1, length)

    def whole(weight, axis):
        return lax.all_gather(weight, "dp", axis=axis, tiled=True)

    flat = [
        [
            w_qkv[layer].reshape(-1, 3 * width),
            w_out[layer],
            w_gate_up[layer].reshape(-1, 2 * ff_local),
            w_down[layer],
        ]
        for layer in range(LAYERS)
    ]
    axes = (0, 1, 0, 1)
    gathered = [[None, whole(flat[0][1], axes[1]), whole(flat[0][2], axes[2]), None]]
    hidden = tokens
    block_tables = tuple(table.reshape(count, rows, -1) for table in tables)
    biases = [
        lax.dynamic_slice_in_dim(b_qkv[layer], tensor_rank * width, width, 1).reshape(1, 3 * width)
        for layer in range(LAYERS)
    ]
    rows_a, mixed, gathered[0][0] = first(
        count, tokens, norm_gain[0, 0:1], norm_bias[0, 0:1], flat[0][0], biases[0], block_tables, width
    )
    mixed, flat[0][3] = after(mixed, flat[0][3])
    gathered[0][3] = whole(flat[0][3], axes[3])
    kept = []
    for layer in range(LAYERS):
        mixed = mixed.reshape(3, length, width)
        attended, logsums = attend(mixed, positions_row)
        if layer + 1 < LAYERS:
            attended, *flat[layer + 1] = after(attended, *flat[layer + 1])
            gathered.append([whole(flat[layer + 1][kind], axes[kind]) for kind in range(4)])
        full_qkv, full_out, full_gu, full_down = gathered[layer]
        hidden_mid, rows_b, act, slope, silu = middle(
            count,
            attended.reshape(count, rows, width),
            full_out,
            hidden,
            norm_gain[layer, 1:2],
            norm_bias[layer, 1:2],
            full_gu,
            LAG if layer == 0 else 0,
        )
        kept.append((hidden, rows_a, mixed, attended, logsums, hidden_mid, rows_b, act, slope, silu))
        if layer + 1 < LAYERS:
            hidden, rows_a, mixed = between(
                count,
                act,
                full_down,
                hidden_mid,
                norm_gain[layer + 1, 0:1],
                norm_bias[layer + 1, 0:1],
                gathered[layer + 1][0],
                biases[layer + 1],
                block_tables,
            )
        else:
            activations, grad_rows_b, wide = turn(
                count, act, full_down, hidden_mid, cotangent, slope, silu
            )
    grad = cotangent
    scattered = [None] * LAYERS
    small = [None] * LAYERS
    for layer in reversed(range(LAYERS)):
        hidden, rows_a, mixed, attended, logsums, hidden_mid, rows_b, act, slope, silu = kept[layer]
        full_qkv, full_out, full_gu, full_down = gathered[layer]
        later = scattered[layer + 1] if layer + 1 < LAYERS else None
        feed_part = weight_grad(
            (rows_b.reshape(length, depth), wide.reshape(1, length, 2 * ff_local)),
            (grad_rows_b.reshape(length, depth), act.reshape(1, length, ff_local)),
        )
        wide, feed_part = after(wide, feed_part)
        feed_grad = owner_sum(feed_part, 0)
        if later:
            wide, later[1] = after(wide, later[1])
        grad, gain_b, shift_b, grad_rows_a, grad_attended = middle_back(
            count, wide, full_gu, grad, hidden_mid, norm_gain[layer, 1:2], full_out
        )
        if later:
            grad_attended, later[0] = after(grad_attended, later[0])
        grad_mixed, bias_sum = attend_backward(
            mixed, positions_row, attended, grad_attended.reshape(length, width), logsums, tables
        )
        attend_part = weight_grad(
            (rows_a.reshape(length, depth), grad_mixed),
            (grad_rows_a.reshape(length, depth), attended.reshape(1, length, width)),
        )
        grad_mixed, attend_part = after(grad_mixed, attend_part)
        attend_grad = owner_sum(attend_part, 0)
        source = grad_mixed.reshape(3, count, rows, width)
        if layer:
            below = kept[layer - 1]
            grad, gain_a, shift_a, grad_rows_b, wide = between_back(
                count,
                source,
                full_qkv,
                grad,
                hidden,
                norm_gain[layer, 0:1],
                gathered[layer - 1][3],
                below[8],
                below[9],
            )
        else:
            grad, gain_a, shift_a = last(count, source, full_qkv, grad, hidden, norm_gain[layer, 0:1])
        bias_full = lax.dynamic_update_slice(
            jnp.zeros((3, b_qkv.shape[2]), F32), bias_sum, (jnp.int32(0), tensor_rank * width)
        )
        small[layer] = jnp.concatenate([gain_a, gain_b, shift_a, shift_b, bias_full], axis=0)
        scattered[layer] = [attend_grad, feed_grad]
    cuts = (
        lambda each: each[0][:, : 3 * width].reshape(-1, 3, width),
        lambda each: each[0][:, 3 * width :].T,
        lambda each: each[1][:, : 2 * ff_local].reshape(-1, 2, ff_local),
        lambda each: each[1][:, 2 * ff_local :].T,
    )
    stacks = [jnp.stack([cut(each).astype(F32) for each in scattered]) for cut in cuts]
    sums, made = all_sum(jnp.stack(small), ("dp", "tensor"), stacks[2:] + stacks[:2])
    stacks = made[2:] + made[:2]
    return (
        activations,
        grad,
        sums[:, 0:2],
        sums[:, 2:4],
        stacks[0],
        sums[:, 4:7],
        stacks[1],
        stacks[2],
        stacks[3],
    )


def norm_parts(hidden):
    average = jnp.mean(hidden, axis=-1, keepdims=True)
    centred = hidden - average
    variance = jnp.mean(centred * centred, axis=-1, keepdims=True)
    inverse = lax.rsqrt(variance + norm_eps)
    return (centred * inverse, inverse)


def norm_back(grad_normed, scaled, inverse, norm_weight):
    weighted = grad_normed * norm_weight
    first_mean = jnp.mean(weighted, axis=-1, keepdims=True)
    second_mean = jnp.mean(weighted * scaled, axis=-1, keepdims=True)
    grad_input = inverse * (weighted - first_mean - scaled * second_mean)
    return (grad_input, jnp.sum(grad_normed * scaled, axis=0), jnp.sum(grad_normed, axis=0))


def plain_tables(positions):
    half_rot = ROT // 2
    frequency = jnp.exp(-(jnp.arange(half_rot, dtype=jnp.float32) * 2.0 / ROT) * theta_log)
    angles = positions.astype(jnp.float32)[:, None] * frequency[None, :]
    return (jnp.cos(angles)[:, None, :], jnp.sin(angles)[:, None, :])


def rotate(values, cos_table, sin_table):
    half_rot = ROT // 2
    first_half = values[..., :half_rot]
    second_half = values[..., half_rot:ROT]
    return jnp.concatenate(
        [
            first_half * cos_table - second_half * sin_table,
            second_half * cos_table + first_half * sin_table,
            values[..., ROT:],
        ],
        axis=-1,
    )


def inner_rows(left, right):
    return lax.dot_general(left, right, rows_rows, preferred_element_type=jnp.float32)


def inner_cols(left, right):
    return lax.dot_general(left, right, cols_cols, preferred_element_type=jnp.float32)


def block_scores(queries, key_rows, positions, number, block_rows, score_scale):
    seq_len = key_rows.shape[0]
    row_start = number * block_rows
    query_block = lax.dynamic_slice_in_dim(queries, row_start, block_rows, 0)
    scores = (
        jnp.einsum("qhd,khd->hqk", query_block, key_rows, preferred_element_type=jnp.float32)
        * score_scale
    )
    row_index = row_start + jnp.arange(block_rows, dtype=jnp.int32)
    first_key = row_index - lax.dynamic_slice_in_dim(positions, row_start, block_rows, 0)
    columns = jnp.arange(seq_len, dtype=jnp.int32)
    allowed = (columns[None, :] <= row_index[:, None]) & (columns[None, :] >= first_key[:, None])
    return (query_block, allowed, jnp.where(allowed[None], scores, masked_score))


def attend_forward(queries, key_rows, values, positions, score_scale):
    seq_len = queries.shape[0]
    block_rows = min(512, seq_len)

    def one_block(number):
        query_block, allowed, scores = block_scores(
            queries, key_rows, positions, number, block_rows, score_scale
        )
        row_max = jnp.max(scores, axis=-1, keepdims=True)
        shifted = jnp.exp(scores - row_max)
        row_sum = jnp.sum(shifted, axis=-1, keepdims=True)
        weights_low = (shifted / row_sum).astype(jnp.bfloat16)
        block_out = jnp.einsum(
            "hqk,khd->qhd", weights_low, values, preferred_element_type=jnp.float32
        )
        return (block_out, row_max + jnp.log(row_sum))

    block_outs, logsums = lax.map(one_block, jnp.arange(seq_len // block_rows, dtype=jnp.int32))
    return (block_outs.reshape(seq_len, -1), logsums)


def attend_back(queries, key_rows, values, positions, logsums, grad_attended, score_scale):
    seq_len = queries.shape[0]
    block_rows = min(512, seq_len)

    def one_block(totals, inputs):
        grad_keys, grad_values = totals
        number, logsum = inputs
        query_block, allowed, scores = block_scores(
            queries, key_rows, positions, number, block_rows, score_scale
        )
        softmax_rows = jnp.exp(scores - logsum)
        grad_block = lax.dynamic_slice_in_dim(grad_attended, number * block_rows, block_rows, 0)
        grad_probs = jnp.einsum(
            "qhd,khd->hqk", grad_block, values, preferred_element_type=jnp.float32
        )
        grad_values = grad_values + jnp.einsum(
            "hqk,qhd->khd",
            softmax_rows.astype(jnp.bfloat16),
            grad_block,
            preferred_element_type=jnp.float32,
        )
        row_inner = jnp.sum(softmax_rows * grad_probs, axis=-1, keepdims=True)
        grad_scores = jnp.where(allowed[None], softmax_rows * (grad_probs - row_inner), 0.0).astype(
            jnp.bfloat16
        )
        grad_query = (
            jnp.einsum("hqk,khd->qhd", grad_scores, key_rows, preferred_element_type=jnp.float32)
            * score_scale
        )
        grad_keys = (
            grad_keys
            + jnp.einsum(
                "hqk,qhd->khd", grad_scores, query_block, preferred_element_type=jnp.float32
            )
            * score_scale
        )
        return ((grad_keys, grad_values), grad_query)

    empty_grad = jnp.zeros(key_rows.shape, jnp.float32)
    numbers = jnp.arange(seq_len // block_rows, dtype=jnp.int32)
    (grad_keys, grad_values), grad_queries = lax.scan(
        one_block, (empty_grad, empty_grad), (numbers, logsums)
    )
    return (grad_queries.reshape(queries.shape), grad_keys, grad_values)


def per_device_plain(
    tokens, positions, norm_gain, norm_bias, w_qkv, b_qkv, w_out, w_gate_up, w_down, cotangent
):
    tensor_rank = lax.axis_index("tensor")
    width_local = w_qkv.shape[3]
    heads_local = width_local // HD
    ff_local = w_gate_up.shape[3]
    local_rows = tokens.shape[0]
    seq_len = positions.shape[0]
    score_scale = 1.0 / math.sqrt(HD)
    cos_table, sin_table = plain_tables(positions)
    hidden = tokens.astype(jnp.float32)
    kept_state = []
    for layer_index in range(LAYERS):
        gathered = (
            lax.all_gather(w_qkv[layer_index], "dp", axis=0, tiled=True),
            lax.all_gather(w_out[layer_index], "dp", axis=1, tiled=True),
            lax.all_gather(w_gate_up[layer_index], "dp", axis=0, tiled=True),
            lax.all_gather(w_down[layer_index], "dp", axis=1, tiled=True),
        )
        full_qkv, full_out, full_gu, full_down = gathered
        scaled_a, inverse_a = norm_parts(hidden)
        normed_a = (scaled_a * norm_gain[layer_index, 0] + norm_bias[layer_index, 0]).astype(
            jnp.bfloat16
        )
        rows_a = lax.all_gather(normed_a, "tensor", axis=0, tiled=True)
        bias_local = lax.dynamic_slice_in_dim(
            b_qkv[layer_index], tensor_rank * width_local, width_local, 1
        )
        mixed = jnp.dot(
            rows_a,
            full_qkv.reshape(full_qkv.shape[0], 3 * width_local),
            preferred_element_type=jnp.float32,
        ) + bias_local.reshape(3 * width_local)
        mixed = mixed.reshape(seq_len, 3, heads_local, HD)
        queries = rotate(mixed[:, 0], cos_table, sin_table).astype(jnp.bfloat16)
        key_rows = rotate(mixed[:, 1], cos_table, sin_table).astype(jnp.bfloat16)
        values = mixed[:, 2].astype(jnp.bfloat16)
        attended, logsums = attend_forward(queries, key_rows, values, positions, score_scale)
        attended = attended.astype(jnp.bfloat16)

        def project_attn(row_start, row_count, source=attended, weight=full_out):
            return jnp.dot(source, weight, preferred_element_type=jnp.float32)

        branch_a = lax.psum_scatter(
            project_attn(jnp.int32(0), local_rows * lax.axis_size("tensor")).astype(jnp.bfloat16),
            "tensor",
            scatter_dimension=0,
            tiled=True,
        ).astype(jnp.float32)
        hidden_mid = hidden + branch_a
        scaled_b, inverse_b = norm_parts(hidden_mid)
        normed_b = (scaled_b * norm_gain[layer_index, 1] + norm_bias[layer_index, 1]).astype(
            jnp.bfloat16
        )
        rows_b = lax.all_gather(normed_b, "tensor", axis=0, tiled=True)
        gate_up = jnp.dot(
            rows_b,
            full_gu.reshape(full_gu.shape[0], 2 * ff_local),
            preferred_element_type=jnp.float32,
        ).reshape(seq_len, 2, ff_local)
        activated = (jax.nn.silu(gate_up[:, 0]) * gate_up[:, 1]).astype(jnp.bfloat16)

        def project_mlp(row_start, row_count, source=activated, weight=full_down):
            return jnp.dot(source, weight, preferred_element_type=jnp.float32)

        hidden = hidden_mid + lax.psum_scatter(
            project_mlp(jnp.int32(0), local_rows * lax.axis_size("tensor")).astype(jnp.bfloat16),
            "tensor",
            scatter_dimension=0,
            tiled=True,
        ).astype(jnp.float32)
        kept_state.append(
            (
                gathered,
                scaled_a,
                inverse_a,
                rows_a,
                queries,
                key_rows,
                values,
                logsums,
                attended,
                scaled_b,
                inverse_b,
                rows_b,
                gate_up,
                activated,
            )
        )
    activations = hidden.astype(jnp.bfloat16)
    grad = cotangent.astype(jnp.float32)
    weight_parts = [None] * LAYERS
    gain_rows = [None] * LAYERS
    shift_rows = [None] * LAYERS
    qkv_shift_rows = [None] * LAYERS
    for layer_index in reversed(range(LAYERS)):
        (
            gathered,
            scaled_a,
            inverse_a,
            rows_a,
            queries,
            key_rows,
            values,
            logsums,
            attended,
            scaled_b,
            inverse_b,
            rows_b,
            gate_up,
            activated,
        ) = kept_state[layer_index]
        full_qkv, full_out, full_gu, full_down = (
            lax.all_gather(w_qkv[layer_index], "dp", axis=0, tiled=True),
            lax.all_gather(w_out[layer_index], "dp", axis=1, tiled=True),
            lax.all_gather(w_gate_up[layer_index], "dp", axis=0, tiled=True),
            lax.all_gather(w_down[layer_index], "dp", axis=1, tiled=True),
        )
        grad_rows_b = lax.all_gather(grad.astype(jnp.bfloat16), "tensor", axis=0, tiled=True)
        grad_down_weight = inner_rows(activated, grad_rows_b)
        grad_act = inner_cols(grad_rows_b, full_down)
        gate_part = gate_up[:, 0]
        up_part = gate_up[:, 1]
        sigmoid_gate = jax.nn.sigmoid(gate_part)
        grad_gate = grad_act * up_part * sigmoid_gate * (1.0 + gate_part * (1.0 - sigmoid_gate))
        grad_up = grad_act * jax.nn.silu(gate_part)
        grad_gate_up = (
            jnp.stack([grad_gate, grad_up], axis=1)
            .astype(jnp.bfloat16)
            .reshape(seq_len, 2 * ff_local)
        )
        grad_gu_weight = inner_rows(rows_b, grad_gate_up).reshape(full_gu.shape)
        flat_gu = full_gu.reshape(full_gu.shape[0], 2 * ff_local)

        def back_mlp(row_start, row_count, source=grad_gate_up, weight=flat_gu):
            return inner_cols(source, weight)

        grad_normed_b = lax.psum_scatter(
            back_mlp(jnp.int32(0), local_rows * lax.axis_size("tensor")).astype(jnp.bfloat16),
            "tensor",
            scatter_dimension=0,
            tiled=True,
        ).astype(jnp.float32)
        grad_in_b, gain_b, shift_b = norm_back(
            grad_normed_b, scaled_b, inverse_b, norm_gain[layer_index, 1]
        )
        grad = grad + grad_in_b
        grad_rows_a = lax.all_gather(grad.astype(jnp.bfloat16), "tensor", axis=0, tiled=True)
        grad_out_weight = inner_rows(attended, grad_rows_a)
        grad_attended = inner_cols(grad_rows_a, full_out).astype(jnp.bfloat16)
        grad_attended = grad_attended.reshape(seq_len, heads_local, HD)
        grad_queries, grad_keys, grad_values = attend_back(
            queries, key_rows, values, positions, logsums, grad_attended, score_scale
        )
        grad_queries = rotate(grad_queries, cos_table, -sin_table)
        grad_keys = rotate(grad_keys, cos_table, -sin_table)
        grad_mixed = jnp.stack([grad_queries, grad_keys, grad_values], axis=1)
        grad_mixed = grad_mixed.reshape(seq_len, 3 * width_local).astype(jnp.bfloat16)
        qkv_shift_local = jnp.sum(grad_mixed, axis=0, dtype=jnp.float32).reshape(3, width_local)
        qkv_shift_rows[layer_index] = lax.dynamic_update_slice(
            jnp.zeros((3, b_qkv.shape[2]), jnp.float32),
            qkv_shift_local,
            (jnp.int32(0), tensor_rank * width_local),
        )
        grad_qkv_weight = inner_rows(rows_a, grad_mixed).reshape(full_qkv.shape)
        flat_qkv = full_qkv.reshape(full_qkv.shape[0], 3 * width_local)

        def back_attn(row_start, row_count, source=grad_mixed, weight=flat_qkv):
            return inner_cols(source, weight)

        grad_normed_a = lax.psum_scatter(
            back_attn(jnp.int32(0), local_rows * lax.axis_size("tensor")).astype(jnp.bfloat16),
            "tensor",
            scatter_dimension=0,
            tiled=True,
        ).astype(jnp.float32)
        grad_in_a, gain_a, shift_a = norm_back(
            grad_normed_a, scaled_a, inverse_a, norm_gain[layer_index, 0]
        )
        grad = grad + grad_in_a
        gain_rows[layer_index] = jnp.stack([gain_a, gain_b])
        shift_rows[layer_index] = jnp.stack([shift_a, shift_b])
        weight_parts[layer_index] = (
            lax.psum_scatter(
                grad_qkv_weight.astype(jnp.bfloat16), "dp", scatter_dimension=0, tiled=True
            ).astype(jnp.float32),
            lax.psum_scatter(
                grad_out_weight.astype(jnp.bfloat16), "dp", scatter_dimension=1, tiled=True
            ).astype(jnp.float32),
            lax.psum_scatter(
                grad_gu_weight.astype(jnp.bfloat16), "dp", scatter_dimension=0, tiled=True
            ).astype(jnp.float32),
            lax.psum_scatter(
                grad_down_weight.astype(jnp.bfloat16), "dp", scatter_dimension=1, tiled=True
            ).astype(jnp.float32),
        )
    stack_qkv = jnp.stack([weight_parts[number][0] for number in range(LAYERS)])
    stack_out = jnp.stack([weight_parts[number][1] for number in range(LAYERS)])
    stack_gu = jnp.stack([weight_parts[number][2] for number in range(LAYERS)])
    stack_down = jnp.stack([weight_parts[number][3] for number in range(LAYERS)])
    gain_grad, norm_bias_grad, qkv_bias_grad = lax.psum(
        (jnp.stack(gain_rows), jnp.stack(shift_rows), jnp.stack(qkv_shift_rows)), ("dp", "tensor")
    )
    return (
        activations,
        grad,
        gain_grad,
        norm_bias_grad,
        stack_qkv,
        qkv_bias_grad,
        stack_out,
        stack_gu,
        stack_down,
    )


def solution(mesh):
    in_specs = (
        P(("dp", "tensor"), None),
        P("dp"),
        P(),
        P(),
        P(None, "dp", None, "tensor"),
        P(),
        P(None, "tensor", "dp"),
        P(None, "dp", None, "tensor"),
        P(None, "tensor", "dp"),
        P(("dp", "tensor"), None),
    )
    out_specs = (
        P(("dp", "tensor"), None),
        P(("dp", "tensor"), None),
        P(),
        P(),
        P(None, "dp", None, "tensor"),
        P(),
        P(None, "tensor", "dp"),
        P(None, "dp", None, "tensor"),
        P(None, "tensor", "dp"),
    )
    def run(*operands):
        fits = operands[7].shape[3] % 128 == 0 and operands[4].shape[3] % PAIR == 0
        return (per_device if fits else per_device_plain)(*operands)

    return jax.shard_map(
        run, mesh=mesh, in_specs=in_specs, out_specs=out_specs, check_vma=False
    )
```
